32 devices in a mesh: wide: 8 (over y, x, core), narrow: 4 (over z).
Axes of the slice: x: 2, y: 2, z: 4, core: 2. Of those that a mesh axis runs over, the one named last changes fastest.
Arguments:
- reference_image: bfloat16 [1024, 512, 128], P('wide', 'narrow'), may hold values from -6 to 6
- deformed_image: bfloat16 [1024, 512, 128], P('wide', 'narrow'), may hold values from -6 to 6
- displacement: float32 [3, 17, 128, 64], P(None, None, 'wide', 'narrow'), may hold values from -0.5 to 0.5
- tile_map: int32 [8, 4, 2], P('wide', 'narrow'), may hold values from -32 to 32, as said below
Outputs:
- updated: float32 [3, 17, 128, 64], P(None, None, 'wide', 'narrow')
- residual: bfloat16 [1024, 512, 128], P('wide', 'narrow')
The draws below stay inside these ranges and needn't reach their ends.
Inputs may be any that keep to these rules, and one draw needn't show every extreme that they name: `tile_map`: each component spans -32 to 32 over the tiles and reaches both ends on some tile.
All inputs are finite; a program needn't handle non-finite values.
Results may differ from the reference program's by a relative error of at most 0.0004.
Values may be sent and summed in bfloat16 or wider, within the bound.
A program may use at most 256 MiB of HBM per device.

```python
import jax
import jax.numpy as jnp
from jax import lax

TX = 128
TY = 128
Z = 128
RIM = 32
EX = 16
EY = 16
S = 17
NTX = 8
NTY = 4
NX = 1024
NY = 512
NXE = 128
NYE = 64


def draw_tile_map(key, part):
    first_key = jax.random.fold_in(key, 11)
    second_key = jax.random.fold_in(key, 12)
    offsets = jax.random.randint(first_key, (NTX * NTY, 2), -RIM, RIM + 1, dtype=jnp.int32)
    chosen = jax.random.permutation(second_key, NTX * NTY)[:4]
    offsets = offsets.at[chosen[0], 0].set(RIM)
    offsets = offsets.at[chosen[1], 0].set(-RIM)
    offsets = offsets.at[chosen[2], 1].set(RIM)
    offsets = offsets.at[chosen[3], 1].set(-RIM)
    return offsets.reshape(NTX, NTY, 2)


def block_levels(own_key, extent, cuts, smallest, largest):
    gain = 1.0
    for dim, blocks in cuts:
        steps = jax.random.uniform(jax.random.fold_in(jax.random.fold_in(own_key, 6), dim), (blocks,), jnp.float32, smallest / len(cuts), largest / len(cuts))
        gain = gain * jnp.repeat(jnp.exp(steps), extent[dim] // blocks).reshape((-1,) + (1,) * (len(extent) - 1 - dim))
    return gain


def gaussian(key, shape, deviation, reach, pieces=(), kind=jnp.bfloat16):
    drawn = deviation * jax.random.normal(key, shape, jnp.float32)
    if pieces:
        drawn = drawn * block_levels(key, shape, pieces, -0.22, 0.18)
    return jnp.clip(drawn, -reach, reach).astype(kind)


def setup_inputs(seed: int = 0) -> dict:
    arg_keys = jax.random.split(jax.random.key(seed), 5)
    reference_image = gaussian(arg_keys[0], (NX, NY, Z), 1.0, 6.0, ((0, 8), (1, 4)))
    deformed_image = gaussian(arg_keys[1], (NX, NY, Z), 1.0, 6.0, ((0, 8), (1, 4)))
    displacement = jnp.clip(jax.random.uniform(arg_keys[2], (3, S, NXE, NYE), jnp.float32, -0.5, 0.5) * block_levels(arg_keys[2], (3, S, NXE, NYE), ((2, 8), (3, 4)), -0.4, 0.0), -0.5, 0.5)
    tile_map = draw_tile_map(jax.random.fold_in(arg_keys[4], 71), 0)
    return dict(reference_image=reference_image, deformed_image=deformed_image, displacement=displacement, tile_map=tile_map)


MU_SHEAR = 1.0
LAMBDA_BULK = 2.0
REG_WEIGHT = 256.0
STIFFNESS = 16.0
PRECISE = lax.Precision.HIGHEST

def shape_table(voxels):
    cell_ids = jnp.arange(voxels, dtype=jnp.int32)
    element = cell_ids // 8
    fraction = ((cell_ids % 8).astype(jnp.float32) + 0.5) / 8.0
    node_ids = jnp.arange(voxels // 8 + 1, dtype=jnp.int32)
    lower_part = jnp.where(node_ids[None, :] == element[:, None], 1.0 - fraction[:, None], 0.0)
    upper_part = jnp.where(node_ids[None, :] == element[:, None] + 1, fraction[:, None], 0.0)
    return (lower_part + upper_part).astype(jnp.float32)

def interpolate(nodal_field, table_x, table_y, table_z):
    step_one = jnp.einsum('zs,cspq->czpq', table_z, nodal_field, precision=PRECISE)
    step_two = jnp.einsum('xp,czpq->cxzq', table_x, step_one, precision=PRECISE)
    return jnp.einsum('yq,cxzq->cxyz', table_y, step_two, precision=PRECISE)

def project(field, table_x, table_y, table_z):
    step_one = jnp.einsum('yq,cxyz->cxzq', table_y, field, precision=PRECISE)
    step_two = jnp.einsum('xp,cxzq->czpq', table_x, step_one, precision=PRECISE)
    return jnp.einsum('zs,czpq->cspq', table_z, step_two, precision=PRECISE)

def tile_terms(reference_tile, window, nodal_field):
    table_x = shape_table(reference_tile.shape[0])
    table_y = shape_table(reference_tile.shape[1])
    table_z = shape_table(reference_tile.shape[2])
    sampled = window[1:-1, 1:-1, :]
    slope_x = 0.5 * (window[2:, 1:-1, :] - window[:-2, 1:-1, :])
    slope_y = 0.5 * (window[1:-1, 2:, :] - window[1:-1, :-2, :])
    padded_z = jnp.pad(sampled, ((0, 0), (0, 0), (1, 1)))
    slope_z = 0.5 * (padded_z[:, :, 2:] - padded_z[:, :, :-2])
    moved = interpolate(nodal_field, table_x, table_y, table_z)
    residual = reference_tile - sampled - (slope_x * moved[0] + slope_y * moved[1] + slope_z * moved[2])
    slopes = jnp.stack([slope_x, slope_y, slope_z])
    data_grad = -project(slopes * residual[None], table_x, table_y, table_z)
    data_diag = project(slopes * slopes, table_x * table_x, table_y * table_y, table_z * table_z)
    return (residual, data_grad, data_diag)

def element_energy(nodal_field):
    diff_x = nodal_field[:, :, 1:, :] - nodal_field[:, :, :-1, :]
    grad_x = 0.03125 * (diff_x[:, :-1, :, :-1] + diff_x[:, 1:, :, :-1] + diff_x[:, :-1, :, 1:] + diff_x[:, 1:, :, 1:])
    diff_y = nodal_field[:, :, :, 1:] - nodal_field[:, :, :, :-1]
    grad_y = 0.03125 * (diff_y[:, :-1, :-1, :] + diff_y[:, 1:, :-1, :] + diff_y[:, :-1, 1:, :] + diff_y[:, 1:, 1:, :])
    diff_z = nodal_field[:, 1:, :, :] - nodal_field[:, :-1, :, :]
    grad_z = 0.03125 * (diff_z[:, :, :-1, :-1] + diff_z[:, :, 1:, :-1] + diff_z[:, :, :-1, 1:] + diff_z[:, :, 1:, 1:])
    columns = (grad_x, grad_y, grad_z)
    entries = [[columns[j][i] + (1.0 if i == j else 0.0) for j in range(3)] for i in range(3)]
    volume_ratio = entries[0][0] * (entries[1][1] * entries[2][2] - entries[1][2] * entries[2][1]) - entries[0][1] * (entries[1][0] * entries[2][2] - entries[1][2] * entries[2][0]) + entries[0][2] * (entries[1][0] * entries[2][1] - entries[1][1] * entries[2][0])
    squares = entries[0][0] * entries[0][0]
    for i in range(3):
        for j in range(3):
            if i + j > 0:
                squares = squares + entries[i][j] * entries[i][j]
    log_ratio = jnp.log(volume_ratio)
    energy = 0.5 * MU_SHEAR * (squares - 3.0 - 2.0 * log_ratio) + 0.5 * LAMBDA_BULK * log_ratio * log_ratio
    return REG_WEIGHT * jnp.sum(energy)

def pad_nodes(nodal_field):
    return jnp.pad(nodal_field, ((0, 0), (0, 0), (0, 1), (0, 1)))

def reference(reference_image, deformed_image, displacement, tile_map):
    margin = RIM + 1
    deformed = jnp.pad(deformed_image.astype(jnp.float32), ((margin, margin), (margin, margin), (0, 0)))
    reference_full = reference_image.astype(jnp.float32)
    nodal_full = pad_nodes(displacement)

    def one_tile(number):
        tile_row = (number // NTY).astype(jnp.int32)
        tile_col = (number % NTY).astype(jnp.int32)
        offset_x = tile_map[tile_row, tile_col, 0]
        offset_y = tile_map[tile_row, tile_col, 1]
        window = lax.dynamic_slice(deformed, (tile_row * TX + offset_x + margin - 1, tile_col * TY + offset_y + margin - 1, jnp.int32(0)), (TX + 2, TY + 2, Z))
        reference_tile = lax.dynamic_slice(reference_full, (tile_row * TX, tile_col * TY, jnp.int32(0)), (TX, TY, Z))
        nodal_tile = lax.dynamic_slice(nodal_full, (jnp.int32(0), jnp.int32(0), tile_row * EX, tile_col * EY), (3, S, EX + 1, EY + 1))
        residual, data_grad, data_diag = tile_terms(reference_tile, window, nodal_tile)
        return (residual.astype(jnp.bfloat16), data_grad, data_diag)
    residuals, grads, diags = lax.map(one_tile, jnp.arange(NTX * NTY, dtype=jnp.int32))

    def add_tile(number, totals):
        number = jnp.asarray(number).astype(jnp.int32)
        tile_row = number // NTY
        tile_col = number % NTY
        corner = (jnp.int32(0), jnp.int32(0), tile_row * EX, tile_col * EY)
        grad_total = lax.dynamic_update_slice(totals[0], lax.dynamic_slice(totals[0], corner, (3, S, EX + 1, EY + 1)) + grads[number], corner)
        diag_total = lax.dynamic_update_slice(totals[1], lax.dynamic_slice(totals[1], corner, (3, S, EX + 1, EY + 1)) + diags[number], corner)
        return (grad_total, diag_total)
    blank = jnp.zeros((3, S, NXE + 1, NYE + 1), jnp.float32)
    grad_total, diag_total = lax.fori_loop(0, NTX * NTY, add_tile, (blank, blank))
    reg_grad = jax.grad(lambda nodal_field: element_energy(pad_nodes(nodal_field)))(displacement)
    gradient = grad_total[:, :, :NXE, :NYE] + reg_grad
    diagonal = diag_total[:, :, :NXE, :NYE] + STIFFNESS
    updated = displacement - gradient / diagonal
    residual = residuals.reshape(NTX, NTY, TX, TY, Z).transpose(0, 2, 1, 3, 4).reshape(NX, NY, Z)
    return (updated, residual)
```

```python
import functools

import jax
import jax.numpy as jnp
import numpy as np
from jax import lax
from jax.experimental import pallas as pl
from jax.experimental.pallas import tpu as pltpu
from jax.sharding import PartitionSpec as P

MU_SHEAR = 1.0
LAMBDA_BULK = 2.0
REG_WEIGHT = 256.0
STIFFNESS = 16.0
MESH = pl.DeviceIdType.MESH
F32 = jnp.float32
BF16 = jnp.bfloat16
SIDE = 48
QPAD = 24


def as_int(flag):
    return flag.astype(jnp.int32)


def halo_kernel(nw, nn, rim, own, extra_in, edge_x, edge_y, out, extra, edges,
                ext, zeros, send, recv, zsem, lsem):
    rows, cols, _ = own.shape
    side = rim - 1
    w = lax.axis_index("wide")
    n = lax.axis_index("narrow")
    lo_w, hi_w, lo_n, hi_n = w > 0, w < nw - 1, n > 0, n < nn - 1
    up_w, dn_w = (w + 1, n), (w - 1, n)
    up_n, dn_n = (w, n + 1), (w, n - 1)
    mid = slice(side, side + cols)
    ylo = slice(0, side)
    yhi = slice(side + cols, 2 * side + cols)
    total = rows + 2 * rim
    emid = slice(SIDE, SIDE + rows)
    local = pltpu.make_async_copy(own, ext.at[rim:rim + rows, mid], lsem.at[0])
    local.start()
    edges[...] = jnp.zeros_like(edges)
    extra[...] = jnp.zeros_like(extra)
    barrier = pltpu.get_barrier_semaphore()
    for there, device in ((lo_w, dn_w), (hi_w, up_w), (lo_n, dn_n), (hi_n, up_n)):
        @pl.when(there)
        def _(device=device):
            pl.semaphore_signal(barrier, inc=1, device_id=device, device_id_type=MESH)
    zeros[...] = jnp.zeros_like(zeros)
    jobs = []

    def fill(cond, dst):
        src = zeros.at[tuple(slice(0, d) for d in dst.shape)]
        jobs.append((cond, pltpu.make_async_copy(src, dst, zsem.at[len(jobs)])))

    for cond, span in ((jnp.logical_not(lo_n), ylo), (jnp.logical_not(hi_n), yhi)):
        fill(cond, ext.at[:, span])
    for cond, band in ((jnp.logical_not(lo_w), slice(0, rim)), (jnp.logical_not(hi_w), slice(rim + rows, total))):
        fill(cond, ext.at[band, mid])
        fill(cond & lo_n, ext.at[band, ylo])
        fill(cond & hi_n, ext.at[band, yhi])
    for cond, job in jobs:
        @pl.when(cond)
        def _(job=job):
            job.start()
    pl.semaphore_wait(barrier, as_int(lo_w) + as_int(hi_w) + as_int(lo_n) + as_int(hi_n))

    def remote(k, src, dst, device):
        return pltpu.make_async_remote_copy(
            src_ref=src, dst_ref=dst, send_sem=send.at[k], recv_sem=recv.at[k],
            device_id=device, device_id_type=MESH)

    first = [
        (lo_w, hi_w, remote(0, edge_x, edges.at[0], dn_w)),
        (lo_n, hi_n, remote(1, edge_y, edges.at[1], dn_n)),
        (hi_n, lo_n, remote(2, extra_in.at[0], extra.at[0, emid], up_n)),
        (lo_n, hi_n, remote(3, extra_in.at[1], extra.at[1, emid], dn_n)),
    ]
    full = (slice(0, rim), slice(rows - rim, rows), slice(rim, rows - rim))
    for j, part in enumerate(full):
        there = slice(part.start + rim, part.stop + rim)
        first.append((hi_n, lo_n, remote(4 + 2 * j, ext.at[there, cols:cols + side], ext.at[there, ylo], up_n)))
        first.append((lo_n, hi_n, remote(5 + 2 * j, ext.at[there, side:2 * side], ext.at[there, yhi], dn_n)))
    first.append((hi_w, lo_w, remote(10, ext.at[rows:rows + rim, mid], ext.at[0:rim, mid], up_w)))
    first.append((lo_w, hi_w, remote(11, ext.at[rim:2 * rim, mid], ext.at[rows + rim:total, mid], dn_w)))
    local.wait()
    saves = []

    def settle(k, span, columns):
        save = pltpu.make_async_copy(ext.at[span, columns], out.at[span, columns], lsem.at[1 + k])
        save.start()
        saves.append(save)

    for goes, _c, copy in first:
        @pl.when(goes)
        def _(copy=copy):
            copy.start()
    settle(0, slice(rim, rim + rows), mid)
    low_rows, high_rows = slice(rim, 2 * rim), slice(rows, rows + rim)
    below, above = slice(0, rim), slice(rim + rows, total)
    elow, ehigh = slice(SIDE, 2 * SIDE), slice(rows, SIDE + rows)
    ebelow, eabove = slice(0, SIDE), slice(SIDE + rows, 2 * SIDE + rows)
    second = {
        0: [(hi_w & lo_n, hi_w & hi_n, remote(12, edges.at[0], edges.at[2], dn_n))],
        2: [(lo_n & lo_w, lo_n & hi_w, remote(13, extra.at[0, elow], extra.at[0, eabove], dn_w)),
            (lo_n & hi_w, lo_n & lo_w, remote(14, extra.at[0, ehigh], extra.at[0, ebelow], up_w))],
        3: [(hi_n & lo_w, hi_n & hi_w, remote(15, extra.at[1, elow], extra.at[1, eabove], dn_w)),
            (hi_n & hi_w, hi_n & lo_w, remote(16, extra.at[1, ehigh], extra.at[1, ebelow], up_w))],
        4: [(lo_n & lo_w, lo_n & hi_w, remote(17, ext.at[low_rows, ylo], ext.at[above, ylo], dn_w))],
        5: [(hi_n & lo_w, hi_n & hi_w, remote(18, ext.at[low_rows, yhi], ext.at[above, yhi], dn_w))],
        6: [(lo_n & hi_w, lo_n & lo_w, remote(19, ext.at[high_rows, ylo], ext.at[below, ylo], up_w))],
        7: [(hi_n & hi_w, hi_n & lo_w, remote(20, ext.at[high_rows, yhi], ext.at[below, yhi], up_w))],
    }
    later = []
    for k, (_g, comes, copy) in enumerate(first):
        @pl.when(comes)
        def _(copy=copy):
            copy.wait_recv()
        for entry in second.get(k, ()):
            later.append(entry)
            @pl.when(entry[0])
            def _(entry=entry):
                entry[2].start()
    for _g, comes, copy in later:
        @pl.when(comes)
        def _(copy=copy):
            copy.wait_recv()
    for cond, job in jobs:
        @pl.when(cond)
        def _(job=job):
            job.wait()
    settle(1, below, mid)
    settle(2, above, mid)
    settle(3, slice(0, total), ylo)
    settle(4, slice(0, total), yhi)
    for goes, _c, copy in first + later:
        @pl.when(goes)
        def _(copy=copy):
            copy.wait_send()
    for save in saves:
        save.wait()


def exchange(deformed, by_node, nw, nn):
    rows, cols, layers = deformed.shape
    rim = rows // 4 + 1
    shape = (rows + 2 * rim, cols + 2 * (rim - 1), layers)
    extra_in = jnp.stack([deformed[:, cols - rim], deformed[:, rim - 1]])
    anywhere = pl.BlockSpec(memory_space=pl.ANY)
    near = pl.BlockSpec(memory_space=pltpu.VMEM)
    lanes = by_node.shape[-1]
    return pl.pallas_call(
        functools.partial(halo_kernel, nw, nn, rim),
        out_shape=[jax.ShapeDtypeStruct(shape, BF16),
                   jax.ShapeDtypeStruct((2, rows + 2 * SIDE, layers), BF16),
                   jax.ShapeDtypeStruct((3,) + by_node.shape[1:], F32)],
        in_specs=[anywhere, near, near, near],
        out_specs=[anywhere, near, near],
        scratch_shapes=[
            pltpu.VMEM(shape, BF16),
            pltpu.VMEM((shape[0], cols, layers), BF16),
            pltpu.SemaphoreType.DMA((21,)),
            pltpu.SemaphoreType.DMA((21,)),
            pltpu.SemaphoreType.DMA((8,)),
            pltpu.SemaphoreType.DMA((6,)),
        ],
        compiler_params=pltpu.CompilerParams(
            collective_id=0, has_side_effects=True, vmem_limit_bytes=62 << 20),
        name="halo",
    )(deformed, extra_in, by_node[0], by_node[:, 0])


def tables(rows, cols, layers, comps):
    def one(voxels):
        t = np.zeros((voxels, voxels // 8 + 1))
        for i in range(voxels):
            f = (i % 8 + 0.5) / 8.0
            t[i, i // 8] += 1.0 - f
            t[i, i // 8 + 1] += f
        return t
    ty, tz = one(cols), one(layers)
    nq, ns = ty.shape[1], tz.shape[1]
    typ = np.zeros((cols, QPAD))
    typ[:, :nq] = ty
    inter = 0.5 * np.concatenate([typ, typ], 1)
    proj = np.concatenate([typ.T, typ.T], 1)
    proj2 = np.concatenate([(typ * typ).T, (typ * typ).T], 1)
    lanes = comps * layers
    up = np.zeros((2 * 128, lanes))
    down = np.zeros((lanes, 128))
    down2 = np.zeros((lanes, 128))
    for c in range(comps):
        for h in range(2):
            up[h * 128 + c * ns:h * 128 + (c + 1) * ns, c * layers:(c + 1) * layers] = tz.T
        down[c * layers:(c + 1) * layers, c * ns:(c + 1) * ns] = -0.5 * tz
        down2[c * layers:(c + 1) * layers, c * ns:(c + 1) * ns] = 0.25 * tz * tz
    as_bf16 = lambda a: jnp.asarray(a.astype(BF16))
    return [as_bf16(a) for a in (inter, proj, proj2, up, down, down2)]


def split(value):
    high = value.astype(BF16)
    return high, (value - high.astype(F32)).astype(BF16)


def strain_pull(ns, nodes, pull):
    npx = nodes.shape[0]
    nel = npx - 1
    lane = lax.broadcasted_iota(jnp.int32, (nel, 128), 1)
    move = lambda a, by: pltpu.roll(a, by % 128, 1)
    pull[...] = jnp.zeros_like(pull)

    @pl.loop(0, nel)
    def _(p):
        a00, a01 = nodes[p, 0:nel], nodes[p, 1:nel + 1]
        a10, a11 = nodes[p + 1, 0:nel], nodes[p + 1, 1:nel + 1]
        dx = (a10 - a00) + (a11 - a01)
        dy = (a01 - a00) + (a11 - a10)
        every = (a00 + a01) + (a10 + a11)
        slopes = (dx + move(dx, -1), dy + move(dy, -1), move(every, -1) - every)
        f = [[0.03125 * (move(h, -ns * i) if i else h) + (1.0 if i == j else 0.0)
              for j, h in enumerate(slopes)] for i in range(3)]
        cof = [[f[(i + 1) % 3][(j + 1) % 3] * f[(i + 2) % 3][(j + 2) % 3]
                - f[(i + 1) % 3][(j + 2) % 3] * f[(i + 2) % 3][(j + 1) % 3]
                for j in range(3)] for i in range(3)]
        ratio = f[0][0] * cof[0][0] + f[0][1] * cof[0][1] + f[0][2] * cof[0][2]
        factor = (LAMBDA_BULK * jnp.log(ratio) - MU_SHEAR) / ratio
        back = []
        for j in range(3):
            parts = [jnp.where(lane < ns - 1, MU_SHEAR * f[i][j] + factor * cof[i][j], 0.0) for i in range(3)]
            back.append((parts[0] + move(parts[1], ns) + move(parts[2], 2 * ns)) * (0.03125 * REG_WEIGHT))
        gx = back[0] + move(back[0], 1)
        gy = back[1] + move(back[1], 1)
        gz = move(back[2], 1) - back[2]
        for dp, dq in ((0, 0), (0, 1), (1, 0), (1, 1)):
            add = (gx if dp else -gx) + (gy if dq else -gy) + gz
            pull[p + dp, dq:dq + nel] = pull[p + dp, dq:dq + nel] + add


def voxels(at, window, ref_rows, left, right, keep_low, keep_high):
    held = [None] * 8
    back = []
    rows = [None] * 8
    for half in range(2):
        run, tot, qrun, qtot, qtwo = ([None] * 3 for _ in range(5))
        inc = [(right(c, half) - left(c, half)) * 0.125 for c in range(3)]
        mv = [left(c, half) + 0.5 * inc[c] for c in range(3)]
        prev, cur = window(0, 0, half), window(1, 0, half)
        for k in range(8):
            nxt = window(k + 2, 0, half)
            g = [nxt - prev,
                 window(k + 1, 1, half) - window(k + 1, -1, half),
                 jnp.where(keep_high, pltpu.roll(cur, 127, 1), 0.0) - jnp.where(keep_low, pltpu.roll(cur, 1, 1), 0.0)]
            r = ref_rows(k, half) - cur
            for c in range(3):
                r = r - g[c] * mv[c]
                if k < 7:
                    mv[c] = mv[c] + inc[c]
            if half == 0:
                held[k] = r
            else:
                rows[k] = jnp.concatenate([held[k], r], axis=0).astype(BF16)
            for c in range(3):
                f = g[c] * r
                q = g[c] * g[c]
                run[c] = f if k == 0 else run[c] + f
                tot[c] = run[c] if k == 0 else tot[c] + run[c]
                qrun[c] = q if k == 0 else qrun[c] + q
                qtot[c] = qrun[c] if k == 0 else qtot[c] + qrun[c]
                qtwo[c] = qtot[c] if k == 0 else qtwo[c] + qtot[c]
            prev, cur = cur, nxt
        part = []
        for c in range(3):
            low = (tot[c] - 0.5 * run[c]) * 0.125
            lin = (qtot[c] - 0.5 * qrun[c]) * 0.125
            qlow = (qtwo[c] - qtot[c] + 0.125 * qrun[c]) * 0.03125
            part.append((low, run[c] - low, qlow, qrun[c] - 2.0 * lin + qlow))
        back.append(part)
    return rows, [[jnp.concatenate([back[0][c][i], back[1][c][i]], axis=0) for i in range(4)] for c in range(3)]


def tile_kernel(rim, ns, map_ref, ref_tile, ext, extra, by_node, edges,
                inter, proj, proj2, up, down, down2,
                res, out,
                rows_in, win, field, sums, carry, gacc, dacc, nodes, pull, rimcol, sem):
    p = pl.program_id(0)
    steps = pl.num_programs(0)
    cols, layers = ref_tile.shape[1], ref_tile.shape[2]
    comps = field.shape[2] // layers
    side = rim - 1
    wide_cols = cols + 2 * side
    start = map_ref[0] + side

    def fetch(first, count, k):
        return pltpu.make_async_copy(
            ext.at[pl.ds(start + first, count)],
            rows_in.at[pl.ds(first, count)], sem.at[k])

    def widen(first, count):
        for a in range(count):
            at = map_ref[0] + (SIDE - 1) + first + a
            win[first + a, 8:8 + wide_cols] = rows_in[first + a].astype(F32)
            win[first + a, 7:8] = rimcol[0, pl.ds(at, 1), :]
            win[first + a, 8 + wide_cols:9 + wide_cols] = rimcol[1, pl.ds(at, 1), :]

    @pl.when(p == 0)
    def _():
        fetch(0, 2, steps).start()

        @pl.loop(0, steps)
        def _(k):
            fetch(8 * k + 2, 8, k).start()
        rimcol[...] = extra[...].astype(F32)
        nel = by_node.shape[0]
        nodes[0:nel, 0:nel] = by_node[...]
        nodes[nel, 0:nel] = edges[0]
        top = lax.broadcasted_iota(jnp.int32, (QPAD - nel, 128), 0) == 0
        for i in range(nel + 1):
            row = edges[1, i:i + 1] if i < nel else edges[2, 0:1]
            nodes[i, nel:QPAD] = jnp.where(top, jnp.broadcast_to(row, (QPAD - nel, 128)), 0.0)
        flat = nodes[...].reshape(-1, 128)
        high = flat.astype(BF16).astype(F32)
        both = jnp.concatenate([high, flat - high], axis=1).astype(BF16)
        level = jnp.dot(both, up[...], preferred_element_type=F32)
        for i in range(nel + 1):
            head, tail = split(level[i * QPAD:(i + 1) * QPAD])
            field[i] = jnp.dot(inter[...], jnp.concatenate([head, tail], axis=0), preferred_element_type=F32)
        strain_pull(ns, nodes, pull)
        carry[...] = jnp.zeros_like(carry)
        fetch(0, 2, steps).wait()
        widen(0, 2)

    base = pl.multiple_of(8 * p, 8)
    fetch(base + 2, 8, p).wait()
    widen(base + 2, 8)
    lane = lax.broadcasted_iota(jnp.int32, (8, layers), 1)
    keep_low, keep_high = lane > 0, lane < layers - 1
    col0 = map_ref[1] + 8 + side

    @pl.loop(0, cols // 16)
    def _(j):
        at = pl.multiple_of(j * 16, 16)
        refs = [ref_tile[k, pl.ds(at, 16), :].astype(F32) for k in range(8)]
        rows, terms = voxels(
            at,
            lambda k, shift, half: win[base + k, pl.ds(col0 + at + (8 * half + shift), 8), :],
            lambda k, half: refs[k][8 * half:8 * half + 8],
            lambda c, half: field[p, pl.ds(at + 8 * half, 8), c * layers:(c + 1) * layers],
            lambda c, half: field[p + 1, pl.ds(at + 8 * half, 8), c * layers:(c + 1) * layers],
            keep_low, keep_high)
        for k in range(8):
            res[k, pl.ds(at, 16), :] = rows[k]
        for c in range(3):
            lanes = slice(c * layers, (c + 1) * layers)
            for i in range(2):
                low, high = terms[c][2 * i:2 * i + 2]
                head, tail = split(carry[i, pl.ds(at, 16), lanes] + low)
                sums[p, i, pl.ds(at, 16), lanes] = head
                sums[p, i, pl.ds(cols + at, 16), lanes] = tail
                carry[i, pl.ds(at, 16), lanes] = high

    @pl.when(p == steps - 1)
    def _():
        for i in range(2):
            head, tail = split(carry[i])
            sums[steps, i, 0:cols] = head
            sums[steps, i, cols:2 * cols] = tail
        for k, (acc, mat, table) in enumerate(((gacc, proj, down), (dacc, proj2, down2))):
            for i in range(steps + 1):
                acc[i] = jnp.dot(mat[...], sums[i, k], preferred_element_type=F32)
            head, tail = split(acc[...].reshape(-1, comps * layers))
            got = (jnp.dot(head, table[...], preferred_element_type=F32)
                   + jnp.dot(tail, table[...], preferred_element_type=F32)).reshape(pull.shape)
            out[k] = got + pull[...] if k == 0 else got


def tile_terms(reference_tile, ext, extra, by_node, edges, offsets, ns):
    rows, cols, layers = reference_tile.shape
    comps = 3
    npx = by_node.shape[0] + 1
    rim = rows // 4 + 1
    tabs = tables(rows, cols, layers, comps)
    steps = rows // 8
    whole = lambda a: pl.BlockSpec(a.shape, lambda p, m: (0,) * a.ndim, pipeline_mode=pl.Buffered(1))
    slab = pl.BlockSpec((8, cols, layers), lambda p, m: (p, 0, 0))
    out_nodes = jax.ShapeDtypeStruct((2, npx, QPAD, 128), F32)
    wide_cols = cols + 2 * (rim - 1)
    grid_spec = pltpu.PrefetchScalarGridSpec(
        num_scalar_prefetch=1,
        grid=(steps,),
        in_specs=[slab, pl.BlockSpec(memory_space=pl.ANY), whole(extra), whole(by_node), whole(edges)]
        + [whole(t) for t in tabs],
        out_specs=[slab, whole(out_nodes)],
        scratch_shapes=[
            pltpu.VMEM((rows + 2, wide_cols, layers), BF16),
            pltpu.VMEM((rows + 2, wide_cols + 16, layers), F32),
            pltpu.VMEM((npx, cols, comps * layers), F32),
            pltpu.VMEM((npx, 2, 2 * cols, comps * layers), BF16),
            pltpu.VMEM((2, cols, comps * layers), F32),
            pltpu.VMEM((npx, QPAD, comps * layers), F32),
            pltpu.VMEM((npx, QPAD, comps * layers), F32),
            pltpu.VMEM((npx, QPAD, 128), F32),
            pltpu.VMEM((npx, QPAD, 128), F32),
            pltpu.VMEM(extra.shape, F32),
            pltpu.SemaphoreType.DMA((steps + 1,)),
        ],
    )
    return pl.pallas_call(
        functools.partial(tile_kernel, rim, ns),
        grid_spec=grid_spec,
        out_shape=[jax.ShapeDtypeStruct(reference_tile.shape, BF16), out_nodes],
        compiler_params=pltpu.CompilerParams(
            dimension_semantics=("arbitrary",), vmem_limit_bytes=62 << 20),
        name="tile",
    )(offsets, reference_tile, ext, extra, by_node, edges, *tabs)


def node_kernel(nw, nn, terms, by_node, out, column, from_w, from_n, from_c, send, recv):
    nel = by_node.shape[0]
    w = lax.axis_index("wide")
    n = lax.axis_index("narrow")
    lo_w, hi_w, lo_n, hi_n = w > 0, w < nw - 1, n > 0, n < nn - 1
    up_w, dn_w = (w + 1, n), (w - 1, n)
    up_n, dn_n = (w, n + 1), (w, n - 1)
    for ref in (from_w, from_n, from_c):
        ref[...] = jnp.zeros_like(ref)
    barrier = pltpu.get_barrier_semaphore()
    for there, device in ((lo_w, dn_w), (hi_w, up_w), (lo_n, dn_n), (hi_n, up_n)):
        @pl.when(there)
        def _(device=device):
            pl.semaphore_signal(barrier, inc=1, device_id=device, device_id_type=MESH)
    for k in range(2):
        for p in range(nel):
            column[k, p:p + 1] = terms[k, p, nel:nel + 1]
    pl.semaphore_wait(barrier, as_int(lo_w) + as_int(hi_w) + as_int(lo_n) + as_int(hi_n))

    def remote(k, src, dst, device):
        return pltpu.make_async_remote_copy(
            src_ref=src, dst_ref=dst, send_sem=send.at[k], recv_sem=recv.at[k],
            device_id=device, device_id_type=MESH)

    wide_copy = remote(0, terms.at[:, nel], from_w, up_w)
    narrow_copy = remote(1, column, from_n, up_n)
    corner_copy = remote(2, from_w.at[:, nel:QPAD], from_c, up_n)

    @pl.when(hi_w)
    def _():
        wide_copy.start()

    @pl.when(hi_n)
    def _():
        narrow_copy.start()

    @pl.when(lo_w)
    def _():
        wide_copy.wait_recv()

    @pl.when(lo_w & hi_n)
    def _():
        corner_copy.start()

    @pl.when(lo_n)
    def _():
        narrow_copy.wait_recv()

    @pl.when(lo_w & lo_n)
    def _():
        corner_copy.wait_recv()

    top = lax.broadcasted_iota(jnp.int32, (nel, 128), 0) == 0
    for p in range(nel):
        sums = []
        for k in range(2):
            value = terms[k, p, 0:nel]
            side = from_n[k, p:p + 1]
            if p == 0:
                value = value + from_w[k, 0:nel]
                side = side + from_c[k, 0:1]
            sums.append(value + jnp.where(top, jnp.broadcast_to(side, (nel, 128)), 0.0))
        out[p] = by_node[p] - sums[0] / (sums[1] + STIFFNESS)

    @pl.when(hi_w)
    def _():
        wide_copy.wait_send()

    @pl.when(hi_n)
    def _():
        narrow_copy.wait_send()

    @pl.when(lo_w & hi_n)
    def _():
        corner_copy.wait_send()


def node_update(terms, by_node, nw, nn):
    nel = by_node.shape[0]
    near = pl.BlockSpec(memory_space=pltpu.VMEM)
    return pl.pallas_call(
        functools.partial(node_kernel, nw, nn),
        out_shape=jax.ShapeDtypeStruct(by_node.shape, F32),
        in_specs=[near, near],
        out_specs=near,
        scratch_shapes=[
            pltpu.VMEM((2, nel, 128), F32),
            pltpu.VMEM((2, QPAD, 128), F32),
            pltpu.VMEM((2, nel, 128), F32),
            pltpu.VMEM((2, QPAD - nel, 128), F32),
            pltpu.SemaphoreType.DMA((3,)),
            pltpu.SemaphoreType.DMA((3,)),
        ],
        compiler_params=pltpu.CompilerParams(collective_id=1, has_side_effects=True),
        name="nodes",
    )(terms, by_node)


def per_device(nw, nn, reference_image, deformed_image, displacement, tile_map):
    comps, ns, nex, ney = displacement.shape
    by_node = displacement.transpose(2, 3, 0, 1).reshape(nex, ney, comps * ns)
    by_node = jnp.pad(by_node, ((0, 0), (0, 0), (0, 128 - comps * ns)))
    ext, extra, edges = exchange(deformed_image, by_node, nw, nn)
    residual, terms = tile_terms(
        reference_image, ext, extra, by_node, edges, tile_map.reshape(2), ns)
    moved = node_update(terms, by_node, nw, nn)
    updated = moved[:, :, :comps * ns].reshape(nex, ney, comps, ns).transpose(2, 3, 0, 1)
    return (updated, residual)


def solution(mesh):
    placed = (
        P("wide", "narrow", None),
        P("wide", "narrow", None),
        P(None, None, "wide", "narrow"),
        P("wide", "narrow", None),
    )
    return jax.shard_map(
        functools.partial(per_device, mesh.shape["wide"], mesh.shape["narrow"]),
        mesh=mesh,
        in_specs=placed,
        out_specs=(P(None, None, "wide", "narrow"), P("wide", "narrow", None)),
        check_vma=False,
    )
```

```python
import functools

import jax
import jax.numpy as jnp
import numpy as np
from jax import lax
from jax.experimental import pallas as pl
from jax.experimental.pallas import tpu as pltpu
from jax.sharding import PartitionSpec as P

MU_SHEAR = 1.0
LAMBDA_BULK = 2.0
REG_WEIGHT = 256.0
STIFFNESS = 16.0
MESH = pl.DeviceIdType.MESH
F32 = jnp.float32
BF16 = jnp.bfloat16
SIDE = 48
QPAD = 24


def as_int(flag):
    return flag.astype(jnp.int32)


def halo_kernel(nw, nn, rim, ns, own, disp, inter, up, out, extra, field, pull,
                ext, passed, nodes, cube, column, side_in, corner_in, colf, colb, ylev,
                send, recv, lsem):
    rows, cols, layers = own.shape
    comps, nel = disp.shape[0], disp.shape[1]
    side = rim - 1
    w = lax.axis_index("wide")
    n = lax.axis_index("narrow")
    lo_w, hi_w, lo_n, hi_n = w > 0, w < nw - 1, n > 0, n < nn - 1
    up_w, dn_w = (w + 1, n), (w - 1, n)
    up_n, dn_n = (w, n + 1), (w, n - 1)
    mid = slice(side, side + cols)
    ylo = slice(0, side)
    yhi = slice(side + cols, 2 * side + cols)
    total = rows + 2 * rim
    emid = slice(SIDE, SIDE + rows)
    detour = nw == 8
    is0, is3, is4, is7 = (w == 0), (w == 3), (w == 4), (w == 7)

    local = pltpu.make_async_copy(own, ext.at[rim:rim + rows, mid], lsem.at[0])
    local.start()
    extra[...] = jnp.zeros_like(extra)
    side_in[...] = jnp.zeros_like(side_in)
    corner_in[...] = jnp.zeros_like(corner_in)
    nodes[nel] = jnp.zeros(nodes.shape[1:], F32)
    cube[...] = jnp.zeros_like(cube)
    cube[:, :, :, 0:ns] = disp[...]
    for i in range(nel):
        value = cube[0, i]
        for c in range(1, comps):
            value = value + pltpu.roll(cube[c, i], ns * c, 1)
        nodes[i, 0:nel] = value
        column[i:i + 1] = value[0:1]

    barrier = pltpu.get_barrier_semaphore()
    greet = [(lo_w, dn_w), (hi_w, up_w), (lo_n, dn_n), (hi_n, up_n)]
    if detour:
        greet += [(is7, (3, n)), (is4, (7, n)), (is0, (4, n)), (is3, (0, n))]
    count = as_int(lo_w) + as_int(hi_w) + as_int(lo_n) + as_int(hi_n)
    if detour:
        count = count + as_int(is0 | is3 | is4 | is7)
    for there, device in greet:
        @pl.when(there)
        def _(device=device):
            pl.semaphore_signal(barrier, inc=1, device_id=device, device_id_type=MESH)
    pl.semaphore_wait(barrier, count)

    everything = []

    def remote(goes, comes, src, dst, device):
        k = len(everything)
        copy = pltpu.make_async_remote_copy(
            src_ref=src, dst_ref=dst, send_sem=send.at[k], recv_sem=recv.at[k],
            device_id=device, device_id_type=MESH)
        everything.append((goes, comes, copy))
        return k

    def go(*ks):
        for k in ks:
            @pl.when(everything[k][0])
            def _(k=k):
                everything[k][2].start()

    def come(*ks):
        for k in ks:
            @pl.when(everything[k][1])
            def _(k=k):
                everything[k][2].wait_recv()

    below, above = slice(0, rim), slice(rim + rows, total)
    edge_x = remote(lo_w, hi_w, nodes.at[0, 0:nel], nodes.at[nel, 0:nel], dn_w)
    edge_y = remote(lo_n, hi_n, column, side_in, dn_n)
    strips = []
    full = (slice(0, rim), slice(rows - rim, rows), slice(rim, rows - rim))
    for part in full:
        there = slice(part.start + rim, part.stop + rim)
        strips.append((
            remote(hi_n, lo_n, own.at[part, cols - side:cols], ext.at[there, ylo], up_n),
            remote(lo_n, hi_n, own.at[part, 0:side], ext.at[there, yhi], dn_n)))
    cut = cols // 4 if detour else cols
    near, far = slice(0, cut), slice(cut, cols)
    enear, efar = slice(side, side + cut), slice(side + cut, side + cols)
    high_own, low_own = slice(rows - rim, rows), slice(0, rim)
    bands = [
        remote(hi_w, lo_w, own.at[high_own, near], ext.at[below, enear], up_w),
        remote(lo_w, hi_w, own.at[low_own, near], ext.at[above, enear], dn_w)]
    first_hop, second_hop = [], []
    if detour:
        bands += [
            remote(hi_w & (w != 3), lo_w & (w != 4), own.at[high_own, far], ext.at[below, efar], up_w),
            remote(lo_w & (w != 4), hi_w & (w != 3), own.at[low_own, far], ext.at[above, efar], dn_w)]
        first_hop = [
            remote(is3, is7, own.at[high_own, far], passed, (7, n)),
            remote(is4, is0, own.at[low_own, far], passed, (0, n))]
        second_hop = [
            remote(is7, is4, passed, ext.at[below, efar], (4, n)),
            remote(is0, is3, passed, ext.at[above, efar], (3, n))]
    go(edge_x, edge_y, *strips[0], *strips[1], *first_hop, *bands, *strips[2])

    local.wait()
    saves = []

    def settle(k, src, dst):
        save = pltpu.make_async_copy(src, dst, lsem.at[1 + k])
        save.start()
        saves.append(save)

    settle(0, ext.at[rim:rim + rows, mid], out.at[rim:rim + rows, mid])
    picks = (side + cols - rim, side + rim - 1)

    @pl.loop(0, rows // 8)
    def _(b):
        for a in range(8):
            for i, col in enumerate(picks):
                tile = ext[rim + 8 * b + a, col // 16 * 16:col // 16 * 16 + 16, :].astype(F32)
                colf[i, pl.ds(8 * b + a, 1), :] = tile[col % 16:col % 16 + 1]
    colb[...] = colf[...].astype(BF16)
    elow, ehigh = slice(SIDE, 2 * SIDE), slice(rows, SIDE + rows)
    ebelow, eabove = slice(0, SIDE), slice(SIDE + rows, 2 * SIDE + rows)
    thin = [remote(hi_n, lo_n, colb.at[0], extra.at[0, emid], up_n),
            remote(lo_n, hi_n, colb.at[1], extra.at[1, emid], dn_n)]
    go(*thin)

    @pl.when(jnp.logical_not(lo_n))
    def _():
        ext[:, ylo] = jnp.zeros((total, side, layers), BF16)

    @pl.when(jnp.logical_not(hi_n))
    def _():
        ext[:, yhi] = jnp.zeros((total, side, layers), BF16)

    @pl.when(jnp.logical_not(lo_w))
    def _():
        ext[below] = jnp.zeros((rim, cols + 2 * side, layers), BF16)

    @pl.when(jnp.logical_not(hi_w))
    def _():
        ext[above] = jnp.zeros((rim, cols + 2 * side, layers), BF16)

    come(edge_x)
    edge_c = remote(hi_w & lo_n, hi_w & hi_n, nodes.at[nel, 0:8], corner_in, dn_n)
    go(edge_c)
    come(edge_y)
    top = lax.broadcasted_iota(jnp.int32, (QPAD - nel, 128), 0) == 0
    for i in range(nel):
        nodes[i, nel:QPAD] = jnp.where(top, jnp.broadcast_to(side_in[i:i + 1], (QPAD - nel, 128)), 0.0)
    come(edge_c)
    nodes[nel, nel:QPAD] = jnp.where(top, jnp.broadcast_to(corner_in[0:1], (QPAD - nel, 128)), 0.0)
    flat = nodes[...].reshape(-1, 128)
    high = flat.astype(BF16).astype(F32)
    both = jnp.concatenate([high, flat - high], axis=1).astype(BF16)
    level = jnp.dot(both, up[...], preferred_element_type=F32)
    for i in range(nel + 1):
        head, tail = split(level[i * QPAD:(i + 1) * QPAD])
        ylev[i] = jnp.dot(inter[...], jnp.concatenate([head, tail], axis=0), preferred_element_type=F32)
    settle(1, ylev, field)
    come(*first_hop)
    go(*second_hop)
    strain_pull(ns, nodes, pull)

    corners = []
    come(*strips[0], *strips[1])
    corners += [
        remote(hi_w & lo_n, lo_w & lo_n, ext.at[rows:rows + rim, ylo], ext.at[below, ylo], up_w),
        remote(hi_w & hi_n, lo_w & hi_n, ext.at[rows:rows + rim, yhi], ext.at[below, yhi], up_w),
        remote(lo_w & lo_n, hi_w & lo_n, ext.at[rim:2 * rim, ylo], ext.at[above, ylo], dn_w),
        remote(lo_w & hi_n, hi_w & hi_n, ext.at[rim:2 * rim, yhi], ext.at[above, yhi], dn_w)]
    come(*thin)
    corners += [
        remote(lo_n & lo_w, lo_n & hi_w, extra.at[0, elow], extra.at[0, eabove], dn_w),
        remote(lo_n & hi_w, lo_n & lo_w, extra.at[0, ehigh], extra.at[0, ebelow], up_w),
        remote(hi_n & lo_w, hi_n & hi_w, extra.at[1, elow], extra.at[1, eabove], dn_w),
        remote(hi_n & hi_w, hi_n & lo_w, extra.at[1, ehigh], extra.at[1, ebelow], up_w)]
    go(*corners)
    come(*strips[2])
    settle(2, ext.at[rim:rim + rows, ylo], out.at[rim:rim + rows, ylo])
    settle(3, ext.at[rim:rim + rows, yhi], out.at[rim:rim + rows, yhi])
    come(*bands, *second_hop)
    settle(4, ext.at[below, mid], out.at[below, mid])
    settle(5, ext.at[above, mid], out.at[above, mid])
    come(*corners)
    for k, (band, span) in enumerate(((below, ylo), (below, yhi), (above, ylo), (above, yhi))):
        settle(6 + k, ext.at[band, span], out.at[band, span])
    for goes, _c, copy in everything:
        @pl.when(goes)
        def _(copy=copy):
            copy.wait_send()
    for save in saves:
        save.wait()


def exchange(deformed, nodal, tabs, nw, nn):
    rows, cols, layers = deformed.shape
    comps, nel, _, ns = nodal.shape
    rim = rows // 4 + 1
    shape = (rows + 2 * rim, cols + 2 * (rim - 1), layers)
    inter, up = tabs
    anywhere = pl.BlockSpec(memory_space=pl.ANY)
    near = pl.BlockSpec(memory_space=pltpu.VMEM)
    field = (nel + 1, cols, comps * layers)
    return pl.pallas_call(
        functools.partial(halo_kernel, nw, nn, rim, ns),
        out_shape=[jax.ShapeDtypeStruct(shape, BF16),
                   jax.ShapeDtypeStruct((2, rows + 2 * SIDE, layers), BF16),
                   jax.ShapeDtypeStruct(field, F32),
                   jax.ShapeDtypeStruct((nel + 1, QPAD, 128), F32)],
        in_specs=[anywhere, near, near, near],
        out_specs=[anywhere, near, anywhere, near],
        scratch_shapes=[
            pltpu.VMEM(shape, BF16),
            pltpu.VMEM((rim, cols - cols // 4, layers), BF16),
            pltpu.VMEM((nel + 1, QPAD, 128), F32),
            pltpu.VMEM((comps, nel, nel, 128), F32),
            pltpu.VMEM((nel, 128), F32),
            pltpu.VMEM((nel, 128), F32),
            pltpu.VMEM((8, 128), F32),
            pltpu.VMEM((2, rows, layers), F32),
            pltpu.VMEM((2, rows, layers), BF16),
            pltpu.VMEM(field, F32),
            pltpu.SemaphoreType.DMA((32,)),
            pltpu.SemaphoreType.DMA((32,)),
            pltpu.SemaphoreType.DMA((11,)),
        ],
        compiler_params=pltpu.CompilerParams(
            collective_id=0, has_side_effects=True, vmem_limit_bytes=56 << 20),
        name="halo",
    )(deformed, nodal, inter, up)


def tables(rows, cols, layers, comps):
    def one(voxels):
        t = np.zeros((voxels, voxels // 8 + 1))
        for i in range(voxels):
            f = (i % 8 + 0.5) / 8.0
            t[i, i // 8] += 1.0 - f
            t[i, i // 8 + 1] += f
        return t
    ty, tz = one(cols), one(layers)
    nq, ns = ty.shape[1], tz.shape[1]
    typ = np.zeros((cols, QPAD))
    typ[:, :nq] = ty
    inter = 0.5 * np.concatenate([typ, typ], 1)
    proj = np.concatenate([typ.T, typ.T], 1)
    proj2 = np.concatenate([(typ * typ).T, (typ * typ).T], 1)
    lanes = comps * layers
    up = np.zeros((2 * 128, lanes))
    down = np.zeros((lanes, 128))
    down2 = np.zeros((lanes, 128))
    for c in range(comps):
        for h in range(2):
            up[h * 128 + c * ns:h * 128 + (c + 1) * ns, c * layers:(c + 1) * layers] = tz.T
        down[c * layers:(c + 1) * layers, c * ns:(c + 1) * ns] = -0.5 * tz
        down2[c * layers:(c + 1) * layers, c * ns:(c + 1) * ns] = 0.25 * tz * tz
    as_bf16 = lambda a: jnp.asarray(a.astype(BF16))
    return [as_bf16(a) for a in (inter, proj, proj2, up, down, down2)]


def split(value):
    high = value.astype(BF16)
    return high, (value - high.astype(F32)).astype(BF16)


def strain_pull(ns, nodes, pull):
    npx = nodes.shape[0]
    nel = npx - 1
    lane = lax.broadcasted_iota(jnp.int32, (nel, 128), 1)
    move = lambda a, by: pltpu.roll(a, by % 128, 1)
    pull[...] = jnp.zeros_like(pull)

    @pl.loop(0, nel)
    def _(p):
        a00, a01 = nodes[p, 0:nel], nodes[p, 1:nel + 1]
        a10, a11 = nodes[p + 1, 0:nel], nodes[p + 1, 1:nel + 1]
        dx = (a10 - a00) + (a11 - a01)
        dy = (a01 - a00) + (a11 - a10)
        every = (a00 + a01) + (a10 + a11)
        slopes = (dx + move(dx, -1), dy + move(dy, -1), move(every, -1) - every)
        f = [[0.03125 * (move(h, -ns * i) if i else h) + (1.0 if i == j else 0.0)
              for j, h in enumerate(slopes)] for i in range(3)]
        cof = [[f[(i + 1) % 3][(j + 1) % 3] * f[(i + 2) % 3][(j + 2) % 3]
                - f[(i + 1) % 3][(j + 2) % 3] * f[(i + 2) % 3][(j + 1) % 3]
                for j in range(3)] for i in range(3)]
        ratio = f[0][0] * cof[0][0] + f[0][1] * cof[0][1] + f[0][2] * cof[0][2]
        factor = (LAMBDA_BULK * jnp.log(ratio) - MU_SHEAR) / ratio
        back = []
        for j in range(3):
            parts = [jnp.where(lane < ns - 1, MU_SHEAR * f[i][j] + factor * cof[i][j], 0.0) for i in range(3)]
            back.append((parts[0] + move(parts[1], ns) + move(parts[2], 2 * ns)) * (0.03125 * REG_WEIGHT))
        gx = back[0] + move(back[0], 1)
        gy = back[1] + move(back[1], 1)
        gz = move(back[2], 1) - back[2]
        for dp, dq in ((0, 0), (0, 1), (1, 0), (1, 1)):
            add = (gx if dp else -gx) + (gy if dq else -gy) + gz
            pull[p + dp, dq:dq + nel] = pull[p + dp, dq:dq + nel] + add


def voxels(at, window, ref_rows, left, right, keep_low, keep_high):
    held = [None] * 8
    back = []
    rows = [None] * 8
    for half in range(2):
        run, tot, qrun, qtot, qtwo = ([None] * 3 for _ in range(5))
        inc = [(right(c, half) - left(c, half)) * 0.125 for c in range(3)]
        mv = [left(c, half) + 0.5 * inc[c] for c in range(3)]
        prev, cur = window(0, 0, half), window(1, 0, half)
        for k in range(8):
            nxt = window(k + 2, 0, half)
            g = [nxt - prev,
                 window(k + 1, 1, half) - window(k + 1, -1, half),
                 jnp.where(keep_high, pltpu.roll(cur, 127, 1), 0.0) - jnp.where(keep_low, pltpu.roll(cur, 1, 1), 0.0)]
            r = ref_rows(k, half) - cur
            for c in range(3):
                r = r - g[c] * mv[c]
                if k < 7:
                    mv[c] = mv[c] + inc[c]
            if half == 0:
                held[k] = r
            else:
                rows[k] = jnp.concatenate([held[k], r], axis=0).astype(BF16)
            for c in range(3):
                f = g[c] * r
                q = g[c] * g[c]
                run[c] = f if k == 0 else run[c] + f
                tot[c] = run[c] if k == 0 else tot[c] + run[c]
                qrun[c] = q if k == 0 else qrun[c] + q
                qtot[c] = qrun[c] if k == 0 else qtot[c] + qrun[c]
                qtwo[c] = qtot[c] if k == 0 else qtwo[c] + qtot[c]
            prev, cur = cur, nxt
        part = []
        for c in range(3):
            low = (tot[c] - 0.5 * run[c]) * 0.125
            lin = (qtot[c] - 0.5 * qrun[c]) * 0.125
            qlow = (qtwo[c] - qtot[c] + 0.125 * qrun[c]) * 0.03125
            part.append((low, run[c] - low, qlow, qrun[c] - 2.0 * lin + qlow))
        back.append(part)
    return rows, [[jnp.concatenate([back[0][c][i], back[1][c][i]], axis=0) for i in range(4)] for c in range(3)]


def tile_kernel(rim, map_ref, ref_hbm, ext, extra, field_hbm, pull, proj, proj2, down, down2,
                res_hbm, out,
                rows_in, win, ref_tile, field, res, sums, carry, gacc, dacc, rimcol,
                esem, rsem, fsem, osem):
    rows, cols, layers = ref_tile.shape
    steps = rows // 8
    comps = field.shape[2] // layers
    side = rim - 1
    wide_cols = cols + 2 * side
    start = map_ref[0] + side

    def fetch(first, count, k):
        return pltpu.make_async_copy(
            ext.at[pl.ds(start + first, count)], rows_in.at[pl.ds(first, count)], esem.at[k])

    def slab(p):
        return pltpu.make_async_copy(ref_hbm.at[pl.ds(8 * p, 8)], ref_tile.at[pl.ds(8 * p, 8)], rsem.at[p])

    def plane(p):
        return pltpu.make_async_copy(field_hbm.at[p], field.at[p], fsem.at[p])

    def store(p):
        return pltpu.make_async_copy(res.at[pl.ds(8 * p, 8)], res_hbm.at[pl.ds(8 * p, 8)], osem.at[p])

    fetch(0, 2, steps).start()
    plane(0).start()

    @pl.loop(0, steps)
    def _(k):
        fetch(8 * k + 2, 8, k).start()
        slab(k).start()
        plane(k + 1).start()

    def widen(first, count):
        for a in range(count):
            at = map_ref[0] + (SIDE - 1) + first + a
            win[first + a, 8:8 + wide_cols] = rows_in[first + a].astype(F32)
            win[first + a, 7:8] = rimcol[0, pl.ds(at, 1), :]
            win[first + a, 8 + wide_cols:9 + wide_cols] = rimcol[1, pl.ds(at, 1), :]

    rimcol[...] = extra[...].astype(F32)
    carry[...] = jnp.zeros_like(carry)
    fetch(0, 2, steps).wait()
    widen(0, 2)
    plane(0).wait()
    lane = lax.broadcasted_iota(jnp.int32, (8, layers), 1)
    keep_low, keep_high = lane > 0, lane < layers - 1
    col0 = map_ref[1] + 8 + side

    @pl.loop(0, steps)
    def _(p):
        base = pl.multiple_of(8 * p, 8)
        fetch(base + 2, 8, p).wait()
        widen(base + 2, 8)
        slab(p).wait()
        plane(p + 1).wait()

        @pl.loop(0, cols // 16)
        def _(j):
            at = pl.multiple_of(j * 16, 16)
            refs = [ref_tile[base + k, pl.ds(at, 16), :].astype(F32) for k in range(8)]
            out_rows, terms = voxels(
                at,
                lambda k, shift, half: win[base + k, pl.ds(col0 + at + (8 * half + shift), 8), :],
                lambda k, half: refs[k][8 * half:8 * half + 8],
                lambda c, half: field[p, pl.ds(at + 8 * half, 8), c * layers:(c + 1) * layers],
                lambda c, half: field[p + 1, pl.ds(at + 8 * half, 8), c * layers:(c + 1) * layers],
                keep_low, keep_high)
            for k in range(8):
                res[base + k, pl.ds(at, 16), :] = out_rows[k]
            for c in range(3):
                lanes = slice(c * layers, (c + 1) * layers)
                for i in range(2):
                    low, high = terms[c][2 * i:2 * i + 2]
                    head, tail = split(carry[i, pl.ds(at, 16), lanes] + low)
                    sums[p, i, pl.ds(at, 16), lanes] = head
                    sums[p, i, pl.ds(cols + at, 16), lanes] = tail
                    carry[i, pl.ds(at, 16), lanes] = high
        store(p).start()

    for i in range(2):
        head, tail = split(carry[i])
        sums[steps, i, 0:cols] = head
        sums[steps, i, cols:2 * cols] = tail
    for k, (acc, mat, table) in enumerate(((gacc, proj, down), (dacc, proj2, down2))):
        for i in range(steps + 1):
            acc[i] = jnp.dot(mat[...], sums[i, k], preferred_element_type=F32)
        head, tail = split(acc[...].reshape(-1, comps * layers))
        got = (jnp.dot(head, table[...], preferred_element_type=F32)
               + jnp.dot(tail, table[...], preferred_element_type=F32)).reshape(pull.shape)
        out[k] = got + pull[...] if k == 0 else got

    @pl.loop(0, steps)
    def _(k):
        store(k).wait()


def tile_terms(reference_tile, ext, extra, field, pull, offsets, tabs):
    rows, cols, layers = reference_tile.shape
    npx, _, lanes = field.shape
    rim = rows // 4 + 1
    steps = rows // 8
    anywhere = pl.BlockSpec(memory_space=pl.ANY)
    near = pl.BlockSpec(memory_space=pltpu.VMEM)
    wide_cols = cols + 2 * (rim - 1)
    return pl.pallas_call(
        functools.partial(tile_kernel, rim),
        out_shape=[jax.ShapeDtypeStruct(reference_tile.shape, BF16),
                   jax.ShapeDtypeStruct((2, npx, QPAD, 128), F32)],
        in_specs=[pl.BlockSpec(memory_space=pltpu.SMEM), anywhere, anywhere, near, anywhere, near] + [near] * 4,
        out_specs=[anywhere, near],
        scratch_shapes=[
            pltpu.VMEM((rows + 2, wide_cols, layers), BF16),
            pltpu.VMEM((rows + 2, wide_cols + 16, layers), F32),
            pltpu.VMEM((rows, cols, layers), BF16),
            pltpu.VMEM((npx, cols, lanes), F32),
            pltpu.VMEM((rows, cols, layers), BF16),
            pltpu.VMEM((npx, 2, 2 * cols, lanes), BF16),
            pltpu.VMEM((2, cols, lanes), F32),
            pltpu.VMEM((npx, QPAD, lanes), F32),
            pltpu.VMEM((npx, QPAD, lanes), F32),
            pltpu.VMEM(extra.shape, F32),
            pltpu.SemaphoreType.DMA((steps + 1,)),
            pltpu.SemaphoreType.DMA((steps,)),
            pltpu.SemaphoreType.DMA((npx,)),
            pltpu.SemaphoreType.DMA((steps,)),
        ],
        compiler_params=pltpu.CompilerParams(vmem_limit_bytes=58 << 20),
        name="tile",
    )(offsets, reference_tile, ext, extra, field, pull, *tabs)


def node_kernel(nw, nn, terms, disp, out, column, from_w, from_n, from_c, send, recv):
    comps, nel, _, ns = disp.shape
    w = lax.axis_index("wide")
    n = lax.axis_index("narrow")
    lo_w, hi_w, lo_n, hi_n = w > 0, w < nw - 1, n > 0, n < nn - 1
    up_w, dn_w = (w + 1, n), (w - 1, n)
    up_n, dn_n = (w, n + 1), (w, n - 1)
    for ref in (from_w, from_n, from_c):
        ref[...] = jnp.zeros_like(ref)
    barrier = pltpu.get_barrier_semaphore()
    for there, device in ((lo_w, dn_w), (hi_w, up_w), (lo_n, dn_n), (hi_n, up_n)):
        @pl.when(there)
        def _(device=device):
            pl.semaphore_signal(barrier, inc=1, device_id=device, device_id_type=MESH)
    for k in range(2):
        for p in range(nel):
            column[k, p:p + 1] = terms[k, p, nel:nel + 1]
    pl.semaphore_wait(barrier, as_int(lo_w) + as_int(hi_w) + as_int(lo_n) + as_int(hi_n))

    def remote(k, src, dst, device):
        return pltpu.make_async_remote_copy(
            src_ref=src, dst_ref=dst, send_sem=send.at[k], recv_sem=recv.at[k],
            device_id=device, device_id_type=MESH)

    wide_copy = remote(0, terms.at[:, nel], from_w, up_w)
    narrow_copy = remote(1, column, from_n, up_n)
    corner_copy = remote(2, from_w.at[:, nel:QPAD], from_c, up_n)

    @pl.when(hi_w)
    def _():
        wide_copy.start()

    @pl.when(hi_n)
    def _():
        narrow_copy.start()

    @pl.when(lo_w)
    def _():
        wide_copy.wait_recv()

    @pl.when(lo_w & hi_n)
    def _():
        corner_copy.start()

    @pl.when(lo_n)
    def _():
        narrow_copy.wait_recv()

    @pl.when(lo_w & lo_n)
    def _():
        corner_copy.wait_recv()

    top = lax.broadcasted_iota(jnp.int32, (nel, 128), 0) == 0
    for p in range(nel):
        sums = []
        for k in range(2):
            value = terms[k, p, 0:nel]
            side = from_n[k, p:p + 1]
            if p == 0:
                value = value + from_w[k, 0:nel]
                side = side + from_c[k, 0:1]
            sums.append(value + jnp.where(top, jnp.broadcast_to(side, (nel, 128)), 0.0))
        step = sums[0] / (sums[1] + STIFFNESS)
        for c in range(comps):
            here = step if c == 0 else pltpu.roll(step, 128 - ns * c, 1)
            out[c, p] = disp[c, p] - here[:, 0:ns]

    @pl.when(hi_w)
    def _():
        wide_copy.wait_send()

    @pl.when(hi_n)
    def _():
        narrow_copy.wait_send()

    @pl.when(lo_w & hi_n)
    def _():
        corner_copy.wait_send()


def node_update(terms, nodal, nw, nn):
    nel = nodal.shape[1]
    near = pl.BlockSpec(memory_space=pltpu.VMEM)
    return pl.pallas_call(
        functools.partial(node_kernel, nw, nn),
        out_shape=jax.ShapeDtypeStruct(nodal.shape, F32),
        in_specs=[near, near],
        out_specs=near,
        scratch_shapes=[
            pltpu.VMEM((2, nel, 128), F32),
            pltpu.VMEM((2, QPAD, 128), F32),
            pltpu.VMEM((2, nel, 128), F32),
            pltpu.VMEM((2, QPAD - nel, 128), F32),
            pltpu.SemaphoreType.DMA((3,)),
            pltpu.SemaphoreType.DMA((3,)),
        ],
        compiler_params=pltpu.CompilerParams(collective_id=1, has_side_effects=True),
        name="nodes",
    )(terms, nodal)


def per_device(nw, nn, reference_image, deformed_image, displacement, tile_map):
    comps = displacement.shape[0]
    nodal = displacement.transpose(0, 2, 3, 1)
    inter, proj, proj2, up, down, down2 = tables(*reference_image.shape, comps)
    ext, extra, field, pull = exchange(deformed_image, nodal, (inter, up), nw, nn)
    residual, terms = tile_terms(
        reference_image, ext, extra, field, pull, tile_map.reshape(2), (proj, proj2, down, down2))
    moved = node_update(terms, nodal, nw, nn)
    return (moved.transpose(0, 3, 1, 2), residual)


def solution(mesh):
    placed = (
        P("wide", "narrow", None),
        P("wide", "narrow", None),
        P(None, None, "wide", "narrow"),
        P("wide", "narrow", None),
    )
    return jax.shard_map(
        functools.partial(per_device, mesh.shape["wide"], mesh.shape["narrow"]),
        mesh=mesh,
        in_specs=placed,
        out_specs=(P(None, None, "wide", "narrow"), P("wide", "narrow", None)),
        check_vma=False,
    )
```

```python
import functools

import jax
import jax.numpy as jnp
import numpy as np
from jax import lax
from jax.experimental import pallas as pl
from jax.experimental.pallas import tpu as pltpu
from jax.sharding import PartitionSpec as P

MU_SHEAR = 1.0
LAMBDA_BULK = 2.0
REG_WEIGHT = 256.0
STIFFNESS = 16.0
MESH = pl.DeviceIdType.MESH
F32 = jnp.float32
BF16 = jnp.bfloat16
SIDE = 48
QPAD = 24


def as_int(flag):
    return flag.astype(jnp.int32)


def tables(rows, cols, layers, comps):
    def one(voxels):
        t = np.zeros((voxels, voxels // 8 + 1))
        for i in range(voxels):
            f = (i % 8 + 0.5) / 8.0
            t[i, i // 8] += 1.0 - f
            t[i, i // 8 + 1] += f
        return t
    ty, tz = one(cols), one(layers)
    nq, ns = ty.shape[1], tz.shape[1]
    typ = np.zeros((cols, QPAD))
    typ[:, :nq] = ty
    inter = 0.5 * np.concatenate([typ, typ], 1)
    proj = np.concatenate([typ.T, typ.T], 1)
    proj2 = np.concatenate([(typ * typ).T, (typ * typ).T], 1)
    lanes = comps * layers
    up = np.zeros((2 * 128, lanes))
    down = np.zeros((lanes, 128))
    down2 = np.zeros((lanes, 128))
    for c in range(comps):
        for h in range(2):
            up[h * 128 + c * ns:h * 128 + (c + 1) * ns, c * layers:(c + 1) * layers] = tz.T
        down[c * layers:(c + 1) * layers, c * ns:(c + 1) * ns] = -0.5 * tz
        down2[c * layers:(c + 1) * layers, c * ns:(c + 1) * ns] = 0.25 * tz * tz
    as_bf16 = lambda a: jnp.asarray(a.astype(BF16))
    return [as_bf16(a) for a in (inter, proj, proj2, up, down, down2)]


def split(value):
    high = value.astype(BF16)
    return high, (value - high.astype(F32)).astype(BF16)


def strain_pull(ns, nodes, pull):
    npx = nodes.shape[0]
    nel = npx - 1
    lane = lax.broadcasted_iota(jnp.int32, (nel, 128), 1)
    move = lambda a, by: pltpu.roll(a, by % 128, 1)
    pull[...] = jnp.zeros_like(pull)

    @pl.loop(0, nel)
    def _(p):
        a00, a01 = nodes[p, 0:nel], nodes[p, 1:nel + 1]
        a10, a11 = nodes[p + 1, 0:nel], nodes[p + 1, 1:nel + 1]
        dx = (a10 - a00) + (a11 - a01)
        dy = (a01 - a00) + (a11 - a10)
        every = (a00 + a01) + (a10 + a11)
        slopes = (dx + move(dx, -1), dy + move(dy, -1), move(every, -1) - every)
        f = [[0.03125 * (move(h, -ns * i) if i else h) + (1.0 if i == j else 0.0)
              for j, h in enumerate(slopes)] for i in range(3)]
        cof = [[f[(i + 1) % 3][(j + 1) % 3] * f[(i + 2) % 3][(j + 2) % 3]
                - f[(i + 1) % 3][(j + 2) % 3] * f[(i + 2) % 3][(j + 1) % 3]
                for j in range(3)] for i in range(3)]
        ratio = f[0][0] * cof[0][0] + f[0][1] * cof[0][1] + f[0][2] * cof[0][2]
        factor = (LAMBDA_BULK * jnp.log(ratio) - MU_SHEAR) / ratio
        back = []
        for j in range(3):
            parts = [jnp.where(lane < ns - 1, MU_SHEAR * f[i][j] + factor * cof[i][j], 0.0) for i in range(3)]
            back.append((parts[0] + move(parts[1], ns) + move(parts[2], 2 * ns)) * (0.03125 * REG_WEIGHT))
        gx = back[0] + move(back[0], 1)
        gy = back[1] + move(back[1], 1)
        gz = move(back[2], 1) - back[2]
        for dp, dq in ((0, 0), (0, 1), (1, 0), (1, 1)):
            add = (gx if dp else -gx) + (gy if dq else -gy) + gz
            pull[p + dp, dq:dq + nel] = pull[p + dp, dq:dq + nel] + add


def voxels(at, window, ref_rows, left, right, keep_low, keep_high):
    held = [None] * 8
    back = []
    rows = [None] * 8
    for half in range(2):
        run, tot, qrun, qtot, qtwo = ([None] * 3 for _ in range(5))
        inc = [(right(c, half) - left(c, half)) * 0.125 for c in range(3)]
        mv = [left(c, half) + 0.5 * inc[c] for c in range(3)]
        prev, cur = window(0, 0, half), window(1, 0, half)
        for k in range(8):
            nxt = window(k + 2, 0, half)
            g = [nxt - prev,
                 window(k + 1, 1, half) - window(k + 1, -1, half),
                 jnp.where(keep_high, pltpu.roll(cur, 127, 1), 0.0) - jnp.where(keep_low, pltpu.roll(cur, 1, 1), 0.0)]
            r = ref_rows(k, half) - cur
            for c in range(3):
                r = r - g[c] * mv[c]
                if k < 7:
                    mv[c] = mv[c] + inc[c]
            if half == 0:
                held[k] = r
            else:
                rows[k] = jnp.concatenate([held[k], r], axis=0).astype(BF16)
            for c in range(3):
                f = g[c] * r
                q = g[c] * g[c]
                run[c] = f if k == 0 else run[c] + f
                tot[c] = run[c] if k == 0 else tot[c] + run[c]
                qrun[c] = q if k == 0 else qrun[c] + q
                qtot[c] = qrun[c] if k == 0 else qtot[c] + qrun[c]
                qtwo[c] = qtot[c] if k == 0 else qtwo[c] + qtot[c]
            prev, cur = cur, nxt
        part = []
        for c in range(3):
            low = (tot[c] - 0.5 * run[c]) * 0.125
            lin = (qtot[c] - 0.5 * qrun[c]) * 0.125
            qlow = (qtwo[c] - qtot[c] + 0.125 * qrun[c]) * 0.03125
            part.append((low, run[c] - low, qlow, qrun[c] - 2.0 * lin + qlow))
        back.append(part)
    return rows, [[jnp.concatenate([back[0][c][i], back[1][c][i]], axis=0) for i in range(4)] for c in range(3)]


def step_kernel(nw, nn, rim, ns, map_ref, own, ref_hbm, disp, inter, proj, proj2, up, down, down2,
                res_hbm, change,
                ext, passed, win, ref_tile, res, field, sums, carry, gacc, dacc, terms,
                extra, rimcol, nodes, pull, cube, column, side_in, corner_in, colf, colb,
                from_w, from_n, from_c, send, recv, lsem, osem):
    rows, cols, layers = own.shape
    comps, nel = disp.shape[0], disp.shape[1]
    side = rim - 1
    w = lax.axis_index("wide")
    n = lax.axis_index("narrow")
    lo_w, hi_w, lo_n, hi_n = w > 0, w < nw - 1, n > 0, n < nn - 1
    up_w, dn_w = (w + 1, n), (w - 1, n)
    up_n, dn_n = (w, n + 1), (w, n - 1)
    mid = slice(side, side + cols)
    ylo = slice(0, side)
    yhi = slice(side + cols, 2 * side + cols)
    total = rows + 2 * rim
    emid = slice(SIDE, SIDE + rows)
    detour = nw == 8
    is0, is3, is4, is7 = (w == 0), (w == 3), (w == 4), (w == 7)

    local = pltpu.make_async_copy(own, ext.at[rim:rim + rows, mid], lsem.at[0])
    local.start()
    slab = pltpu.make_async_copy(ref_hbm, ref_tile, lsem.at[1])
    slab.start()
    extra[...] = jnp.zeros_like(extra)
    side_in[...] = jnp.zeros_like(side_in)
    corner_in[...] = jnp.zeros_like(corner_in)
    for ref in (from_w, from_n, from_c):
        ref[...] = jnp.zeros_like(ref)
    nodes[nel] = jnp.zeros(nodes.shape[1:], F32)
    cube[...] = jnp.zeros_like(cube)
    cube[:, :, :, 0:ns] = disp[...]
    for i in range(nel):
        value = cube[0, i]
        for c in range(1, comps):
            value = value + pltpu.roll(cube[c, i], ns * c, 1)
        nodes[i, 0:nel] = value
        column[i:i + 1] = value[0:1]

    barrier = pltpu.get_barrier_semaphore()
    greet = [(lo_w, dn_w), (hi_w, up_w), (lo_n, dn_n), (hi_n, up_n)]
    if detour:
        greet += [(is7, (3, n)), (is4, (7, n)), (is0, (4, n)), (is3, (0, n))]
    count = as_int(lo_w) + as_int(hi_w) + as_int(lo_n) + as_int(hi_n)
    if detour:
        count = count + as_int(is0 | is3 | is4 | is7)
    for there, device in greet:
        @pl.when(there)
        def _(device=device):
            pl.semaphore_signal(barrier, inc=1, device_id=device, device_id_type=MESH)
    pl.semaphore_wait(barrier, count)

    everything = []

    def remote(goes, comes, src, dst, device):
        k = len(everything)
        copy = pltpu.make_async_remote_copy(
            src_ref=src, dst_ref=dst, send_sem=send.at[k], recv_sem=recv.at[k],
            device_id=device, device_id_type=MESH)
        everything.append((goes, comes, copy))
        return k

    def go(*ks):
        for k in ks:
            @pl.when(everything[k][0])
            def _(k=k):
                everything[k][2].start()

    def come(*ks):
        for k in ks:
            @pl.when(everything[k][1])
            def _(k=k):
                everything[k][2].wait_recv()

    below, above = slice(0, rim), slice(rim + rows, total)
    edge_x = remote(lo_w, hi_w, nodes.at[0, 0:nel], nodes.at[nel, 0:nel], dn_w)
    edge_y = remote(lo_n, hi_n, column, side_in, dn_n)
    strips = []
    full = (slice(0, rim), slice(rows - rim, rows), slice(rim, rows - rim))
    for part in full:
        there = slice(part.start + rim, part.stop + rim)
        strips.append((
            remote(hi_n, lo_n, own.at[part, cols - side:cols], ext.at[there, ylo], up_n),
            remote(lo_n, hi_n, own.at[part, 0:side], ext.at[there, yhi], dn_n)))
    cut = cols // 4 if detour else cols
    near, far = slice(0, cut), slice(cut, cols)
    enear, efar = slice(side, side + cut), slice(side + cut, side + cols)
    high_own, low_own = slice(rows - rim, rows), slice(0, rim)
    bands = [
        remote(hi_w, lo_w, own.at[high_own, near], ext.at[below, enear], up_w),
        remote(lo_w, hi_w, own.at[low_own, near], ext.at[above, enear], dn_w)]
    first_hop, second_hop = [], []
    if detour:
        bands += [
            remote(hi_w & (w != 3), lo_w & (w != 4), own.at[high_own, far], ext.at[below, efar], up_w),
            remote(lo_w & (w != 4), hi_w & (w != 3), own.at[low_own, far], ext.at[above, efar], dn_w)]
        first_hop = [
            remote(is3, is7, own.at[high_own, far], passed, (7, n)),
            remote(is4, is0, own.at[low_own, far], passed, (0, n))]
        second_hop = [
            remote(is7, is4, passed, ext.at[below, efar], (4, n)),
            remote(is0, is3, passed, ext.at[above, efar], (3, n))]
    go(edge_x, edge_y, *strips[0], *strips[1], *first_hop, *bands)

    def widen(first, count, columns, together):
        to = slice(columns.start + 8, columns.stop + 8)

        @pl.loop(0, count // together)
        def _(b):
            for a in range(together):
                win[first + together * b + a, to] = ext[first + together * b + a, columns].astype(F32)
        for r in range(first + count // together * together, first + count):
            win[r, to] = ext[r, columns].astype(F32)

    local.wait()
    picks = (side + cols - rim, side + rim - 1)

    @pl.loop(0, rows // 8)
    def _(b):
        for a in range(8):
            for i, col in enumerate(picks):
                tile = ext[rim + 8 * b + a, col // 16 * 16:col // 16 * 16 + 16, :].astype(F32)
                colf[i, pl.ds(8 * b + a, 1), :] = tile[col % 16:col % 16 + 1]
    colb[...] = colf[...].astype(BF16)
    elow, ehigh = slice(SIDE, 2 * SIDE), slice(rows, SIDE + rows)
    ebelow, eabove = slice(0, SIDE), slice(SIDE + rows, 2 * SIDE + rows)
    thin = [remote(hi_n, lo_n, colb.at[0], extra.at[0, emid], up_n),
            remote(lo_n, hi_n, colb.at[1], extra.at[1, emid], dn_n)]
    go(*thin)

    @pl.when(jnp.logical_not(lo_n))
    def _():
        ext[:, ylo] = jnp.zeros((total, side, layers), BF16)

    @pl.when(jnp.logical_not(hi_n))
    def _():
        ext[:, yhi] = jnp.zeros((total, side, layers), BF16)

    @pl.when(jnp.logical_not(lo_w))
    def _():
        ext[below] = jnp.zeros((rim, cols + 2 * side, layers), BF16)

    @pl.when(jnp.logical_not(hi_w))
    def _():
        ext[above] = jnp.zeros((rim, cols + 2 * side, layers), BF16)

    come(edge_x)
    edge_c = remote(hi_w & lo_n, hi_w & hi_n, nodes.at[nel, 0:8], corner_in, dn_n)
    go(edge_c)
    come(edge_y)
    top = lax.broadcasted_iota(jnp.int32, (QPAD - nel, 128), 0) == 0
    for i in range(nel):
        nodes[i, nel:QPAD] = jnp.where(top, jnp.broadcast_to(side_in[i:i + 1], (QPAD - nel, 128)), 0.0)
    come(edge_c)
    nodes[nel, nel:QPAD] = jnp.where(top, jnp.broadcast_to(corner_in[0:1], (QPAD - nel, 128)), 0.0)
    strain_pull(ns, nodes, pull)
    come(*first_hop)
    go(*second_hop)
    corners = []
    come(*strips[0], *strips[1])
    corners += [
        remote(hi_w & lo_n, lo_w & lo_n, ext.at[rows:rows + rim, ylo], ext.at[below, ylo], up_w),
        remote(hi_w & hi_n, lo_w & hi_n, ext.at[rows:rows + rim, yhi], ext.at[below, yhi], up_w),
        remote(lo_w & lo_n, hi_w & lo_n, ext.at[rim:2 * rim, ylo], ext.at[above, ylo], dn_w),
        remote(lo_w & hi_n, hi_w & hi_n, ext.at[rim:2 * rim, yhi], ext.at[above, yhi], dn_w)]
    come(*thin)
    corners += [
        remote(lo_n & lo_w, lo_n & hi_w, extra.at[0, elow], extra.at[0, eabove], dn_w),
        remote(lo_n & hi_w, lo_n & lo_w, extra.at[0, ehigh], extra.at[0, ebelow], up_w),
        remote(hi_n & lo_w, hi_n & hi_w, extra.at[1, elow], extra.at[1, eabove], dn_w),
        remote(hi_n & hi_w, hi_n & lo_w, extra.at[1, ehigh], extra.at[1, ebelow], up_w)]
    go(*corners)
    for k in strips[0] + strips[1]:
        @pl.when(everything[k][0])
        def _(k=k):
            everything[k][2].wait_send()
    go(*strips[2])

    flat = nodes[...].reshape(-1, 128)
    high = flat.astype(BF16).astype(F32)
    both = jnp.concatenate([high, flat - high], axis=1).astype(BF16)
    level = jnp.dot(both, up[...], preferred_element_type=F32)
    for i in range(nel + 1):
        head, tail = split(level[i * QPAD:(i + 1) * QPAD])
        field[i] = jnp.dot(inter[...], jnp.concatenate([head, tail], axis=0), preferred_element_type=F32)
    carry[...] = jnp.zeros_like(carry)
    widen(rim, rows, mid, 2)
    for part in full[:2]:
        widen(part.start + rim, rim, ylo, 4)
        widen(part.start + rim, rim, yhi, 4)
    come(*strips[2])
    widen(2 * rim, rows - 2 * rim, ylo, 4)
    widen(2 * rim, rows - 2 * rim, yhi, 4)
    come(*bands, *second_hop)
    widen(0, rim, mid, 2)
    widen(rim + rows, rim, mid, 2)
    come(*corners)
    for first in (0, rim + rows):
        widen(first, rim, ylo, 4)
        widen(first, rim, yhi, 4)
    rimcol[...] = extra[...].astype(F32)
    spots = (7, 8 + cols + 2 * side)

    @pl.loop(0, total // 2)
    def _(b):
        for a in range(2):
            for i, spot in enumerate(spots):
                win[2 * b + a, spot:spot + 1] = rimcol[i, pl.ds(SIDE - rim + 2 * b + a, 1), :]

    slab.wait()
    steps = rows // 8
    start = map_ref[0] + side
    col0 = map_ref[1] + 8 + side
    lane = lax.broadcasted_iota(jnp.int32, (8, layers), 1)
    keep_low, keep_high = lane > 0, lane < layers - 1

    def store(p):
        return pltpu.make_async_copy(res.at[pl.ds(8 * p, 8)], res_hbm.at[pl.ds(8 * p, 8)], osem.at[p])

    @pl.loop(0, steps)
    def _(p):
        base = pl.multiple_of(8 * p, 8)
        row0 = start + base

        @pl.loop(0, cols // 16)
        def _(j):
            at = pl.multiple_of(j * 16, 16)
            refs = [ref_tile[base + k, pl.ds(at, 16), :].astype(F32) for k in range(8)]
            out_rows, parts = voxels(
                at,
                lambda k, shift, half: win[row0 + k, pl.ds(col0 + at + (8 * half + shift), 8), :],
                lambda k, half: refs[k][8 * half:8 * half + 8],
                lambda c, half: field[p, pl.ds(at + 8 * half, 8), c * layers:(c + 1) * layers],
                lambda c, half: field[p + 1, pl.ds(at + 8 * half, 8), c * layers:(c + 1) * layers],
                keep_low, keep_high)
            for k in range(8):
                res[base + k, pl.ds(at, 16), :] = out_rows[k]
            for c in range(comps):
                lanes = slice(c * layers, (c + 1) * layers)
                for i in range(2):
                    low, high = parts[c][2 * i:2 * i + 2]
                    head, tail = split(carry[i, pl.ds(at, 16), lanes] + low)
                    sums[p, i, pl.ds(at, 16), lanes] = head
                    sums[p, i, pl.ds(cols + at, 16), lanes] = tail
                    carry[i, pl.ds(at, 16), lanes] = high
        store(p).start()

    for i in range(2):
        head, tail = split(carry[i])
        sums[steps, i, 0:cols] = head
        sums[steps, i, cols:2 * cols] = tail
    for k, (acc, mat, table) in enumerate(((gacc, proj, down), (dacc, proj2, down2))):
        for i in range(steps + 1):
            acc[i] = jnp.dot(mat[...], sums[i, k], preferred_element_type=F32)
        head, tail = split(acc[...].reshape(-1, comps * layers))
        got = (jnp.dot(head, table[...], preferred_element_type=F32)
               + jnp.dot(tail, table[...], preferred_element_type=F32)).reshape(pull.shape)
        terms[k] = got + pull[...] if k == 0 else got

    for k in range(2):
        for p in range(nel):
            colf[k, p:p + 1] = terms[k, p, nel:nel + 1]
    to_w = remote(hi_w, lo_w, terms.at[:, nel], from_w, up_w)
    to_n = remote(hi_n, lo_n, colf.at[:, 0:nel], from_n, up_n)
    to_c = remote(lo_w & hi_n, lo_w & lo_n, from_w.at[:, nel:QPAD], from_c, up_n)
    go(to_w, to_n)
    come(to_w)
    go(to_c)
    come(to_n, to_c)
    first_row = lax.broadcasted_iota(jnp.int32, (nel, 128), 0) == 0
    for p in range(nel):
        both = []
        for k in range(2):
            value = terms[k, p, 0:nel]
            beside = from_n[k, p:p + 1]
            if p == 0:
                value = value + from_w[k, 0:nel]
                beside = beside + from_c[k, 0:1]
            both.append(value + jnp.where(first_row, jnp.broadcast_to(beside, (nel, 128)), 0.0))
        step = both[0] / (both[1] + STIFFNESS)
        for c in range(comps):
            here = step if c == 0 else pltpu.roll(step, 128 - ns * c, 1)
            change[c, p] = here[:, 0:ns]
    sent = strips[0] + strips[1]
    for k, (goes, _c, copy) in enumerate(everything):
        if k not in sent:
            @pl.when(goes)
            def _(copy=copy):
                copy.wait_send()

    @pl.loop(0, steps)
    def _(k):
        store(k).wait()


def per_device(nw, nn, reference_image, deformed_image, displacement, tile_map):
    comps, ns, nel, _ = displacement.shape
    rows, cols, layers = reference_image.shape
    nodal = displacement.transpose(0, 2, 3, 1)
    tabs = tables(rows, cols, layers, comps)
    rim = rows // 4 + 1
    steps, npx, lanes = rows // 8, nel + 1, comps * layers
    total, across = rows + 2 * rim, cols + 2 * (rim - 1)
    anywhere = pl.BlockSpec(memory_space=pl.ANY)
    near = pl.BlockSpec(memory_space=pltpu.VMEM)
    residual, change = pl.pallas_call(
        functools.partial(step_kernel, nw, nn, rim, ns),
        out_shape=[jax.ShapeDtypeStruct(reference_image.shape, BF16),
                   jax.ShapeDtypeStruct(nodal.shape, F32)],
        in_specs=[pl.BlockSpec(memory_space=pltpu.SMEM), anywhere, anywhere] + [near] * 7,
        out_specs=[anywhere, near],
        scratch_shapes=[
            pltpu.VMEM((total, across, layers), BF16),
            pltpu.VMEM((rim, cols - cols // 4, layers), BF16),
            pltpu.VMEM((total, across + 16, layers), F32),
            pltpu.VMEM((rows, cols, layers), BF16),
            pltpu.VMEM((rows, cols, layers), BF16),
            pltpu.VMEM((npx, cols, lanes), F32),
            pltpu.VMEM((npx, 2, 2 * cols, lanes), BF16),
            pltpu.VMEM((2, cols, lanes), F32),
            pltpu.VMEM((npx, QPAD, lanes), F32),
            pltpu.VMEM((npx, QPAD, lanes), F32),
            pltpu.VMEM((2, npx, QPAD, 128), F32),
            pltpu.VMEM((2, rows + 2 * SIDE, layers), BF16),
            pltpu.VMEM((2, rows + 2 * SIDE, layers), F32),
            pltpu.VMEM((npx, QPAD, 128), F32),
            pltpu.VMEM((npx, QPAD, 128), F32),
            pltpu.VMEM((comps, nel, nel, 128), F32),
            pltpu.VMEM((nel, 128), F32),
            pltpu.VMEM((nel, 128), F32),
            pltpu.VMEM((8, 128), F32),
            pltpu.VMEM((2, rows, layers), F32),
            pltpu.VMEM((2, rows, layers), BF16),
            pltpu.VMEM((2, QPAD, 128), F32),
            pltpu.VMEM((2, nel, 128), F32),
            pltpu.VMEM((2, QPAD - nel, 128), F32),
            pltpu.SemaphoreType.DMA((34,)),
            pltpu.SemaphoreType.DMA((34,)),
            pltpu.SemaphoreType.DMA((2,)),
            pltpu.SemaphoreType.DMA((steps,)),
        ],
        compiler_params=pltpu.CompilerParams(
            collective_id=0, has_side_effects=True, vmem_limit_bytes=62 << 20),
        name="step",
    )(tile_map.reshape(2), deformed_image, reference_image, nodal, *tabs)
    return (displacement - change.transpose(0, 3, 1, 2), residual)


def solution(mesh):
    placed = (
        P("wide", "narrow", None),
        P("wide", "narrow", None),
        P(None, None, "wide", "narrow"),
        P("wide", "narrow", None),
    )
    return jax.shard_map(
        functools.partial(per_device, mesh.shape["wide"], mesh.shape["narrow"]),
        mesh=mesh,
        in_specs=placed,
        out_specs=(P(None, None, "wide", "narrow"), P("wide", "narrow", None)),
        check_vma=False,
    )
```

```python
import functools

import jax
import jax.numpy as jnp
import numpy as np
from jax import lax
from jax.experimental import pallas as pl
from jax.experimental.pallas import tpu as pltpu
from jax.sharding import PartitionSpec as P

MU_SHEAR = 1.0
LAMBDA_BULK = 2.0
REG_WEIGHT = 256.0
STIFFNESS = 16.0
MESH = pl.DeviceIdType.MESH
F32 = jnp.float32
BF16 = jnp.bfloat16
SIDE = 48
QPAD = 24


def as_int(flag):
    return flag.astype(jnp.int32)


def tables(rows, cols, layers, comps):
    def one(voxels):
        t = np.zeros((voxels, voxels // 8 + 1))
        for i in range(voxels):
            f = (i % 8 + 0.5) / 8.0
            t[i, i // 8] += 1.0 - f
            t[i, i // 8 + 1] += f
        return t
    ty, tz = one(cols), one(layers)
    nq, ns = ty.shape[1], tz.shape[1]
    typ = np.zeros((cols, QPAD))
    typ[:, :nq] = ty
    inter = 0.5 * np.concatenate([typ, typ], 1)
    proj = np.concatenate([typ.T, typ.T], 1)
    proj2 = np.concatenate([(typ * typ).T, (typ * typ).T], 1)
    lanes = comps * layers
    up = np.zeros((2 * 128, lanes))
    down = np.zeros((lanes, 128))
    down2 = np.zeros((lanes, 128))
    for c in range(comps):
        for h in range(2):
            up[h * 128 + c * ns:h * 128 + (c + 1) * ns, c * layers:(c + 1) * layers] = tz.T
        down[c * layers:(c + 1) * layers, c * ns:(c + 1) * ns] = -0.5 * tz
        down2[c * layers:(c + 1) * layers, c * ns:(c + 1) * ns] = 0.25 * tz * tz
    as_bf16 = lambda a: jnp.asarray(a.astype(BF16))
    return [as_bf16(a) for a in (inter, proj, proj2, up, down, down2)]


def split(value):
    high = value.astype(BF16)
    return high, (value - high.astype(F32)).astype(BF16)


def strain_pull(ns, nodes, pull):
    npx = nodes.shape[0]
    nel = npx - 1
    lane = lax.broadcasted_iota(jnp.int32, (nel, 128), 1)
    move = lambda a, by: pltpu.roll(a, by % 128, 1)
    pull[...] = jnp.zeros_like(pull)

    @pl.loop(0, nel)
    def _(p):
        a00, a01 = nodes[p, 0:nel], nodes[p, 1:nel + 1]
        a10, a11 = nodes[p + 1, 0:nel], nodes[p + 1, 1:nel + 1]
        dx = (a10 - a00) + (a11 - a01)
        dy = (a01 - a00) + (a11 - a10)
        every = (a00 + a01) + (a10 + a11)
        slopes = (dx + move(dx, -1), dy + move(dy, -1), move(every, -1) - every)
        f = [[0.03125 * (move(h, -ns * i) if i else h) + (1.0 if i == j else 0.0)
              for j, h in enumerate(slopes)] for i in range(3)]
        cof = [[f[(i + 1) % 3][(j + 1) % 3] * f[(i + 2) % 3][(j + 2) % 3]
                - f[(i + 1) % 3][(j + 2) % 3] * f[(i + 2) % 3][(j + 1) % 3]
                for j in range(3)] for i in range(3)]
        ratio = f[0][0] * cof[0][0] + f[0][1] * cof[0][1] + f[0][2] * cof[0][2]
        factor = (LAMBDA_BULK * jnp.log(ratio) - MU_SHEAR) / ratio
        back = []
        for j in range(3):
            parts = [jnp.where(lane < ns - 1, MU_SHEAR * f[i][j] + factor * cof[i][j], 0.0) for i in range(3)]
            back.append((parts[0] + move(parts[1], ns) + move(parts[2], 2 * ns)) * (0.03125 * REG_WEIGHT))
        gx = back[0] + move(back[0], 1)
        gy = back[1] + move(back[1], 1)
        gz = move(back[2], 1) - back[2]
        for dp, dq in ((0, 0), (0, 1), (1, 0), (1, 1)):
            add = (gx if dp else -gx) + (gy if dq else -gy) + gz
            pull[p + dp, dq:dq + nel] = pull[p + dp, dq:dq + nel] + add


def voxels(at, window, ref_rows, left, right, keep_low, keep_high):
    held = [None] * 8
    back = []
    rows = [None] * 8
    for half in range(2):
        run, tot, qrun, qtot, qtwo = ([None] * 3 for _ in range(5))
        inc = [(right(c, half) - left(c, half)) * 0.125 for c in range(3)]
        mv = [left(c, half) + 0.5 * inc[c] for c in range(3)]
        prev, cur = window(0, 0, half), window(1, 0, half)
        for k in range(8):
            nxt = window(k + 2, 0, half)
            g = [nxt - prev,
                 window(k + 1, 1, half) - window(k + 1, -1, half),
                 jnp.where(keep_high, pltpu.roll(cur, 127, 1), 0.0) - jnp.where(keep_low, pltpu.roll(cur, 1, 1), 0.0)]
            r = ref_rows(k, half) - cur
            for c in range(3):
                r = r - g[c] * mv[c]
                if k < 7:
                    mv[c] = mv[c] + inc[c]
            if half == 0:
                held[k] = r
            else:
                rows[k] = jnp.concatenate([held[k], r], axis=0).astype(BF16)
            for c in range(3):
                f = g[c] * r
                q = g[c] * g[c]
                run[c] = f if k == 0 else run[c] + f
                tot[c] = run[c] if k == 0 else tot[c] + run[c]
                qrun[c] = q if k == 0 else qrun[c] + q
                qtot[c] = qrun[c] if k == 0 else qtot[c] + qrun[c]
                qtwo[c] = qtot[c] if k == 0 else qtwo[c] + qtot[c]
            prev, cur = cur, nxt
        part = []
        for c in range(3):
            low = (tot[c] - 0.5 * run[c]) * 0.125
            lin = (qtot[c] - 0.5 * qrun[c]) * 0.125
            qlow = (qtwo[c] - qtot[c] + 0.125 * qrun[c]) * 0.03125
            part.append((low, run[c] - low, qlow, qrun[c] - 2.0 * lin + qlow))
        back.append(part)
    return rows, [[jnp.concatenate([back[0][c][i], back[1][c][i]], axis=0) for i in range(4)] for c in range(3)]


def step_kernel(nw, nn, rim, ns, map_ref, own, ref_hbm, disp, inter, proj, proj2, up, down, down2,
                res, change,
                ext, passed, win, field, sums, carry, gacc, dacc, terms,
                extra, rimcol, nodes, pull, cube, column, side_in, corner_in, colf, colb,
                from_w, from_n, from_c, send, recv, lsem):
    rows, cols, layers = own.shape
    comps, nel = disp.shape[0], disp.shape[1]
    side = rim - 1
    w = lax.axis_index("wide")
    n = lax.axis_index("narrow")
    lo_w, hi_w, lo_n, hi_n = w > 0, w < nw - 1, n > 0, n < nn - 1
    up_w, dn_w = (w + 1, n), (w - 1, n)
    up_n, dn_n = (w, n + 1), (w, n - 1)
    mid = slice(side, side + cols)
    ylo = slice(0, side)
    yhi = slice(side + cols, 2 * side + cols)
    total = rows + 2 * rim
    emid = slice(SIDE, SIDE + rows)
    detour = nw == 8
    is0, is3, is4, is7 = (w == 0), (w == 3), (w == 4), (w == 7)

    local = pltpu.make_async_copy(own, ext.at[rim:rim + rows, mid], lsem.at[0])
    local.start()
    slab = pltpu.make_async_copy(ref_hbm, res, lsem.at[1])
    slab.start()
    extra[...] = jnp.zeros_like(extra)
    side_in[...] = jnp.zeros_like(side_in)
    corner_in[...] = jnp.zeros_like(corner_in)
    for ref in (from_w, from_n, from_c):
        ref[...] = jnp.zeros_like(ref)
    nodes[nel] = jnp.zeros(nodes.shape[1:], F32)
    cube[...] = jnp.zeros_like(cube)
    cube[:, :, :, 0:ns] = disp[...]
    for i in range(nel):
        value = cube[0, i]
        for c in range(1, comps):
            value = value + pltpu.roll(cube[c, i], ns * c, 1)
        nodes[i, 0:nel] = value
        column[i:i + 1] = value[0:1]

    barrier = pltpu.get_barrier_semaphore()
    greet = [(lo_w, dn_w), (hi_w, up_w), (lo_n, dn_n), (hi_n, up_n)]
    if detour:
        greet += [(is7, (3, n)), (is4, (7, n)), (is0, (4, n)), (is3, (0, n))]
    count = as_int(lo_w) + as_int(hi_w) + as_int(lo_n) + as_int(hi_n)
    if detour:
        count = count + as_int(is0 | is3 | is4 | is7)
    for there, device in greet:
        @pl.when(there)
        def _(device=device):
            pl.semaphore_signal(barrier, inc=1, device_id=device, device_id_type=MESH)
    pl.semaphore_wait(barrier, count)

    everything = []

    def remote(goes, comes, src, dst, device):
        k = len(everything)
        copy = pltpu.make_async_remote_copy(
            src_ref=src, dst_ref=dst, send_sem=send.at[k], recv_sem=recv.at[k],
            device_id=device, device_id_type=MESH)
        everything.append((goes, comes, copy))
        return k

    def go(*ks):
        for k in ks:
            @pl.when(everything[k][0])
            def _(k=k):
                everything[k][2].start()

    def come(*ks):
        for k in ks:
            @pl.when(everything[k][1])
            def _(k=k):
                everything[k][2].wait_recv()

    below, above = slice(0, rim), slice(rim + rows, total)
    edge_x = remote(lo_w, hi_w, nodes.at[0, 0:nel], nodes.at[nel, 0:nel], dn_w)
    edge_y = remote(lo_n, hi_n, column, side_in, dn_n)
    strips = []
    full = (slice(0, rim), slice(rows - rim, rows), slice(rim, rows - rim))
    for part in full:
        there = slice(part.start + rim, part.stop + rim)
        strips.append((
            remote(hi_n, lo_n, own.at[part, cols - side:cols], ext.at[there, ylo], up_n),
            remote(lo_n, hi_n, own.at[part, 0:side], ext.at[there, yhi], dn_n)))
    cut = cols // 4 if detour else cols
    near, far = slice(0, cut), slice(cut, cols)
    enear, efar = slice(side, side + cut), slice(side + cut, side + cols)
    high_own, low_own = slice(rows - rim, rows), slice(0, rim)
    bands = [
        remote(hi_w, lo_w, own.at[high_own, near], ext.at[below, enear], up_w),
        remote(lo_w, hi_w, own.at[low_own, near], ext.at[above, enear], dn_w)]
    first_hop, second_hop = [], []
    if detour:
        bands += [
            remote(hi_w & (w != 3), lo_w & (w != 4), own.at[high_own, far], ext.at[below, efar], up_w),
            remote(lo_w & (w != 4), hi_w & (w != 3), own.at[low_own, far], ext.at[above, efar], dn_w)]
        first_hop = [
            remote(is3, is7, own.at[high_own, far], passed, (7, n)),
            remote(is4, is0, own.at[low_own, far], passed, (0, n))]
        second_hop = [
            remote(is7, is4, passed, ext.at[below, efar], (4, n)),
            remote(is0, is3, passed, ext.at[above, efar], (3, n))]
    go(edge_x, edge_y, *strips[0], *strips[1], *first_hop, *bands)

    def widen(first, count, columns, together):
        to = slice(columns.start + 8, columns.stop + 8)

        @pl.loop(0, count // together)
        def _(b):
            for a in range(together):
                win[first + together * b + a, to] = ext[first + together * b + a, columns].astype(F32)
        for r in range(first + count // together * together, first + count):
            win[r, to] = ext[r, columns].astype(F32)

    local.wait()
    picks = (side + cols - rim, side + rim - 1)

    @pl.loop(0, rows // 8)
    def _(b):
        for a in range(8):
            for i, col in enumerate(picks):
                tile = ext[rim + 8 * b + a, col // 16 * 16:col // 16 * 16 + 16, :].astype(F32)
                colf[i, pl.ds(8 * b + a, 1), :] = tile[col % 16:col % 16 + 1]
    colb[...] = colf[...].astype(BF16)
    elow, ehigh = slice(SIDE, 2 * SIDE), slice(rows, SIDE + rows)
    ebelow, eabove = slice(0, SIDE), slice(SIDE + rows, 2 * SIDE + rows)
    thin = [remote(hi_n, lo_n, colb.at[0], extra.at[0, emid], up_n),
            remote(lo_n, hi_n, colb.at[1], extra.at[1, emid], dn_n)]
    go(*thin)

    @pl.when(jnp.logical_not(lo_n))
    def _():
        ext[:, ylo] = jnp.zeros((total, side, layers), BF16)

    @pl.when(jnp.logical_not(hi_n))
    def _():
        ext[:, yhi] = jnp.zeros((total, side, layers), BF16)

    @pl.when(jnp.logical_not(lo_w))
    def _():
        ext[below] = jnp.zeros((rim, cols + 2 * side, layers), BF16)

    @pl.when(jnp.logical_not(hi_w))
    def _():
        ext[above] = jnp.zeros((rim, cols + 2 * side, layers), BF16)

    widen(rim, rows, mid, 2)
    come(edge_x)
    edge_c = remote(hi_w & lo_n, hi_w & hi_n, nodes.at[nel, 0:8], corner_in, dn_n)
    go(edge_c)
    come(edge_y)
    top = lax.broadcasted_iota(jnp.int32, (QPAD - nel, 128), 0) == 0
    for i in range(nel):
        nodes[i, nel:QPAD] = jnp.where(top, jnp.broadcast_to(side_in[i:i + 1], (QPAD - nel, 128)), 0.0)
    come(edge_c)
    nodes[nel, nel:QPAD] = jnp.where(top, jnp.broadcast_to(corner_in[0:1], (QPAD - nel, 128)), 0.0)
    come(*first_hop)
    go(*second_hop)
    corners = []
    come(*strips[0], *strips[1])
    corners += [
        remote(hi_w & lo_n, lo_w & lo_n, ext.at[rows:rows + rim, ylo], ext.at[below, ylo], up_w),
        remote(hi_w & hi_n, lo_w & hi_n, ext.at[rows:rows + rim, yhi], ext.at[below, yhi], up_w),
        remote(lo_w & lo_n, hi_w & lo_n, ext.at[rim:2 * rim, ylo], ext.at[above, ylo], dn_w),
        remote(lo_w & hi_n, hi_w & hi_n, ext.at[rim:2 * rim, yhi], ext.at[above, yhi], dn_w)]
    come(*thin)
    corners += [
        remote(lo_n & lo_w, lo_n & hi_w, extra.at[0, elow], extra.at[0, eabove], dn_w),
        remote(lo_n & hi_w, lo_n & lo_w, extra.at[0, ehigh], extra.at[0, ebelow], up_w),
        remote(hi_n & lo_w, hi_n & hi_w, extra.at[1, elow], extra.at[1, eabove], dn_w),
        remote(hi_n & hi_w, hi_n & lo_w, extra.at[1, ehigh], extra.at[1, ebelow], up_w)]
    go(*corners)
    for k in strips[0] + strips[1]:
        @pl.when(everything[k][0])
        def _(k=k):
            everything[k][2].wait_send()
    go(*strips[2])

    flat = nodes[...].reshape(-1, 128)
    high = flat.astype(BF16).astype(F32)
    both = jnp.concatenate([high, flat - high], axis=1).astype(BF16)
    level = jnp.dot(both, up[...], preferred_element_type=F32)
    for i in range(nel + 1):
        head, tail = split(level[i * QPAD:(i + 1) * QPAD])
        field[i] = jnp.dot(inter[...], jnp.concatenate([head, tail], axis=0), preferred_element_type=F32)
    strain_pull(ns, nodes, pull)
    carry[...] = jnp.zeros_like(carry)
    for part in full[:2]:
        widen(part.start + rim, rim, ylo, 4)
        widen(part.start + rim, rim, yhi, 4)
    spots = (7, 8 + cols + 2 * side)

    def rims(span, source, first, count):
        rimcol[:, span] = extra[:, span].astype(F32)
        for r in range(count % 4):
            for i, spot in enumerate(spots):
                win[first + r, spot:spot + 1] = rimcol[i, source + r:source + r + 1]

        @pl.loop(0, count // 4)
        def _(b):
            for a in range(4):
                r = count % 4 + 4 * b + a
                for i, spot in enumerate(spots):
                    win[first + r, spot:spot + 1] = rimcol[i, pl.ds(source + r, 1), :]

    rims(emid, SIDE, rim, rows)
    come(*strips[2])
    widen(2 * rim, rows - 2 * rim, ylo, 4)
    widen(2 * rim, rows - 2 * rim, yhi, 4)
    come(*bands, *second_hop)
    widen(0, rim, mid, 2)
    widen(rim + rows, rim, mid, 2)
    come(*corners)
    for first in (0, rim + rows):
        widen(first, rim, ylo, 4)
        widen(first, rim, yhi, 4)
    rims(slice(0, SIDE), SIDE - rim, 0, rim)
    rims(slice(SIDE + rows, 2 * SIDE + rows), SIDE + rows, rim + rows, rim)
    slab.wait()
    steps = rows // 8
    start = map_ref[0] + side
    col0 = map_ref[1] + 8 + side
    lane = lax.broadcasted_iota(jnp.int32, (8, layers), 1)
    keep_low, keep_high = lane > 0, lane < layers - 1

    @pl.loop(0, steps)
    def _(p):
        base = pl.multiple_of(8 * p, 8)
        row0 = start + base

        @pl.loop(0, cols // 16)
        def _(j):
            at = pl.multiple_of(j * 16, 16)
            refs = [res[base + k, pl.ds(at, 16), :].astype(F32) for k in range(8)]
            out_rows, parts = voxels(
                at,
                lambda k, shift, half: win[row0 + k, pl.ds(col0 + at + (8 * half + shift), 8), :],
                lambda k, half: refs[k][8 * half:8 * half + 8],
                lambda c, half: field[p, pl.ds(at + 8 * half, 8), c * layers:(c + 1) * layers],
                lambda c, half: field[p + 1, pl.ds(at + 8 * half, 8), c * layers:(c + 1) * layers],
                keep_low, keep_high)
            for k in range(8):
                res[base + k, pl.ds(at, 16), :] = out_rows[k]
            for c in range(comps):
                lanes = slice(c * layers, (c + 1) * layers)
                for i in range(2):
                    low, high = parts[c][2 * i:2 * i + 2]
                    head, tail = split(carry[i, pl.ds(at, 16), lanes] + low)
                    sums[p, i, pl.ds(at, 16), lanes] = head
                    sums[p, i, pl.ds(cols + at, 16), lanes] = tail
                    carry[i, pl.ds(at, 16), lanes] = high

    for i in range(2):
        head, tail = split(carry[i])
        sums[steps, i, 0:cols] = head
        sums[steps, i, cols:2 * cols] = tail
    for k, (acc, mat, table) in enumerate(((gacc, proj, down), (dacc, proj2, down2))):
        for i in range(steps + 1):
            acc[i] = jnp.dot(mat[...], sums[i, k], preferred_element_type=F32)
        head, tail = split(acc[...].reshape(-1, comps * layers))
        got = (jnp.dot(head, table[...], preferred_element_type=F32)
               + jnp.dot(tail, table[...], preferred_element_type=F32)).reshape(pull.shape)
        terms[k] = got + pull[...] if k == 0 else got

    for k in range(2):
        for p in range(nel):
            colf[k, p:p + 1] = terms[k, p, nel:nel + 1]
    to_w = remote(hi_w, lo_w, terms.at[:, nel], from_w, up_w)
    to_n = remote(hi_n, lo_n, colf.at[:, 0:nel], from_n, up_n)
    to_c = remote(lo_w & hi_n, lo_w & lo_n, from_w.at[:, nel:QPAD], from_c, up_n)
    go(to_w, to_n)
    come(to_w)
    go(to_c)
    come(to_n, to_c)
    first_row = lax.broadcasted_iota(jnp.int32, (nel, 128), 0) == 0
    for p in range(nel):
        both = []
        for k in range(2):
            value = terms[k, p, 0:nel]
            beside = from_n[k, p:p + 1]
            if p == 0:
                value = value + from_w[k, 0:nel]
                beside = beside + from_c[k, 0:1]
            both.append(value + jnp.where(first_row, jnp.broadcast_to(beside, (nel, 128)), 0.0))
        step = both[0] / (both[1] + STIFFNESS)
        for c in range(comps):
            here = step if c == 0 else pltpu.roll(step, 128 - ns * c, 1)
            change[c, p] = here[:, 0:ns]
    sent = strips[0] + strips[1]
    for k, (goes, _c, copy) in enumerate(everything):
        if k not in sent:
            @pl.when(goes)
            def _(copy=copy):
                copy.wait_send()


def emit_kernel(parts, kept, change, disp, residual, updated, sem):
    rows = kept.shape[0] // parts
    copies = [pltpu.make_async_copy(kept.at[k * rows:(k + 1) * rows], residual.at[k * rows:(k + 1) * rows], sem.at[k])
              for k in range(parts)]
    for copy in copies:
        copy.start()
    updated[...] = disp[...] - change[...]
    for copy in copies:
        copy.wait()


def emit(kept, change, nodal):
    anywhere = pl.BlockSpec(memory_space=pl.ANY)
    near = pl.BlockSpec(memory_space=pltpu.VMEM)
    parts = 8
    return pl.pallas_call(
        functools.partial(emit_kernel, parts),
        out_shape=[jax.ShapeDtypeStruct(kept.shape, BF16), jax.ShapeDtypeStruct(nodal.shape, F32)],
        in_specs=[anywhere, near, near],
        out_specs=[anywhere, near],
        scratch_shapes=[pltpu.SemaphoreType.DMA((parts,))],
        compiler_params=pltpu.CompilerParams(vmem_limit_bytes=8 << 20),
        name="emit",
    )(kept, change, nodal)


def per_device(nw, nn, reference_image, deformed_image, displacement, tile_map):
    comps, ns, nel, _ = displacement.shape
    rows, cols, layers = reference_image.shape
    nodal = displacement.transpose(0, 2, 3, 1)
    tabs = tables(rows, cols, layers, comps)
    rim = rows // 4 + 1
    npx, lanes = nel + 1, comps * layers
    total, across = rows + 2 * rim, cols + 2 * (rim - 1)
    anywhere = pl.BlockSpec(memory_space=pl.ANY)
    near = pl.BlockSpec(memory_space=pltpu.VMEM)
    kept, change = pl.pallas_call(
        functools.partial(step_kernel, nw, nn, rim, ns),
        out_shape=[jax.ShapeDtypeStruct(reference_image.shape, BF16),
                   jax.ShapeDtypeStruct(nodal.shape, F32)],
        in_specs=[pl.BlockSpec(memory_space=pltpu.SMEM), anywhere, anywhere] + [near] * 7,
        out_specs=[near, near],
        scratch_shapes=[
            pltpu.VMEM((total, across, layers), BF16),
            pltpu.VMEM((rim, cols - cols // 4, layers), BF16),
            pltpu.VMEM((total, across + 16, layers), F32),
            pltpu.VMEM((npx, cols, lanes), F32),
            pltpu.VMEM((npx, 2, 2 * cols, lanes), BF16),
            pltpu.VMEM((2, cols, lanes), F32),
            pltpu.VMEM((npx, QPAD, lanes), F32),
            pltpu.VMEM((npx, QPAD, lanes), F32),
            pltpu.VMEM((2, npx, QPAD, 128), F32),
            pltpu.VMEM((2, rows + 2 * SIDE, layers), BF16),
            pltpu.VMEM((2, rows + 2 * SIDE, layers), F32),
            pltpu.VMEM((npx, QPAD, 128), F32),
            pltpu.VMEM((npx, QPAD, 128), F32),
            pltpu.VMEM((comps, nel, nel, 128), F32),
            pltpu.VMEM((nel, 128), F32),
            pltpu.VMEM((nel, 128), F32),
            pltpu.VMEM((8, 128), F32),
            pltpu.VMEM((2, rows, layers), F32),
            pltpu.VMEM((2, rows, layers), BF16),
            pltpu.VMEM((2, QPAD, 128), F32),
            pltpu.VMEM((2, nel, 128), F32),
            pltpu.VMEM((2, QPAD - nel, 128), F32),
            pltpu.SemaphoreType.DMA((34,)),
            pltpu.SemaphoreType.DMA((34,)),
            pltpu.SemaphoreType.DMA((2,)),
        ],
        compiler_params=pltpu.CompilerParams(
            collective_id=0, has_side_effects=True, vmem_limit_bytes=48 << 20),
        name="step",
    )(tile_map.reshape(2), deformed_image, reference_image, nodal, *tabs)
    residual, updated = emit(kept, change, nodal)
    return (updated.transpose(0, 3, 1, 2), residual)


def solution(mesh):
    placed = (
        P("wide", "narrow", None),
        P("wide", "narrow", None),
        P(None, None, "wide", "narrow"),
        P("wide", "narrow", None),
    )
    return jax.shard_map(
        functools.partial(per_device, mesh.shape["wide"], mesh.shape["narrow"]),
        mesh=mesh,
        in_specs=placed,
        out_specs=(P(None, None, "wide", "narrow"), P("wide", "narrow", None)),
        check_vma=False,
    )
```

```python
import functools

import jax
import jax.numpy as jnp
from jax import lax
from jax.experimental import pallas as pl
from jax.experimental.pallas import tpu as pltpu
from jax.sharding import PartitionSpec as P

MU_SHEAR = 1.0
LAMBDA_BULK = 2.0
REG_WEIGHT = 256.0
STIFFNESS = 16.0
MESH = pl.DeviceIdType.MESH
F32 = jnp.float32
BF16 = jnp.bfloat16
SIDE = 48
QPAD = 24


def as_int(flag):
    return flag.astype(jnp.int32)


def hat(place, node):
    at = (place.astype(F32) + 0.5) * 0.125
    return jnp.maximum(1.0 - jnp.abs(at - node.astype(F32)), 0.0)


def build_tables(ns, inter, proj, up, down, down2, square, gather, dz):
    def grid(ref):
        return (lax.broadcasted_iota(jnp.int32, ref.shape, 0), lax.broadcasted_iota(jnp.int32, ref.shape, 1))

    cols = inter.shape[0]
    r, c = grid(inter)
    inter[...] = (0.5 * hat(r, jnp.where(c < QPAD, c, c - QPAD))).astype(BF16)
    r, c = grid(proj)
    proj[...] = hat(jnp.where(c < cols, c, c - cols), r).astype(BF16)
    r, c = grid(up)
    up[...] = hat(c % 128, r % 128 - ns * (c // 128)).astype(BF16)
    r, c = grid(down)
    layer = hat(r % 128, c - ns * (r // 128))
    down[...] = (-0.5 * layer).astype(BF16)
    down2[...] = (0.25 * layer * layer).astype(BF16)
    r, c = grid(square)
    along = (c // 16).astype(F32) * 0.125 + 0.0625
    along = jnp.where(r % 16 < 8, 1.0 - along, along)
    across = hat(c % 16, r % 8)
    whole = (along * along) * (across * across)
    head = whole.astype(BF16).astype(F32)
    square[...] = jnp.where(r < 16, head, whole - head).astype(BF16)
    r, c = grid(dz)
    dz[...] = (jnp.where(r == c + 1, 1.0, 0.0) - jnp.where(r == c - 1, 1.0, 0.0)).astype(BF16)
    r, c = grid(gather)
    low = r < QPAD
    node = jnp.where(low, r, r - QPAD)
    k = c % 128
    same = (node == 2 * (k // 16) + k % 8) & (k % 8 < 3) & (low == (k % 16 < 8))
    gather[...] = jnp.where(same, 1.0, 0.0).astype(BF16)


def split(value):
    high = value.astype(BF16)
    return high, (value - high.astype(F32)).astype(BF16)


def strain_pull(ns, nodes, pull):
    npx = nodes.shape[0]
    nel = npx - 1
    lane = lax.broadcasted_iota(jnp.int32, (nel, 128), 1)
    move = lambda a, by: pltpu.roll(a, by % 128, 1)
    pull[...] = jnp.zeros_like(pull)

    @pl.loop(0, nel)
    def _(p):
        a00, a01 = nodes[p, 0:nel], nodes[p, 1:nel + 1]
        a10, a11 = nodes[p + 1, 0:nel], nodes[p + 1, 1:nel + 1]
        dx = (a10 - a00) + (a11 - a01)
        dy = (a01 - a00) + (a11 - a10)
        every = (a00 + a01) + (a10 + a11)
        slopes = (dx + move(dx, -1), dy + move(dy, -1), move(every, -1) - every)
        f = [[0.03125 * (move(h, -ns * i) if i else h) + (1.0 if i == j else 0.0)
              for j, h in enumerate(slopes)] for i in range(3)]
        cof = [[f[(i + 1) % 3][(j + 1) % 3] * f[(i + 2) % 3][(j + 2) % 3]
                - f[(i + 1) % 3][(j + 2) % 3] * f[(i + 2) % 3][(j + 1) % 3]
                for j in range(3)] for i in range(3)]
        ratio = f[0][0] * cof[0][0] + f[0][1] * cof[0][1] + f[0][2] * cof[0][2]
        factor = (LAMBDA_BULK * jnp.log(ratio) - MU_SHEAR) / ratio
        back = []
        for j in range(3):
            parts = [jnp.where(lane < ns - 1, MU_SHEAR * f[i][j] + factor * cof[i][j], 0.0) for i in range(3)]
            back.append((parts[0] + move(parts[1], ns) + move(parts[2], 2 * ns)) * (0.03125 * REG_WEIGHT))
        gx = back[0] + move(back[0], 1)
        gy = back[1] + move(back[1], 1)
        gz = move(back[2], 1) - back[2]
        for dp, dq in ((0, 0), (0, 1), (1, 0), (1, 1)):
            add = (gx if dp else -gx) + (gy if dq else -gy) + gz
            pull[p + dp, dq:dq + nel] = pull[p + dp, dq:dq + nel] + add


def voxels(window, slope_z, ref_rows, left, right):
    back = []
    rows, squares = [None] * 8, [[None] * 3 for _ in range(8)]
    join = lambda a, b: jnp.concatenate([a, b], axis=0)
    for half in range(2):
        run, tot = [None] * 3, [None] * 3
        inc = [(right(c, half) - left(c, half)) * 0.125 for c in range(3)]
        mv = [left(c, half) + 0.5 * inc[c] for c in range(3)]
        prev, cur = window(0, 0, half), window(1, 0, half)
        for k in range(8):
            nxt = window(k + 2, 0, half)
            g = [nxt - prev,
                 window(k + 1, 1, half) - window(k + 1, -1, half),
                 slope_z(k, half)]
            r = ref_rows(k, half) - cur
            for c in range(3):
                r = r - g[c] * mv[c]
                if k < 7:
                    mv[c] = mv[c] + inc[c]
            rows[k] = r if half == 0 else join(rows[k], r).astype(BF16)
            for c in range(3):
                f = g[c] * r
                q = g[c] * g[c]
                run[c] = f if k == 0 else run[c] + f
                tot[c] = run[c] if k == 0 else tot[c] + run[c]
                squares[k][c] = q if half == 0 else join(squares[k][c], q).astype(BF16)
            prev, cur = cur, nxt
        part = []
        for c in range(3):
            low = (tot[c] - 0.5 * run[c]) * 0.125
            part.append((low, run[c] - low))
        back.append(part)
    return rows, squares, [[join(back[0][c][i], back[1][c][i]) for i in range(2)] for c in range(3)]


def step_kernel(nw, nn, rim, ns, map_ref, own, ref_hbm, disp,
                res, change,
                inter, proj, up, down, down2, square, gather, dz,
                ext, passed, win, field, sums, carry, qbuf, zbuf, dpart, gacc, dacc, terms,
                extra, rimcol, nodes, pull, cube, column, side_in, corner_in, colf, colb,
                from_w, from_n, from_c, send, recv, lsem):
    rows, cols, layers = own.shape
    comps, nel = disp.shape[0], disp.shape[1]
    side = rim - 1
    w = lax.axis_index("wide")
    n = lax.axis_index("narrow")
    lo_w, hi_w, lo_n, hi_n = w > 0, w < nw - 1, n > 0, n < nn - 1
    up_w, dn_w = (w + 1, n), (w - 1, n)
    up_n, dn_n = (w, n + 1), (w, n - 1)
    mid = slice(side, side + cols)
    ylo = slice(0, side)
    yhi = slice(side + cols, 2 * side + cols)
    total = rows + 2 * rim
    emid = slice(SIDE, SIDE + rows)
    detour = nw == 8
    is0, is3, is4, is7 = (w == 0), (w == 3), (w == 4), (w == 7)

    local = pltpu.make_async_copy(own, ext.at[rim:rim + rows, mid], lsem.at[0])
    local.start()
    slab = pltpu.make_async_copy(ref_hbm, res, lsem.at[1])
    slab.start()
    extra[...] = jnp.zeros_like(extra)
    side_in[...] = jnp.zeros_like(side_in)
    corner_in[...] = jnp.zeros_like(corner_in)
    for ref in (from_w, from_n, from_c):
        ref[...] = jnp.zeros_like(ref)
    nodes[nel] = jnp.zeros(nodes.shape[1:], F32)
    cube[...] = jnp.zeros_like(cube)
    cube[:, :, :, 0:ns] = disp[...]
    for i in range(nel):
        value = cube[0, i]
        for c in range(1, comps):
            value = value + pltpu.roll(cube[c, i], ns * c, 1)
        nodes[i, 0:nel] = value
        column[i:i + 1] = value[0:1]

    barrier = pltpu.get_barrier_semaphore()
    greet = [(lo_w, dn_w), (hi_w, up_w), (lo_n, dn_n), (hi_n, up_n)]
    if detour:
        greet += [(is7, (3, n)), (is4, (7, n)), (is0, (4, n)), (is3, (0, n))]
    count = as_int(lo_w) + as_int(hi_w) + as_int(lo_n) + as_int(hi_n)
    if detour:
        count = count + as_int(is0 | is3 | is4 | is7)
    for there, device in greet:
        @pl.when(there)
        def _(device=device):
            pl.semaphore_signal(barrier, inc=1, device_id=device, device_id_type=MESH)
    pl.semaphore_wait(barrier, count)

    everything = []

    def remote(goes, comes, src, dst, device):
        k = len(everything)
        copy = pltpu.make_async_remote_copy(
            src_ref=src, dst_ref=dst, send_sem=send.at[k], recv_sem=recv.at[k],
            device_id=device, device_id_type=MESH)
        everything.append((goes, comes, copy))
        return k

    def go(*ks):
        for k in ks:
            @pl.when(everything[k][0])
            def _(k=k):
                everything[k][2].start()

    def come(*ks):
        for k in ks:
            @pl.when(everything[k][1])
            def _(k=k):
                everything[k][2].wait_recv()

    below, above = slice(0, rim), slice(rim + rows, total)
    edge_x = remote(lo_w, hi_w, nodes.at[0, 0:nel], nodes.at[nel, 0:nel], dn_w)
    edge_y = remote(lo_n, hi_n, column, side_in, dn_n)
    strips = []
    full = (slice(0, rim), slice(rows - rim, rows), slice(rim, rows - rim))
    for part in full:
        there = slice(part.start + rim, part.stop + rim)
        strips.append((
            remote(hi_n, lo_n, own.at[part, cols - side:cols], ext.at[there, ylo], up_n),
            remote(lo_n, hi_n, own.at[part, 0:side], ext.at[there, yhi], dn_n)))
    cut = cols // 4 if detour else cols
    near, far = slice(0, cut), slice(cut, cols)
    enear, efar = slice(side, side + cut), slice(side + cut, side + cols)
    high_own, low_own = slice(rows - rim, rows), slice(0, rim)
    bands = [
        remote(hi_w, lo_w, own.at[high_own, near], ext.at[below, enear], up_w),
        remote(lo_w, hi_w, own.at[low_own, near], ext.at[above, enear], dn_w)]
    first_hop, second_hop = [], []
    if detour:
        bands += [
            remote(hi_w & (w != 3), lo_w & (w != 4), own.at[high_own, far], ext.at[below, efar], up_w),
            remote(lo_w & (w != 4), hi_w & (w != 3), own.at[low_own, far], ext.at[above, efar], dn_w)]
        first_hop = [
            remote(is3, is7, own.at[high_own, far], passed, (7, n)),
            remote(is4, is0, own.at[low_own, far], passed, (0, n))]
        second_hop = [
            remote(is7, is4, passed, ext.at[below, efar], (4, n)),
            remote(is0, is3, passed, ext.at[above, efar], (3, n))]
    go(edge_x, edge_y, *strips[0], *strips[1], *first_hop, *bands)

    def widen(first, count, columns, together):
        to = slice(columns.start + 8, columns.stop + 8)

        @pl.loop(0, count // together)
        def _(b):
            for a in range(together):
                win[first + together * b + a, to] = ext[first + together * b + a, columns].astype(F32)
        for r in range(first + count // together * together, first + count):
            win[r, to] = ext[r, columns].astype(F32)

    local.wait()
    build_tables(ns, inter, proj, up, down, down2, square, gather, dz)
    picks = (side + cols - rim, side + rim - 1)

    @pl.loop(0, rows // 8)
    def _(b):
        for a in range(8):
            for i, col in enumerate(picks):
                tile = ext[rim + 8 * b + a, col // 16 * 16:col // 16 * 16 + 16, :].astype(F32)
                colf[i, pl.ds(8 * b + a, 1), :] = tile[col % 16:col % 16 + 1]
    colb[...] = colf[...].astype(BF16)
    elow, ehigh = slice(SIDE, 2 * SIDE), slice(rows, SIDE + rows)
    ebelow, eabove = slice(0, SIDE), slice(SIDE + rows, 2 * SIDE + rows)
    thin = [remote(hi_n, lo_n, colb.at[0], extra.at[0, emid], up_n),
            remote(lo_n, hi_n, colb.at[1], extra.at[1, emid], dn_n)]
    go(*thin)

    @pl.when(jnp.logical_not(lo_n))
    def _():
        ext[:, ylo] = jnp.zeros((total, side, layers), BF16)

    @pl.when(jnp.logical_not(hi_n))
    def _():
        ext[:, yhi] = jnp.zeros((total, side, layers), BF16)

    @pl.when(jnp.logical_not(lo_w))
    def _():
        ext[below] = jnp.zeros((rim, cols + 2 * side, layers), BF16)

    @pl.when(jnp.logical_not(hi_w))
    def _():
        ext[above] = jnp.zeros((rim, cols + 2 * side, layers), BF16)

    widen(rim, rows, mid, 2)
    come(edge_x)
    edge_c = remote(hi_w & lo_n, hi_w & hi_n, nodes.at[nel, 0:8], corner_in, dn_n)
    go(edge_c)
    come(edge_y)
    top = lax.broadcasted_iota(jnp.int32, (QPAD - nel, 128), 0) == 0
    for i in range(nel):
        nodes[i, nel:QPAD] = jnp.where(top, jnp.broadcast_to(side_in[i:i + 1], (QPAD - nel, 128)), 0.0)
    come(edge_c)
    nodes[nel, nel:QPAD] = jnp.where(top, jnp.broadcast_to(corner_in[0:1], (QPAD - nel, 128)), 0.0)
    come(*first_hop)
    go(*second_hop)
    corners = []
    come(*strips[0], *strips[1])
    corners += [
        remote(hi_w & lo_n, lo_w & lo_n, ext.at[rows:rows + rim, ylo], ext.at[below, ylo], up_w),
        remote(hi_w & hi_n, lo_w & hi_n, ext.at[rows:rows + rim, yhi], ext.at[below, yhi], up_w),
        remote(lo_w & lo_n, hi_w & lo_n, ext.at[rim:2 * rim, ylo], ext.at[above, ylo], dn_w),
        remote(lo_w & hi_n, hi_w & hi_n, ext.at[rim:2 * rim, yhi], ext.at[above, yhi], dn_w)]
    come(*thin)
    corners += [
        remote(lo_n & lo_w, lo_n & hi_w, extra.at[0, elow], extra.at[0, eabove], dn_w),
        remote(lo_n & hi_w, lo_n & lo_w, extra.at[0, ehigh], extra.at[0, ebelow], up_w),
        remote(hi_n & lo_w, hi_n & hi_w, extra.at[1, elow], extra.at[1, eabove], dn_w),
        remote(hi_n & hi_w, hi_n & lo_w, extra.at[1, ehigh], extra.at[1, ebelow], up_w)]
    go(*corners)
    for k in strips[0] + strips[1]:
        @pl.when(everything[k][0])
        def _(k=k):
            everything[k][2].wait_send()
    go(*strips[2])

    flat = nodes[...].reshape(-1, 128)
    high = flat.astype(BF16).astype(F32)
    both = jnp.concatenate([high, flat - high], axis=1).astype(BF16)
    level = jnp.dot(both, up[...], preferred_element_type=F32)
    for i in range(nel + 1):
        head, tail = split(level[i * QPAD:(i + 1) * QPAD])
        field[i] = jnp.dot(inter[...], jnp.concatenate([head, tail], axis=0), preferred_element_type=F32)
    strain_pull(ns, nodes, pull)
    carry[...] = jnp.zeros_like(carry)
    qbuf[...] = jnp.zeros_like(qbuf)
    dacc[...] = jnp.zeros_like(dacc)
    for part in full[:2]:
        widen(part.start + rim, rim, ylo, 4)
        widen(part.start + rim, rim, yhi, 4)
    spots = (7, 8 + cols + 2 * side)

    def rims(span, source, first, count):
        rimcol[:, span] = extra[:, span].astype(F32)
        for r in range(count % 4):
            for i, spot in enumerate(spots):
                win[first + r, spot:spot + 1] = rimcol[i, source + r:source + r + 1]

        @pl.loop(0, count // 4)
        def _(b):
            for a in range(4):
                r = count % 4 + 4 * b + a
                for i, spot in enumerate(spots):
                    win[first + r, spot:spot + 1] = rimcol[i, pl.ds(source + r, 1), :]

    rims(emid, SIDE, rim, rows)
    come(*strips[2])
    widen(2 * rim, rows - 2 * rim, ylo, 4)
    widen(2 * rim, rows - 2 * rim, yhi, 4)
    come(*bands, *second_hop)
    widen(0, rim, mid, 2)
    widen(rim + rows, rim, mid, 2)
    come(*corners)
    for first in (0, rim + rows):
        widen(first, rim, ylo, 4)
        widen(first, rim, yhi, 4)
    rims(slice(0, SIDE), SIDE - rim, 0, rim)
    rims(slice(SIDE + rows, 2 * SIDE + rows), SIDE + rows, rim + rows, rim)
    slab.wait()
    steps = rows // 8
    start = map_ref[0] + side
    col0 = map_ref[1] + 8 + side
    chunks, pair = cols // 16, 2

    def fold(u, t):
        got = jnp.dot(square[...], qbuf[u], preferred_element_type=F32)
        dpart[t] = got[0:16] + got[16:32]

    def slopes(t):
        row0 = start + 8 * lax.div(t, chunks) + 1
        at = col0 + 16 * lax.rem(t, chunks)
        here = jnp.concatenate([win[row0 + k, pl.ds(at, 16), :].astype(BF16) for k in range(8)], axis=0)
        return jnp.dot(here, dz[...], preferred_element_type=F32)

    for u in range(pair):
        zbuf[u] = slopes(jnp.int32(u))

    @pl.loop(0, steps * chunks // pair)
    def _(b):
        first = pair * b
        coming = [slopes(jnp.minimum(first + pair + u, steps * chunks - 1)) for u in range(pair)]
        for u in range(pair):
            fold(u, jnp.maximum(first - pair + u, 0))
        for u in range(pair):
            t = first + u
            p = lax.div(t, chunks)
            at = pl.multiple_of(16 * lax.rem(t, chunks), 16)
            base = 8 * p
            row0 = start + base
            refs = [res[base + k, pl.ds(at, 16), :].astype(F32) for k in range(8)]
            out_rows, squares, parts = voxels(
                lambda k, shift, half: win[row0 + k, pl.ds(col0 + at + (8 * half + shift), 8), :],
                lambda k, half: zbuf[u, 16 * k + 8 * half:16 * k + 8 * half + 8, :],
                lambda k, half: refs[k][8 * half:8 * half + 8],
                lambda c, half: field[p, pl.ds(at + 8 * half, 8), c * layers:(c + 1) * layers],
                lambda c, half: field[p + 1, pl.ds(at + 8 * half, 8), c * layers:(c + 1) * layers])
            for k in range(8):
                res[base + k, pl.ds(at, 16), :] = out_rows[k]
            for c in range(comps):
                lanes = slice(c * layers, (c + 1) * layers)
                for k in range(8):
                    qbuf[u, 16 * k:16 * k + 16, lanes] = squares[k][c]
                low, high = parts[c]
                head, tail = split(carry[pl.ds(at, 16), lanes] + low)
                sums[p, pl.ds(at, 16), lanes] = head
                sums[p, pl.ds(cols + at, 16), lanes] = tail
                carry[pl.ds(at, 16), lanes] = high
        for u in range(pair):
            zbuf[u] = coming[u]

    for u in range(pair):
        fold(u, steps * chunks - pair + u)
    head, tail = split(carry[...])
    sums[steps, 0:cols] = head
    sums[steps, cols:2 * cols] = tail
    for i in range(steps + 1):
        gacc[i] = jnp.dot(proj[...], sums[i], preferred_element_type=F32)
    for i in range(steps):
        head, tail = split(dpart[i * chunks:(i + 1) * chunks].reshape(cols, comps * layers))
        got = jnp.dot(gather[...], jnp.concatenate([head, tail], axis=0), preferred_element_type=F32)
        dacc[i] = dacc[i] + got[0:QPAD]
        dacc[i + 1] = got[QPAD:2 * QPAD]
    for k, (acc, table) in enumerate(((gacc, down), (dacc, down2))):
        head, tail = split(acc[...].reshape(-1, comps * layers))
        got = (jnp.dot(head, table[...], preferred_element_type=F32)
               + jnp.dot(tail, table[...], preferred_element_type=F32)).reshape(pull.shape)
        terms[k] = got + pull[...] if k == 0 else got

    for k in range(2):
        for p in range(nel):
            colf[k, p:p + 1] = terms[k, p, nel:nel + 1]
    to_w = remote(hi_w, lo_w, terms.at[:, nel], from_w, up_w)
    to_n = remote(hi_n, lo_n, colf.at[:, 0:nel], from_n, up_n)
    to_c = remote(lo_w & hi_n, lo_w & lo_n, from_w.at[:, nel:QPAD], from_c, up_n)
    go(to_w, to_n)
    come(to_w)
    go(to_c)
    come(to_n, to_c)
    first_row = lax.broadcasted_iota(jnp.int32, (nel, 128), 0) == 0
    for p in range(nel):
        both = []
        for k in range(2):
            value = terms[k, p, 0:nel]
            beside = from_n[k, p:p + 1]
            if p == 0:
                value = value + from_w[k, 0:nel]
                beside = beside + from_c[k, 0:1]
            both.append(value + jnp.where(first_row, jnp.broadcast_to(beside, (nel, 128)), 0.0))
        step = both[0] / (both[1] + STIFFNESS)
        for c in range(comps):
            here = step if c == 0 else pltpu.roll(step, 128 - ns * c, 1)
            change[c, p] = here[:, 0:ns]
    sent = strips[0] + strips[1]
    for k, (goes, _c, copy) in enumerate(everything):
        if k not in sent:
            @pl.when(goes)
            def _(copy=copy):
                copy.wait_send()


def emit_kernel(parts, kept, change, disp, residual, updated, fresh, sem):
    rows = kept.shape[0] // parts
    copies = [pltpu.make_async_copy(kept.at[k * rows:(k + 1) * rows], residual.at[k * rows:(k + 1) * rows], sem.at[k])
              for k in range(parts)]
    for copy in copies:
        copy.start()
    fresh[...] = disp[...] - change[...]
    last = pltpu.make_async_copy(fresh, updated, sem.at[parts])
    last.start()
    for copy in copies + [last]:
        copy.wait()


def emit(kept, change, nodal):
    anywhere = pl.BlockSpec(memory_space=pl.ANY)
    near = pl.BlockSpec(memory_space=pltpu.VMEM)
    parts = 8
    return pl.pallas_call(
        functools.partial(emit_kernel, parts),
        out_shape=[jax.ShapeDtypeStruct(kept.shape, BF16), jax.ShapeDtypeStruct(nodal.shape, F32)],
        in_specs=[anywhere, near, near],
        out_specs=[anywhere, anywhere],
        scratch_shapes=[pltpu.VMEM(nodal.shape, F32), pltpu.SemaphoreType.DMA((parts + 1,))],
        compiler_params=pltpu.CompilerParams(vmem_limit_bytes=8 << 20),
        name="emit",
    )(kept, change, nodal)


def per_device(nw, nn, reference_image, deformed_image, displacement, tile_map):
    comps, ns, nel, _ = displacement.shape
    rows, cols, layers = reference_image.shape
    nodal = displacement.transpose(0, 2, 3, 1)
    rim = rows // 4 + 1
    npx, lanes = nel + 1, comps * layers
    total, across = rows + 2 * rim, cols + 2 * (rim - 1)
    anywhere = pl.BlockSpec(memory_space=pl.ANY)
    near = pl.BlockSpec(memory_space=pltpu.VMEM)
    kept, change = pl.pallas_call(
        functools.partial(step_kernel, nw, nn, rim, ns),
        out_shape=[jax.ShapeDtypeStruct(reference_image.shape, BF16),
                   jax.ShapeDtypeStruct(nodal.shape, F32)],
        in_specs=[pl.BlockSpec(memory_space=pltpu.SMEM), anywhere, anywhere, near],
        out_specs=[near, near],
        scratch_shapes=[
            pltpu.VMEM((cols, 2 * QPAD), BF16),
            pltpu.VMEM((QPAD, 2 * cols), BF16),
            pltpu.VMEM((2 * 128, lanes), BF16),
            pltpu.VMEM((lanes, 128), BF16),
            pltpu.VMEM((lanes, 128), BF16),
            pltpu.VMEM((32, 8 * 16), BF16),
            pltpu.VMEM((2 * QPAD, 2 * cols), BF16),
            pltpu.VMEM((layers, layers), BF16),
            pltpu.VMEM((total, across, layers), BF16),
            pltpu.VMEM((rim, cols - cols // 4, layers), BF16),
            pltpu.VMEM((total, across + 16, layers), F32),
            pltpu.VMEM((npx, cols, lanes), F32),
            pltpu.VMEM((npx, 2 * cols, lanes), BF16),
            pltpu.VMEM((cols, lanes), F32),
            pltpu.VMEM((2, 8 * 16, lanes), BF16),
            pltpu.VMEM((2, 8 * 16, layers), F32),
            pltpu.VMEM((rows // 8 * (cols // 16), 16, lanes), F32),
            pltpu.VMEM((npx, QPAD, lanes), F32),
            pltpu.VMEM((npx, QPAD, lanes), F32),
            pltpu.VMEM((2, npx, QPAD, 128), F32),
            pltpu.VMEM((2, rows + 2 * SIDE, layers), BF16),
            pltpu.VMEM((2, rows + 2 * SIDE, layers), F32),
            pltpu.VMEM((npx, QPAD, 128), F32),
            pltpu.VMEM((npx, QPAD, 128), F32),
            pltpu.VMEM((comps, nel, nel, 128), F32),
            pltpu.VMEM((nel, 128), F32),
            pltpu.VMEM((nel, 128), F32),
            pltpu.VMEM((8, 128), F32),
            pltpu.VMEM((2, rows, layers), F32),
            pltpu.VMEM((2, rows, layers), BF16),
            pltpu.VMEM((2, QPAD, 128), F32),
            pltpu.VMEM((2, nel, 128), F32),
            pltpu.VMEM((2, QPAD - nel, 128), F32),
            pltpu.SemaphoreType.DMA((34,)),
            pltpu.SemaphoreType.DMA((34,)),
            pltpu.SemaphoreType.DMA((2,)),
        ],
        compiler_params=pltpu.CompilerParams(
            collective_id=0, has_side_effects=True, vmem_limit_bytes=48 << 20),
        name="step",
    )(tile_map.reshape(2), deformed_image, reference_image, nodal)
    residual, updated = emit(kept, change, nodal)
    return (updated.transpose(0, 3, 1, 2), residual)


def solution(mesh):
    placed = (
        P("wide", "narrow", None),
        P("wide", "narrow", None),
        P(None, None, "wide", "narrow"),
        P("wide", "narrow", None),
    )
    return jax.shard_map(
        functools.partial(per_device, mesh.shape["wide"], mesh.shape["narrow"]),
        mesh=mesh,
        in_specs=placed,
        out_specs=(P(None, None, "wide", "narrow"), P("wide", "narrow", None)),
        check_vma=False,
    )
```

```python
import functools

import jax
import jax.numpy as jnp
from jax import lax
from jax.experimental import pallas as pl
from jax.experimental.pallas import tpu as pltpu
from jax.sharding import PartitionSpec as P

MU_SHEAR = 1.0
LAMBDA_BULK = 2.0
REG_WEIGHT = 256.0
STIFFNESS = 16.0
MESH = pl.DeviceIdType.MESH
F32 = jnp.float32
BF16 = jnp.bfloat16
SIDE = 48
QPAD = 24


def as_int(flag):
    return flag.astype(jnp.int32)


def hat(place, node):
    at = (place.astype(F32) + 0.5) * 0.125
    return jnp.maximum(1.0 - jnp.abs(at - node.astype(F32)), 0.0)


def build_tables(ns, inter, proj, up, down, down2, square, gather, dz):
    def grid(ref):
        return (lax.broadcasted_iota(jnp.int32, ref.shape, 0), lax.broadcasted_iota(jnp.int32, ref.shape, 1))

    cols = inter.shape[0]
    r, c = grid(inter)
    inter[...] = (0.5 * hat(r, jnp.where(c < QPAD, c, c - QPAD))).astype(BF16)
    r, c = grid(proj)
    proj[...] = hat(jnp.where(c < cols, c, c - cols), r).astype(BF16)
    r, c = grid(up)
    up[...] = hat(c % 128, r % 128 - ns * (c // 128)).astype(BF16)
    r, c = grid(down)
    layer = hat(r % 128, c - ns * (r // 128))
    down[...] = (-0.5 * layer).astype(BF16)
    down2[...] = (0.25 * layer * layer).astype(BF16)
    r, c = grid(square)
    along = (c // 16).astype(F32) * 0.125 + 0.0625
    along = jnp.where(r % 16 < 8, 1.0 - along, along)
    across = hat(c % 16, r % 8)
    whole = (along * along) * (across * across)
    head = whole.astype(BF16).astype(F32)
    square[...] = jnp.where(r < 16, head, whole - head).astype(BF16)
    r, c = grid(dz)
    dz[...] = (jnp.where(r == c + 1, 1.0, 0.0) - jnp.where(r == c - 1, 1.0, 0.0)).astype(BF16)
    r, c = grid(gather)
    low = r < QPAD
    node = jnp.where(low, r, r - QPAD)
    k = c % 128
    same = (node == 2 * (k // 16) + k % 8) & (k % 8 < 3) & (low == (k % 16 < 8))
    gather[...] = jnp.where(same, 1.0, 0.0).astype(BF16)


def split(value):
    high = value.astype(BF16)
    return high, (value - high.astype(F32)).astype(BF16)


def strain_pull(ns, nodes, pull):
    npx = nodes.shape[0]
    nel = npx - 1
    lane = lax.broadcasted_iota(jnp.int32, (nel, 128), 1)
    move = lambda a, by: pltpu.roll(a, by % 128, 1)
    pull[...] = jnp.zeros_like(pull)

    @pl.loop(0, nel)
    def _(p):
        a00, a01 = nodes[p, 0:nel], nodes[p, 1:nel + 1]
        a10, a11 = nodes[p + 1, 0:nel], nodes[p + 1, 1:nel + 1]
        dx = (a10 - a00) + (a11 - a01)
        dy = (a01 - a00) + (a11 - a10)
        every = (a00 + a01) + (a10 + a11)
        slopes = (dx + move(dx, -1), dy + move(dy, -1), move(every, -1) - every)
        f = [[0.03125 * (move(h, -ns * i) if i else h) + (1.0 if i == j else 0.0)
              for j, h in enumerate(slopes)] for i in range(3)]
        cof = [[f[(i + 1) % 3][(j + 1) % 3] * f[(i + 2) % 3][(j + 2) % 3]
                - f[(i + 1) % 3][(j + 2) % 3] * f[(i + 2) % 3][(j + 1) % 3]
                for j in range(3)] for i in range(3)]
        ratio = f[0][0] * cof[0][0] + f[0][1] * cof[0][1] + f[0][2] * cof[0][2]
        factor = (LAMBDA_BULK * jnp.log(ratio) - MU_SHEAR) / ratio
        back = []
        for j in range(3):
            parts = [jnp.where(lane < ns - 1, MU_SHEAR * f[i][j] + factor * cof[i][j], 0.0) for i in range(3)]
            back.append((parts[0] + move(parts[1], ns) + move(parts[2], 2 * ns)) * (0.03125 * REG_WEIGHT))
        gx = back[0] + move(back[0], 1)
        gy = back[1] + move(back[1], 1)
        gz = move(back[2], 1) - back[2]
        for dp, dq in ((0, 0), (0, 1), (1, 0), (1, 1)):
            add = (gx if dp else -gx) + (gy if dq else -gy) + gz
            pull[p + dp, dq:dq + nel] = pull[p + dp, dq:dq + nel] + add


def voxels(window, slope_z, ref_rows, left, right):
    back = []
    rows, squares = [None] * 8, [[None] * 3 for _ in range(8)]
    join = lambda a, b: jnp.concatenate([a, b], axis=0)
    for half in range(2):
        run, tot = [None] * 3, [None] * 3
        inc = [(right(c, half) - left(c, half)) * 0.125 for c in range(3)]
        mv = [left(c, half) + 0.5 * inc[c] for c in range(3)]
        prev, cur = window(0, 0, half), window(1, 0, half)
        for k in range(8):
            nxt = window(k + 2, 0, half)
            g = [nxt - prev,
                 window(k + 1, 1, half) - window(k + 1, -1, half),
                 slope_z(k, half)]
            r = ref_rows(k, half) - cur
            for c in range(3):
                r = r - g[c] * mv[c]
                if k < 7:
                    mv[c] = mv[c] + inc[c]
            rows[k] = r if half == 0 else join(rows[k], r).astype(BF16)
            for c in range(3):
                f = g[c] * r
                q = g[c] * g[c]
                run[c] = f if k == 0 else run[c] + f
                tot[c] = run[c] if k == 0 else tot[c] + run[c]
                squares[k][c] = q if half == 0 else join(squares[k][c], q).astype(BF16)
            prev, cur = cur, nxt
        part = []
        for c in range(3):
            low = (tot[c] - 0.5 * run[c]) * 0.125
            part.append((low, run[c] - low))
        back.append(part)
    return rows, squares, [[join(back[0][c][i], back[1][c][i]) for i in range(2)] for c in range(3)]


def step_kernel(nw, nn, rim, ns, map_hbm, own, ref_hbm, disp_hbm,
                res, change,
                inter, proj, up, down, down2, square, gather, dz,
                ext, passed, win, field, gsum, qbuf, zbuf, dpart, gacc, dacc, terms,
                extra, rimcol, nodes, pull, cube, column, side_in, corner_in, colf, colb,
                from_w, from_n, from_c, disp, map_ref, send, recv, lsem):
    rows, cols, layers = own.shape
    comps, nel = disp.shape[0], disp.shape[1]
    side = rim - 1
    w = lax.axis_index("wide")
    n = lax.axis_index("narrow")
    lo_w, hi_w, lo_n, hi_n = w > 0, w < nw - 1, n > 0, n < nn - 1
    up_w, dn_w = (w + 1, n), (w - 1, n)
    up_n, dn_n = (w, n + 1), (w, n - 1)
    mid = slice(side, side + cols)
    ylo = slice(0, side)
    yhi = slice(side + cols, 2 * side + cols)
    total = rows + 2 * rim
    emid = slice(SIDE, SIDE + rows)
    detour = nw == 8
    is0, is3, is4, is7 = (w == 0), (w == 3), (w == 4), (w == 7)

    barrier = pltpu.get_barrier_semaphore()
    greet = [(lo_w, dn_w), (hi_w, up_w), (lo_n, dn_n), (hi_n, up_n)]
    if detour:
        greet += [(is7, (3, n)), (is4, (7, n)), (is0, (4, n)), (is3, (0, n))]
    count = as_int(lo_w) + as_int(hi_w) + as_int(lo_n) + as_int(hi_n)
    if detour:
        count = count + as_int(is0 | is3 | is4 | is7)
    for there, device in greet:
        @pl.when(there)
        def _(device=device):
            pl.semaphore_signal(barrier, inc=1, device_id=device, device_id_type=MESH)
    loads = [pltpu.make_async_copy(disp_hbm, disp, lsem.at[2]),
             pltpu.make_async_copy(own, ext.at[rim:rim + rows, mid], lsem.at[0]),
             pltpu.make_async_copy(ref_hbm, res, lsem.at[1]),
             pltpu.make_async_copy(map_hbm, map_ref, lsem.at[3])]
    for load in loads:
        load.start()
    nodal, local, slab, offsets = loads

    def absent(there, *spans):
        @pl.when(jnp.logical_not(there))
        def _():
            for ref, span in spans:
                ref[span] = jnp.zeros(ref.at[span].shape, ref.dtype)

    elow, ehigh = slice(SIDE, 2 * SIDE), slice(rows, SIDE + rows)
    ebelow, eabove = slice(0, SIDE), slice(SIDE + rows, 2 * SIDE + rows)
    every = slice(None)
    absent(hi_w, (nodes, (nel, slice(0, nel))))
    absent(hi_n, (side_in, every), (extra, 1))
    absent(hi_w & hi_n, (corner_in, every), (extra, (1, eabove)))
    absent(lo_w & hi_n, (extra, (1, ebelow)))
    absent(lo_w, (from_w, every))
    absent(lo_n, (from_n, every), (extra, 0))
    absent(lo_w & lo_n, (from_c, every), (extra, (0, ebelow)))
    absent(hi_w & lo_n, (extra, (0, eabove)))
    pl.semaphore_wait(barrier, count)

    everything = []

    def remote(goes, comes, src, dst, device):
        k = len(everything)
        copy = pltpu.make_async_remote_copy(
            src_ref=src, dst_ref=dst, send_sem=send.at[k], recv_sem=recv.at[k],
            device_id=device, device_id_type=MESH)
        everything.append((goes, comes, copy))
        return k

    def go(*ks):
        for k in ks:
            @pl.when(everything[k][0])
            def _(k=k):
                everything[k][2].start()

    def come(*ks):
        for k in ks:
            @pl.when(everything[k][1])
            def _(k=k):
                everything[k][2].wait_recv()

    below, above = slice(0, rim), slice(rim + rows, total)
    edge_x = remote(lo_w, hi_w, nodes.at[0, 0:nel], nodes.at[nel, 0:nel], dn_w)
    edge_y = remote(lo_n, hi_n, column, side_in, dn_n)
    strips = []
    full = (slice(0, rim), slice(rows - rim, rows), slice(rim, rows - rim))
    for part in full:
        there = slice(part.start + rim, part.stop + rim)
        strips.append((
            remote(hi_n, lo_n, own.at[part, cols - side:cols], ext.at[there, ylo], up_n),
            remote(lo_n, hi_n, own.at[part, 0:side], ext.at[there, yhi], dn_n)))
    cut = cols // 4 if detour else cols
    near, far = slice(0, cut), slice(cut, cols)
    enear, efar = slice(side, side + cut), slice(side + cut, side + cols)
    high_own, low_own = slice(rows - rim, rows), slice(0, rim)
    bands = [
        remote(hi_w, lo_w, own.at[high_own, near], ext.at[below, enear], up_w),
        remote(lo_w, hi_w, own.at[low_own, near], ext.at[above, enear], dn_w)]
    first_hop, second_hop = [], []
    if detour:
        bands += [
            remote(hi_w & (w != 3), lo_w & (w != 4), own.at[high_own, far], ext.at[below, efar], up_w),
            remote(lo_w & (w != 4), hi_w & (w != 3), own.at[low_own, far], ext.at[above, efar], dn_w)]
        first_hop = [
            remote(is3, is7, own.at[high_own, far], passed, (7, n)),
            remote(is4, is0, own.at[low_own, far], passed, (0, n))]
        second_hop = [
            remote(is7, is4, passed, ext.at[below, efar], (4, n)),
            remote(is0, is3, passed, ext.at[above, efar], (3, n))]
    go(*strips[0], *strips[1], *first_hop, *bands)
    cube[...] = jnp.zeros_like(cube)
    nodal.wait()
    cube[:, :, :, 0:ns] = disp[...]
    for i in range(nel):
        value = cube[0, i]
        for c in range(1, comps):
            value = value + pltpu.roll(cube[c, i], ns * c, 1)
        nodes[i, 0:nel] = value
        column[i:i + 1] = value[0:1]
    go(edge_x, edge_y)

    def widen(first, count, columns, together):
        to = slice(columns.start + 8, columns.stop + 8)

        @pl.loop(0, count // together)
        def _(b):
            for a in range(together):
                win[first + together * b + a, to] = ext[first + together * b + a, columns].astype(F32)
        for r in range(first + count // together * together, first + count):
            win[r, to] = ext[r, columns].astype(F32)

    local.wait()
    build_tables(ns, inter, proj, up, down, down2, square, gather, dz)
    picks = (side + cols - rim, side + rim - 1)

    @pl.loop(0, rows // 8)
    def _(b):
        for a in range(8):
            for i, col in enumerate(picks):
                tile = ext[rim + 8 * b + a, col // 16 * 16:col // 16 * 16 + 16, :].astype(F32)
                colf[i, pl.ds(8 * b + a, 1), :] = tile[col % 16:col % 16 + 1]
    colb[...] = colf[...].astype(BF16)
    thin = [remote(hi_n, lo_n, colb.at[0], extra.at[0, emid], up_n),
            remote(lo_n, hi_n, colb.at[1], extra.at[1, emid], dn_n)]
    go(*thin)

    absent(lo_n, (ext, (every, ylo)))
    absent(hi_n, (ext, (every, yhi)))
    absent(lo_w, (ext, below))
    absent(hi_w, (ext, above))
    widen(rim, rows, mid, 2)
    come(edge_x)
    edge_c = remote(hi_w & lo_n, hi_w & hi_n, nodes.at[nel, 0:8], corner_in, dn_n)
    go(edge_c)
    come(edge_y)
    top = lax.broadcasted_iota(jnp.int32, (QPAD - nel, 128), 0) == 0
    for i in range(nel):
        nodes[i, nel:QPAD] = jnp.where(top, jnp.broadcast_to(side_in[i:i + 1], (QPAD - nel, 128)), 0.0)
    come(edge_c)
    nodes[nel, nel:QPAD] = jnp.where(top, jnp.broadcast_to(corner_in[0:1], (QPAD - nel, 128)), 0.0)
    flat = nodes[...].reshape(-1, 128)
    high = flat.astype(BF16).astype(F32)
    both = jnp.concatenate([high, flat - high], axis=1).astype(BF16)
    level = jnp.dot(both, up[...], preferred_element_type=F32)
    for i in range(nel + 1):
        head, tail = split(level[i * QPAD:(i + 1) * QPAD])
        field[i] = jnp.dot(inter[...], jnp.concatenate([head, tail], axis=0), preferred_element_type=F32)
    for ref in (gsum, qbuf, dacc):
        ref[...] = jnp.zeros_like(ref)
    come(*first_hop)
    go(*second_hop)
    offsets.wait()
    slab.wait()
    steps, chunks = rows // 8, cols // 16
    start = map_ref[0] + side
    col0 = map_ref[1] + 8 + side

    def fold(u, t):
        got = jnp.dot(square[...], qbuf[u], preferred_element_type=F32)
        dpart[t] = got[0:16] + got[16:32]

    def slopes(p, j):
        row0 = start + 8 * p + 1
        at = col0 + 16 * j
        here = jnp.concatenate([win[row0 + k, pl.ds(at, 16), :].astype(BF16) for k in range(8)], axis=0)
        return jnp.dot(here, dz[...], preferred_element_type=F32)

    def phase(pairs, place, before):
        for u in range(2):
            zbuf[u] = slopes(*place(0, u))

        @pl.loop(0, pairs)
        def _(b):
            coming = [slopes(*place(jnp.minimum(b + 1, pairs - 1), u)) for u in range(2)]
            for u in range(2):
                last = place(jnp.maximum(b - 1, 0), u)
                fold(u, jnp.where(b == 0, before[u][0] * chunks + before[u][1], last[0] * chunks + last[1]))
            for u in range(2):
                p, j = place(b, u)
                at = 16 * j if isinstance(j, int) else pl.multiple_of(16 * j, 16)
                base = 8 * p
                row0 = start + base
                refs = [res[base + k, pl.ds(at, 16), :].astype(F32) for k in range(8)]
                out_rows, squares, parts = voxels(
                    lambda k, shift, half: win[row0 + k, pl.ds(col0 + at + (8 * half + shift), 8), :],
                    lambda k, half: zbuf[u, 16 * k + 8 * half:16 * k + 8 * half + 8, :],
                    lambda k, half: refs[k][8 * half:8 * half + 8],
                    lambda c, half: field[p, pl.ds(at + 8 * half, 8), c * layers:(c + 1) * layers],
                    lambda c, half: field[p + 1, pl.ds(at + 8 * half, 8), c * layers:(c + 1) * layers])
                for k in range(8):
                    res[base + k, pl.ds(at, 16), :] = out_rows[k]
                for c in range(comps):
                    lanes = slice(c * layers, (c + 1) * layers)
                    for k in range(8):
                        qbuf[u, 16 * k:16 * k + 16, lanes] = squares[k][c]
                    for i in range(2):
                        gsum[p + i, pl.ds(at, 16), lanes] = gsum[p + i, pl.ds(at, 16), lanes] + parts[c][i]
            for u in range(2):
                zbuf[u] = coming[u]
        return [place(pairs - 1, u) for u in range(2)]

    p_in = (rim + 7) // 8
    n_in = steps - 2 * p_in
    j_in = (rim + 15) // 16
    other = (chunks - 2) // 2

    def inner_rows(i):
        return p_in + i

    def outer_rows(i):
        return i + n_in * as_int(jnp.asarray(i) >= p_in) if not isinstance(i, int) else i + n_in * (i >= p_in)

    def outer_chunk(i, u):
        m = 2 * i + u
        return m + 2 * (m >= j_in) if isinstance(m, int) else m + 2 * as_int(m >= j_in)

    def by_row(rows_of):
        return lambda b, u: (rows_of(b), j_in + u)

    def by_rest(rows_of):
        def place(b, u):
            if isinstance(b, int):
                return rows_of(b // other), outer_chunk(b % other, u)
            return rows_of(lax.div(b, other)), outer_chunk(lax.rem(b, other), u)
        return place

    done = [by_row(inner_rows)(0, u) for u in range(2)]
    done = phase(n_in, by_row(inner_rows), done)
    corners = []
    come(*strips[0], *strips[1])
    corners += [
        remote(hi_w & lo_n, lo_w & lo_n, ext.at[rows:rows + rim, ylo], ext.at[below, ylo], up_w),
        remote(hi_w & hi_n, lo_w & hi_n, ext.at[rows:rows + rim, yhi], ext.at[below, yhi], up_w),
        remote(lo_w & lo_n, hi_w & lo_n, ext.at[rim:2 * rim, ylo], ext.at[above, ylo], dn_w),
        remote(lo_w & hi_n, hi_w & hi_n, ext.at[rim:2 * rim, yhi], ext.at[above, yhi], dn_w)]
    come(*thin)
    corners += [
        remote(lo_n & lo_w, lo_n & hi_w, extra.at[0, elow], extra.at[0, eabove], dn_w),
        remote(lo_n & hi_w, lo_n & lo_w, extra.at[0, ehigh], extra.at[0, ebelow], up_w),
        remote(hi_n & lo_w, hi_n & hi_w, extra.at[1, elow], extra.at[1, eabove], dn_w),
        remote(hi_n & hi_w, hi_n & lo_w, extra.at[1, ehigh], extra.at[1, ebelow], up_w)]
    go(*corners)
    for k in strips[0] + strips[1]:
        @pl.when(everything[k][0])
        def _(k=k):
            everything[k][2].wait_send()
    go(*strips[2])

    strain_pull(ns, nodes, pull)
    for part in full[:2]:
        widen(part.start + rim, rim, ylo, 4)
        widen(part.start + rim, rim, yhi, 4)
    spots = (7, 8 + cols + 2 * side)

    def rims(span, source, first, count):
        rimcol[:, span] = extra[:, span].astype(F32)
        for r in range(count % 4):
            for i, spot in enumerate(spots):
                win[first + r, spot:spot + 1] = rimcol[i, source + r:source + r + 1]

        @pl.loop(0, count // 4)
        def _(b):
            for a in range(4):
                r = count % 4 + 4 * b + a
                for i, spot in enumerate(spots):
                    win[first + r, spot:spot + 1] = rimcol[i, pl.ds(source + r, 1), :]

    come(*bands, *second_hop)
    widen(0, rim, mid, 2)
    widen(rim + rows, rim, mid, 2)
    done = phase(2 * p_in, by_row(outer_rows), done)
    rims(emid, SIDE, rim, rows)
    come(*strips[2])
    widen(2 * rim, rows - 2 * rim, ylo, 4)
    widen(2 * rim, rows - 2 * rim, yhi, 4)
    done = phase(n_in * other, by_rest(inner_rows), done)
    come(*corners)
    for first in (0, rim + rows):
        widen(first, rim, ylo, 4)
        widen(first, rim, yhi, 4)
    rims(slice(0, SIDE), SIDE - rim, 0, rim)
    rims(slice(SIDE + rows, 2 * SIDE + rows), SIDE + rows, rim + rows, rim)
    done = phase(2 * p_in * other, by_rest(outer_rows), done)
    for u in range(2):
        fold(u, done[u][0] * chunks + done[u][1])
    for i in range(steps + 1):
        head, tail = split(gsum[i])
        gacc[i] = jnp.dot(proj[...], jnp.concatenate([head, tail], axis=0), preferred_element_type=F32)
    for i in range(steps):
        head, tail = split(dpart[i * chunks:(i + 1) * chunks].reshape(cols, comps * layers))
        got = jnp.dot(gather[...], jnp.concatenate([head, tail], axis=0), preferred_element_type=F32)
        dacc[i] = dacc[i] + got[0:QPAD]
        dacc[i + 1] = got[QPAD:2 * QPAD]
    for k, (acc, table) in enumerate(((gacc, down), (dacc, down2))):
        head, tail = split(acc[...].reshape(-1, comps * layers))
        got = (jnp.dot(head, table[...], preferred_element_type=F32)
               + jnp.dot(tail, table[...], preferred_element_type=F32)).reshape(pull.shape)
        terms[k] = got + pull[...] if k == 0 else got

    for k in range(2):
        for p in range(nel):
            colf[k, p:p + 1] = terms[k, p, nel:nel + 1]
    to_w = remote(hi_w, lo_w, terms.at[:, nel], from_w, up_w)
    to_n = remote(hi_n, lo_n, colf.at[:, 0:nel], from_n, up_n)
    to_c = remote(lo_w & hi_n, lo_w & lo_n, from_w.at[:, nel:QPAD], from_c, up_n)
    go(to_w, to_n)
    come(to_w)
    go(to_c)
    come(to_n, to_c)
    first_row = lax.broadcasted_iota(jnp.int32, (nel, 128), 0) == 0
    for p in range(nel):
        both = []
        for k in range(2):
            value = terms[k, p, 0:nel]
            beside = from_n[k, p:p + 1]
            if p == 0:
                value = value + from_w[k, 0:nel]
                beside = beside + from_c[k, 0:1]
            both.append(value + jnp.where(first_row, jnp.broadcast_to(beside, (nel, 128)), 0.0))
        step = both[0] / (both[1] + STIFFNESS)
        for c in range(comps):
            here = step if c == 0 else pltpu.roll(step, 128 - ns * c, 1)
            change[c, p] = here[:, 0:ns]
    sent = strips[0] + strips[1]
    for k, (goes, _c, copy) in enumerate(everything):
        if k not in sent:
            @pl.when(goes)
            def _(copy=copy):
                copy.wait_send()


def emit_kernel(parts, kept, change, disp, residual, updated, fresh, sem):
    rows = kept.shape[0] // parts
    copies = [pltpu.make_async_copy(kept.at[k * rows:(k + 1) * rows], residual.at[k * rows:(k + 1) * rows], sem.at[k])
              for k in range(parts)]
    for copy in copies:
        copy.start()
    fresh[...] = disp[...] - change[...]
    last = pltpu.make_async_copy(fresh, updated, sem.at[parts])
    last.start()
    for copy in copies + [last]:
        copy.wait()


def emit(kept, change, nodal):
    anywhere = pl.BlockSpec(memory_space=pl.ANY)
    near = pl.BlockSpec(memory_space=pltpu.VMEM)
    parts = 8
    return pl.pallas_call(
        functools.partial(emit_kernel, parts),
        out_shape=[jax.ShapeDtypeStruct(kept.shape, BF16), jax.ShapeDtypeStruct(nodal.shape, F32)],
        in_specs=[anywhere, near, near],
        out_specs=[anywhere, anywhere],
        scratch_shapes=[pltpu.VMEM(nodal.shape, F32), pltpu.SemaphoreType.DMA((parts + 1,))],
        compiler_params=pltpu.CompilerParams(vmem_limit_bytes=8 << 20),
        name="emit",
    )(kept, change, nodal)


def per_device(nw, nn, reference_image, deformed_image, displacement, tile_map):
    comps, ns, nel, _ = displacement.shape
    rows, cols, layers = reference_image.shape
    nodal = displacement.transpose(0, 2, 3, 1)
    rim = rows // 4 + 1
    npx, lanes = nel + 1, comps * layers
    total, across = rows + 2 * rim, cols + 2 * (rim - 1)
    anywhere = pl.BlockSpec(memory_space=pl.ANY)
    near = pl.BlockSpec(memory_space=pltpu.VMEM)
    kept, change = pl.pallas_call(
        functools.partial(step_kernel, nw, nn, rim, ns),
        out_shape=[jax.ShapeDtypeStruct(reference_image.shape, BF16),
                   jax.ShapeDtypeStruct(nodal.shape, F32)],
        in_specs=[anywhere] * 4,
        out_specs=[near, near],
        scratch_shapes=[
            pltpu.VMEM((cols, 2 * QPAD), BF16),
            pltpu.VMEM((QPAD, 2 * cols), BF16),
            pltpu.VMEM((2 * 128, lanes), BF16),
            pltpu.VMEM((lanes, 128), BF16),
            pltpu.VMEM((lanes, 128), BF16),
            pltpu.VMEM((32, 8 * 16), BF16),
            pltpu.VMEM((2 * QPAD, 2 * cols), BF16),
            pltpu.VMEM((layers, layers), BF16),
            pltpu.VMEM((total, across, layers), BF16),
            pltpu.VMEM((rim, cols - cols // 4, layers), BF16),
            pltpu.VMEM((total, across + 16, layers), F32),
            pltpu.VMEM((npx, cols, lanes), F32),
            pltpu.VMEM((npx, cols, lanes), F32),
            pltpu.VMEM((2, 8 * 16, lanes), BF16),
            pltpu.VMEM((2, 8 * 16, layers), F32),
            pltpu.VMEM((rows // 8 * (cols // 16), 16, lanes), F32),
            pltpu.VMEM((npx, QPAD, lanes), F32),
            pltpu.VMEM((npx, QPAD, lanes), F32),
            pltpu.VMEM((2, npx, QPAD, 128), F32),
            pltpu.VMEM((2, rows + 2 * SIDE, layers), BF16),
            pltpu.VMEM((2, rows + 2 * SIDE, layers), F32),
            pltpu.VMEM((npx, QPAD, 128), F32),
            pltpu.VMEM((npx, QPAD, 128), F32),
            pltpu.VMEM((comps, nel, nel, 128), F32),
            pltpu.VMEM((nel, 128), F32),
            pltpu.VMEM((nel, 128), F32),
            pltpu.VMEM((8, 128), F32),
            pltpu.VMEM((2, rows, layers), F32),
            pltpu.VMEM((2, rows, layers), BF16),
            pltpu.VMEM((2, QPAD, 128), F32),
            pltpu.VMEM((2, nel, 128), F32),
            pltpu.VMEM((2, QPAD - nel, 128), F32),
            pltpu.VMEM(nodal.shape, F32),
            pltpu.SMEM((2,), jnp.int32),
            pltpu.SemaphoreType.DMA((34,)),
            pltpu.SemaphoreType.DMA((34,)),
            pltpu.SemaphoreType.DMA((4,)),
        ],
        compiler_params=pltpu.CompilerParams(
            collective_id=0, has_side_effects=True, vmem_limit_bytes=48 << 20),
        name="step",
    )(tile_map.reshape(2), deformed_image, reference_image, nodal)
    residual, updated = emit(kept, change, nodal)
    return (updated.transpose(0, 3, 1, 2), residual)


def solution(mesh):
    placed = (
        P("wide", "narrow", None),
        P("wide", "narrow", None),
        P(None, None, "wide", "narrow"),
        P("wide", "narrow", None),
    )
    return jax.shard_map(
        functools.partial(per_device, mesh.shape["wide"], mesh.shape["narrow"]),
        mesh=mesh,
        in_specs=placed,
        out_specs=(P(None, None, "wide", "narrow"), P("wide", "narrow", None)),
        check_vma=False,
    )
```

```python
import functools

import jax
import jax.numpy as jnp
from jax import lax
from jax.experimental import pallas as pl
from jax.experimental.pallas import tpu as pltpu
from jax.sharding import PartitionSpec as P

MU_SHEAR = 1.0
LAMBDA_BULK = 2.0
REG_WEIGHT = 256.0
STIFFNESS = 16.0
MESH = pl.DeviceIdType.MESH
F32 = jnp.float32
BF16 = jnp.bfloat16
SIDE = 48
QPAD = 24


def as_int(flag):
    return flag.astype(jnp.int32)


def hat(place, node):
    at = (place.astype(F32) + 0.5) * 0.125
    return jnp.maximum(1.0 - jnp.abs(at - node.astype(F32)), 0.0)


def build_tables(ns, inter, proj, up, down, down2, square, gather, dz):
    def grid(ref):
        return (lax.broadcasted_iota(jnp.int32, ref.shape, 0), lax.broadcasted_iota(jnp.int32, ref.shape, 1))

    cols = inter.shape[0]
    r, c = grid(inter)
    inter[...] = (0.5 * hat(r, jnp.where(c < QPAD, c, c - QPAD))).astype(BF16)
    r, c = grid(proj)
    proj[...] = hat(jnp.where(c < cols, c, c - cols), r).astype(BF16)
    r, c = grid(up)
    up[...] = hat(c % 128, r % 128 - ns * (c // 128)).astype(BF16)
    r, c = grid(down)
    layer = hat(r % 128, c - ns * (r // 128))
    down[...] = (-0.5 * layer).astype(BF16)
    down2[...] = (0.25 * layer * layer).astype(BF16)
    r, c = grid(square)
    along = (c // 16).astype(F32) * 0.125 + 0.0625
    along = jnp.where(r % 16 < 8, 1.0 - along, along)
    across = hat(c % 16, r % 8)
    whole = (along * along) * (across * across)
    head = whole.astype(BF16).astype(F32)
    square[...] = jnp.where(r < 16, head, whole - head).astype(BF16)
    r, c = grid(dz)
    dz[...] = (jnp.where(r == c + 1, 1.0, 0.0) - jnp.where(r == c - 1, 1.0, 0.0)).astype(BF16)
    r, c = grid(gather)
    low = r < QPAD
    node = jnp.where(low, r, r - QPAD)
    k = c % 128
    same = (node == 2 * (k // 16) + k % 8) & (k % 8 < 3) & (low == (k % 16 < 8))
    gather[...] = jnp.where(same, 1.0, 0.0).astype(BF16)


def split(value):
    high = value.astype(BF16)
    return high, (value - high.astype(F32)).astype(BF16)


def strain_pull(ns, nodes, pull):
    npx = nodes.shape[0]
    nel = npx - 1
    lane = lax.broadcasted_iota(jnp.int32, (nel, 128), 1)
    move = lambda a, by: pltpu.roll(a, by % 128, 1)
    pull[...] = jnp.zeros_like(pull)

    @pl.loop(0, nel)
    def _(p):
        a00, a01 = nodes[p, 0:nel], nodes[p, 1:nel + 1]
        a10, a11 = nodes[p + 1, 0:nel], nodes[p + 1, 1:nel + 1]
        dx = (a10 - a00) + (a11 - a01)
        dy = (a01 - a00) + (a11 - a10)
        every = (a00 + a01) + (a10 + a11)
        slopes = (dx + move(dx, -1), dy + move(dy, -1), move(every, -1) - every)
        f = [[0.03125 * (move(h, -ns * i) if i else h) + (1.0 if i == j else 0.0)
              for j, h in enumerate(slopes)] for i in range(3)]
        cof = [[f[(i + 1) % 3][(j + 1) % 3] * f[(i + 2) % 3][(j + 2) % 3]
                - f[(i + 1) % 3][(j + 2) % 3] * f[(i + 2) % 3][(j + 1) % 3]
                for j in range(3)] for i in range(3)]
        ratio = f[0][0] * cof[0][0] + f[0][1] * cof[0][1] + f[0][2] * cof[0][2]
        factor = (LAMBDA_BULK * jnp.log(ratio) - MU_SHEAR) / ratio
        back = []
        for j in range(3):
            parts = [jnp.where(lane < ns - 1, MU_SHEAR * f[i][j] + factor * cof[i][j], 0.0) for i in range(3)]
            back.append((parts[0] + move(parts[1], ns) + move(parts[2], 2 * ns)) * (0.03125 * REG_WEIGHT))
        gx = back[0] + move(back[0], 1)
        gy = back[1] + move(back[1], 1)
        gz = move(back[2], 1) - back[2]
        for dp, dq in ((0, 0), (0, 1), (1, 0), (1, 1)):
            add = (gx if dp else -gx) + (gy if dq else -gy) + gz
            pull[p + dp, dq:dq + nel] = pull[p + dp, dq:dq + nel] + add


def voxels(window, slope_z, ref_rows, left, right):
    back = []
    rows, squares = [None] * 8, [[None] * 3 for _ in range(8)]
    join = lambda a, b: jnp.concatenate([a, b], axis=0)
    for half in range(2):
        run, tot = [None] * 3, [None] * 3
        inc = [(right(c, half) - left(c, half)) * 0.125 for c in range(3)]
        mv = [left(c, half) + 0.5 * inc[c] for c in range(3)]
        prev, cur = window(0, 0, half), window(1, 0, half)
        for k in range(8):
            nxt = window(k + 2, 0, half)
            g = [nxt - prev,
                 window(k + 1, 1, half) - window(k + 1, -1, half),
                 slope_z(k, half)]
            r = ref_rows(k, half) - cur
            for c in range(3):
                r = r - g[c] * mv[c]
                if k < 7:
                    mv[c] = mv[c] + inc[c]
            rows[k] = r if half == 0 else join(rows[k], r).astype(BF16)
            for c in range(3):
                f = g[c] * r
                q = g[c] * g[c]
                run[c] = f if k == 0 else run[c] + f
                tot[c] = run[c] if k == 0 else tot[c] + run[c]
                squares[k][c] = q if half == 0 else join(squares[k][c], q).astype(BF16)
            prev, cur = cur, nxt
        part = []
        for c in range(3):
            low = (tot[c] - 0.5 * run[c]) * 0.125
            part.append((low, run[c] - low))
        back.append(part)
    return rows, squares, [[join(back[0][c][i], back[1][c][i]) for i in range(2)] for c in range(3)]


def step_kernel(nw, nn, rim, ns, map_hbm, own, ref_hbm, disp_hbm,
                res, change,
                inter, proj, up, down, down2, square, gather, dz,
                ext, passed, win, field, gsum, qbuf, zbuf, dpart, gacc, dacc, terms,
                extra, rimcol, nodes, pull, cube, column, side_in, corner_in, colf, colb,
                from_w, from_n, from_c, disp, map_ref, send, recv, lsem):
    rows, cols, layers = own.shape
    comps, nel = disp.shape[0], disp.shape[1]
    side = rim - 1
    w = lax.axis_index("wide")
    n = lax.axis_index("narrow")
    lo_w, hi_w, lo_n, hi_n = w > 0, w < nw - 1, n > 0, n < nn - 1
    up_w, dn_w = (w + 1, n), (w - 1, n)
    up_n, dn_n = (w, n + 1), (w, n - 1)
    mid = slice(side, side + cols)
    ylo = slice(0, side)
    yhi = slice(side + cols, 2 * side + cols)
    total = rows + 2 * rim
    emid = slice(SIDE, SIDE + rows)
    detour = nw == 8
    is0, is3, is4, is7 = (w == 0), (w == 3), (w == 4), (w == 7)

    barrier = pltpu.get_barrier_semaphore()
    greet = [(lo_w, dn_w), (hi_w, up_w), (lo_n, dn_n), (hi_n, up_n), (lo_w & lo_n, (w - 1, n - 1))]
    if detour:
        greet += [(is7, (3, n)), (is4, (7, n)), (is0, (4, n)), (is3, (0, n))]
    count = as_int(lo_w) + as_int(hi_w) + as_int(lo_n) + as_int(hi_n) + as_int(hi_w & hi_n)
    if detour:
        count = count + as_int(is0 | is3 | is4 | is7)
    for there, device in greet:
        @pl.when(there)
        def _(device=device):
            pl.semaphore_signal(barrier, inc=1, device_id=device, device_id_type=MESH)
    loads = [pltpu.make_async_copy(disp_hbm, disp, lsem.at[2]),
             pltpu.make_async_copy(own, ext.at[rim:rim + rows, mid], lsem.at[0]),
             pltpu.make_async_copy(ref_hbm, res, lsem.at[1]),
             pltpu.make_async_copy(map_hbm, map_ref, lsem.at[3])]
    for load in loads:
        load.start()
    nodal, local, slab, offsets = loads

    def absent(there, *spans):
        @pl.when(jnp.logical_not(there))
        def _():
            for ref, span in spans:
                ref[span] = jnp.zeros(ref.at[span].shape, ref.dtype)

    elow, ehigh = slice(SIDE, 2 * SIDE), slice(rows, SIDE + rows)
    ebelow, eabove = slice(0, SIDE), slice(SIDE + rows, 2 * SIDE + rows)
    every = slice(None)
    absent(hi_w, (nodes, (nel, slice(0, nel))))
    absent(hi_n, (side_in, every), (extra, 1))
    absent(hi_w & hi_n, (corner_in, every), (extra, (1, eabove)))
    absent(lo_w & hi_n, (extra, (1, ebelow)))
    absent(lo_w, (from_w, every))
    absent(lo_n, (from_n, every), (extra, 0))
    absent(lo_w & lo_n, (from_c, every), (extra, (0, ebelow)))
    absent(hi_w & lo_n, (extra, (0, eabove)))
    pl.semaphore_wait(barrier, count)

    everything = []

    def remote(goes, comes, src, dst, device):
        k = len(everything)
        copy = pltpu.make_async_remote_copy(
            src_ref=src, dst_ref=dst, send_sem=send.at[k], recv_sem=recv.at[k],
            device_id=device, device_id_type=MESH)
        everything.append((goes, comes, copy))
        return k

    def go(*ks):
        for k in ks:
            @pl.when(everything[k][0])
            def _(k=k):
                everything[k][2].start()

    def come(*ks):
        for k in ks:
            @pl.when(everything[k][1])
            def _(k=k):
                everything[k][2].wait_recv()

    below, above = slice(0, rim), slice(rim + rows, total)
    edge_x = remote(lo_w, hi_w, nodes.at[0, 0:nel], nodes.at[nel, 0:nel], dn_w)
    edge_y = remote(lo_n, hi_n, column, side_in, dn_n)
    strips = []
    full = (slice(0, rim), slice(rows - rim, rows), slice(rim, rows - rim))
    for part in full:
        there = slice(part.start + rim, part.stop + rim)
        strips.append((
            remote(hi_n, lo_n, own.at[part, cols - side:cols], ext.at[there, ylo], up_n),
            remote(lo_n, hi_n, own.at[part, 0:side], ext.at[there, yhi], dn_n)))
    cut = cols // 4 if detour else cols
    near, far = slice(0, cut), slice(cut, cols)
    enear, efar = slice(side, side + cut), slice(side + cut, side + cols)
    high_own, low_own = slice(rows - rim, rows), slice(0, rim)
    bands = [
        remote(hi_w, lo_w, own.at[high_own, near], ext.at[below, enear], up_w),
        remote(lo_w, hi_w, own.at[low_own, near], ext.at[above, enear], dn_w)]
    first_hop, second_hop = [], []
    if detour:
        bands += [
            remote(hi_w & (w != 3), lo_w & (w != 4), own.at[high_own, far], ext.at[below, efar], up_w),
            remote(lo_w & (w != 4), hi_w & (w != 3), own.at[low_own, far], ext.at[above, efar], dn_w)]
        first_hop = [
            remote(is3, is7, own.at[high_own, far], passed, (7, n)),
            remote(is4, is0, own.at[low_own, far], passed, (0, n))]
        second_hop = [
            remote(is7, is4, passed, ext.at[below, efar], (4, n)),
            remote(is0, is3, passed, ext.at[above, efar], (3, n))]
    go(*strips[0], *strips[1], *first_hop, *bands)
    cube[...] = jnp.zeros_like(cube)
    nodal.wait()
    cube[:, :, :, 0:ns] = disp[...]
    for i in range(nel):
        value = cube[0, i]
        for c in range(1, comps):
            value = value + pltpu.roll(cube[c, i], ns * c, 1)
        nodes[i, 0:nel] = value
        column[i:i + 1] = value[0:1]
    go(edge_x, edge_y)

    def widen(first, count, columns, together):
        to = slice(columns.start + 8, columns.stop + 8)

        @pl.loop(0, count // together)
        def _(b):
            for a in range(together):
                win[first + together * b + a, to] = ext[first + together * b + a, columns].astype(F32)
        for r in range(first + count // together * together, first + count):
            win[r, to] = ext[r, columns].astype(F32)

    local.wait()
    widen(rim, rows, mid, 2)
    build_tables(ns, inter, proj, up, down, down2, square, gather, dz)
    absent(lo_n, (ext, (every, ylo)))
    absent(hi_n, (ext, (every, yhi)))
    absent(lo_w, (ext, below))
    absent(hi_w, (ext, above))
    come(edge_x)
    edge_c = remote(hi_w & lo_n, hi_w & hi_n, nodes.at[nel, 0:8], corner_in, dn_n)
    go(edge_c)
    come(edge_y)
    top = lax.broadcasted_iota(jnp.int32, (QPAD - nel, 128), 0) == 0
    for i in range(nel):
        nodes[i, nel:QPAD] = jnp.where(top, jnp.broadcast_to(side_in[i:i + 1], (QPAD - nel, 128)), 0.0)
    come(edge_c)
    nodes[nel, nel:QPAD] = jnp.where(top, jnp.broadcast_to(corner_in[0:1], (QPAD - nel, 128)), 0.0)
    flat = nodes[...].reshape(-1, 128)
    high = flat.astype(BF16).astype(F32)
    both = jnp.concatenate([high, flat - high], axis=1).astype(BF16)
    level = jnp.dot(both, up[...], preferred_element_type=F32)
    for i in range(nel + 1):
        head, tail = split(level[i * QPAD:(i + 1) * QPAD])
        field[i] = jnp.dot(inter[...], jnp.concatenate([head, tail], axis=0), preferred_element_type=F32)
    for ref in (gsum, qbuf, dacc):
        ref[...] = jnp.zeros_like(ref)
    offsets.wait()
    slab.wait()
    steps, chunks = rows // 8, cols // 16
    start = map_ref[0] + side
    col0 = map_ref[1] + 8 + side

    def fold(u, t):
        got = jnp.dot(square[...], qbuf[u], preferred_element_type=F32)
        dpart[t] = got[0:16] + got[16:32]

    def slopes(p, j):
        row0 = start + 8 * p + 1
        at = col0 + 16 * j
        here = jnp.concatenate([win[row0 + k, pl.ds(at, 16), :].astype(BF16) for k in range(8)], axis=0)
        return jnp.dot(here, dz[...], preferred_element_type=F32)

    def phase(pairs, place, before):
        for u in range(2):
            zbuf[u] = slopes(*place(0, u))

        @pl.loop(0, pairs)
        def _(b):
            coming = [slopes(*place(jnp.minimum(b + 1, pairs - 1), u)) for u in range(2)]
            for u in range(2):
                last = place(jnp.maximum(b - 1, 0), u)
                fold(u, jnp.where(b == 0, before[u][0] * chunks + before[u][1], last[0] * chunks + last[1]))
            for u in range(2):
                p, j = place(b, u)
                at = 16 * j if isinstance(j, int) else pl.multiple_of(16 * j, 16)
                base = 8 * p
                row0 = start + base
                refs = [res[base + k, pl.ds(at, 16), :].astype(F32) for k in range(8)]
                out_rows, squares, parts = voxels(
                    lambda k, shift, half: win[row0 + k, pl.ds(col0 + at + (8 * half + shift), 8), :],
                    lambda k, half: zbuf[u, 16 * k + 8 * half:16 * k + 8 * half + 8, :],
                    lambda k, half: refs[k][8 * half:8 * half + 8],
                    lambda c, half: field[p, pl.ds(at + 8 * half, 8), c * layers:(c + 1) * layers],
                    lambda c, half: field[p + 1, pl.ds(at + 8 * half, 8), c * layers:(c + 1) * layers])
                for k in range(8):
                    res[base + k, pl.ds(at, 16), :] = out_rows[k]
                for c in range(comps):
                    lanes = slice(c * layers, (c + 1) * layers)
                    for k in range(8):
                        qbuf[u, 16 * k:16 * k + 16, lanes] = squares[k][c]
                    for i in range(2):
                        gsum[p + i, pl.ds(at, 16), lanes] = gsum[p + i, pl.ds(at, 16), lanes] + parts[c][i]
            for u in range(2):
                zbuf[u] = coming[u]
        return [place(pairs - 1, u) for u in range(2)]

    p_in = (rim + 7) // 8
    n_in = steps - 2 * p_in
    j_in = (rim + 15) // 16
    other = (chunks - 2) // 2

    def inner_rows(i):
        return p_in + i

    def outer_rows(i):
        return i + n_in * as_int(jnp.asarray(i) >= p_in) if not isinstance(i, int) else i + n_in * (i >= p_in)

    def outer_chunk(i, u):
        m = 2 * i + u
        return m + 2 * (m >= j_in) if isinstance(m, int) else m + 2 * as_int(m >= j_in)

    def by_row(rows_of):
        return lambda b, u: (rows_of(b), j_in + u)

    def by_rest(rows_of):
        def place(b, u):
            if isinstance(b, int):
                return rows_of(b // other), outer_chunk(b % other, u)
            return rows_of(lax.div(b, other)), outer_chunk(lax.rem(b, other), u)
        return place

    done = [by_row(inner_rows)(0, u) for u in range(2)]
    done = phase(n_in, by_row(inner_rows), done)
    come(*first_hop)
    go(*second_hop)
    corners = []
    come(*strips[0], *strips[1])
    corners += [
        remote(hi_w & lo_n, lo_w & lo_n, ext.at[rows:rows + rim, ylo], ext.at[below, ylo], up_w),
        remote(hi_w & hi_n, lo_w & hi_n, ext.at[rows:rows + rim, yhi], ext.at[below, yhi], up_w),
        remote(lo_w & lo_n, hi_w & lo_n, ext.at[rim:2 * rim, ylo], ext.at[above, ylo], dn_w),
        remote(lo_w & hi_n, hi_w & hi_n, ext.at[rim:2 * rim, yhi], ext.at[above, yhi], dn_w)]
    go(*corners)
    for k in strips[0] + strips[1]:
        @pl.when(everything[k][0])
        def _(k=k):
            everything[k][2].wait_send()
    go(*strips[2])

    picks = (side + cols - rim, side + rim - 1)

    @pl.loop(0, rows // 8)
    def _(b):
        for a in range(8):
            for i, col in enumerate(picks):
                tile = ext[rim + 8 * b + a, col // 16 * 16:col // 16 * 16 + 16, :].astype(F32)
                colf[i, pl.ds(8 * b + a, 1), :] = tile[col % 16:col % 16 + 1]
    colb[...] = colf[...].astype(BF16)
    thin = [remote(hi_n, lo_n, colb.at[0], extra.at[0, emid], up_n),
            remote(lo_n, hi_n, colb.at[1], extra.at[1, emid], dn_n)]
    go(*thin)

    strain_pull(ns, nodes, pull)
    for part in full[:2]:
        widen(part.start + rim, rim, ylo, 4)
        widen(part.start + rim, rim, yhi, 4)
    come(*thin)
    thin_corners = [
        remote(lo_n & lo_w, lo_n & hi_w, extra.at[0, elow], extra.at[0, eabove], dn_w),
        remote(lo_n & hi_w, lo_n & lo_w, extra.at[0, ehigh], extra.at[0, ebelow], up_w),
        remote(hi_n & lo_w, hi_n & hi_w, extra.at[1, elow], extra.at[1, eabove], dn_w),
        remote(hi_n & hi_w, hi_n & lo_w, extra.at[1, ehigh], extra.at[1, ebelow], up_w)]
    go(*thin_corners)
    spots = (7, 8 + cols + 2 * side)

    def rims(span, source, first, count):
        rimcol[:, span] = extra[:, span].astype(F32)
        for r in range(count % 4):
            for i, spot in enumerate(spots):
                win[first + r, spot:spot + 1] = rimcol[i, source + r:source + r + 1]

        @pl.loop(0, count // 4)
        def _(b):
            for a in range(4):
                r = count % 4 + 4 * b + a
                for i, spot in enumerate(spots):
                    win[first + r, spot:spot + 1] = rimcol[i, pl.ds(source + r, 1), :]

    come(*bands, *second_hop)
    widen(0, rim, mid, 2)
    widen(rim + rows, rim, mid, 2)
    done = phase(2 * p_in, by_row(outer_rows), done)
    rims(emid, SIDE, rim, rows)
    come(*strips[2])
    widen(2 * rim, rows - 2 * rim, ylo, 4)
    widen(2 * rim, rows - 2 * rim, yhi, 4)
    done = phase(n_in * other, by_rest(inner_rows), done)
    come(*corners, *thin_corners)
    for first in (0, rim + rows):
        widen(first, rim, ylo, 4)
        widen(first, rim, yhi, 4)
    rims(slice(0, SIDE), SIDE - rim, 0, rim)
    rims(slice(SIDE + rows, 2 * SIDE + rows), SIDE + rows, rim + rows, rim)
    done = phase(2 * p_in * other, by_rest(outer_rows), done)
    for u in range(2):
        fold(u, done[u][0] * chunks + done[u][1])
    for i in range(steps + 1):
        head, tail = split(gsum[i])
        gacc[i] = jnp.dot(proj[...], jnp.concatenate([head, tail], axis=0), preferred_element_type=F32)
    for i in range(steps):
        head, tail = split(dpart[i * chunks:(i + 1) * chunks].reshape(cols, comps * layers))
        got = jnp.dot(gather[...], jnp.concatenate([head, tail], axis=0), preferred_element_type=F32)
        dacc[i] = dacc[i] + got[0:QPAD]
        dacc[i + 1] = got[QPAD:2 * QPAD]
    for k, (acc, table) in enumerate(((gacc, down), (dacc, down2))):
        head, tail = split(acc[...].reshape(-1, comps * layers))
        got = (jnp.dot(head, table[...], preferred_element_type=F32)
               + jnp.dot(tail, table[...], preferred_element_type=F32)).reshape(pull.shape)
        terms[k] = got + pull[...] if k == 0 else got

    for k in range(2):
        for p in range(nel):
            colf[k, p:p + 1] = terms[k, p, nel:nel + 1]
    to_w = remote(hi_w, lo_w, terms.at[:, nel], from_w, up_w)
    to_n = remote(hi_n, lo_n, colf.at[:, 0:nel], from_n, up_n)
    to_c = remote(hi_w & hi_n, lo_w & lo_n, terms.at[:, nel, nel:QPAD], from_c, (w + 1, n + 1))
    go(to_w, to_n, to_c)
    come(to_w, to_n, to_c)
    first_row = lax.broadcasted_iota(jnp.int32, (nel, 128), 0) == 0
    for p in range(nel):
        both = []
        for k in range(2):
            value = terms[k, p, 0:nel]
            beside = from_n[k, p:p + 1]
            if p == 0:
                value = value + from_w[k, 0:nel]
                beside = beside + from_c[k, 0:1]
            both.append(value + jnp.where(first_row, jnp.broadcast_to(beside, (nel, 128)), 0.0))
        step = both[0] / (both[1] + STIFFNESS)
        for c in range(comps):
            here = step if c == 0 else pltpu.roll(step, 128 - ns * c, 1)
            change[c, p] = here[:, 0:ns]
    sent = strips[0] + strips[1]
    for k, (goes, _c, copy) in enumerate(everything):
        if k not in sent:
            @pl.when(goes)
            def _(copy=copy):
                copy.wait_send()


def emit_kernel(parts, kept, change, disp, residual, updated, fresh, sem):
    rows = kept.shape[0] // parts
    copies = [pltpu.make_async_copy(kept.at[k * rows:(k + 1) * rows], residual.at[k * rows:(k + 1) * rows], sem.at[k])
              for k in range(parts)]
    for copy in copies:
        copy.start()
    fresh[...] = disp[...] - change[...]
    last = pltpu.make_async_copy(fresh, updated, sem.at[parts])
    last.start()
    for copy in copies + [last]:
        copy.wait()


def emit(kept, change, nodal):
    anywhere = pl.BlockSpec(memory_space=pl.ANY)
    near = pl.BlockSpec(memory_space=pltpu.VMEM)
    parts = 8
    return pl.pallas_call(
        functools.partial(emit_kernel, parts),
        out_shape=[jax.ShapeDtypeStruct(kept.shape, BF16), jax.ShapeDtypeStruct(nodal.shape, F32)],
        in_specs=[anywhere, near, near],
        out_specs=[anywhere, anywhere],
        scratch_shapes=[pltpu.VMEM(nodal.shape, F32), pltpu.SemaphoreType.DMA((parts + 1,))],
        compiler_params=pltpu.CompilerParams(vmem_limit_bytes=8 << 20),
        name="emit",
    )(kept, change, nodal)


def per_device(nw, nn, reference_image, deformed_image, displacement, tile_map):
    comps, ns, nel, _ = displacement.shape
    rows, cols, layers = reference_image.shape
    nodal = displacement.transpose(0, 2, 3, 1)
    rim = rows // 4 + 1
    npx, lanes = nel + 1, comps * layers
    total, across = rows + 2 * rim, cols + 2 * (rim - 1)
    anywhere = pl.BlockSpec(memory_space=pl.ANY)
    near = pl.BlockSpec(memory_space=pltpu.VMEM)
    kept, change = pl.pallas_call(
        functools.partial(step_kernel, nw, nn, rim, ns),
        out_shape=[jax.ShapeDtypeStruct(reference_image.shape, BF16),
                   jax.ShapeDtypeStruct(nodal.shape, F32)],
        in_specs=[anywhere] * 4,
        out_specs=[near, near],
        scratch_shapes=[
            pltpu.VMEM((cols, 2 * QPAD), BF16),
            pltpu.VMEM((QPAD, 2 * cols), BF16),
            pltpu.VMEM((2 * 128, lanes), BF16),
            pltpu.VMEM((lanes, 128), BF16),
            pltpu.VMEM((lanes, 128), BF16),
            pltpu.VMEM((32, 8 * 16), BF16),
            pltpu.VMEM((2 * QPAD, 2 * cols), BF16),
            pltpu.VMEM((layers, layers), BF16),
            pltpu.VMEM((total, across, layers), BF16),
            pltpu.VMEM((rim, cols - cols // 4, layers), BF16),
            pltpu.VMEM((total, across + 16, layers), F32),
            pltpu.VMEM((npx, cols, lanes), F32),
            pltpu.VMEM((npx, cols, lanes), F32),
            pltpu.VMEM((2, 8 * 16, lanes), BF16),
            pltpu.VMEM((2, 8 * 16, layers), F32),
            pltpu.VMEM((rows // 8 * (cols // 16), 16, lanes), F32),
            pltpu.VMEM((npx, QPAD, lanes), F32),
            pltpu.VMEM((npx, QPAD, lanes), F32),
            pltpu.VMEM((2, npx, QPAD, 128), F32),
            pltpu.VMEM((2, rows + 2 * SIDE, layers), BF16),
            pltpu.VMEM((2, rows + 2 * SIDE, layers), F32),
            pltpu.VMEM((npx, QPAD, 128), F32),
            pltpu.VMEM((npx, QPAD, 128), F32),
            pltpu.VMEM((comps, nel, nel, 128), F32),
            pltpu.VMEM((nel, 128), F32),
            pltpu.VMEM((nel, 128), F32),
            pltpu.VMEM((8, 128), F32),
            pltpu.VMEM((2, rows, layers), F32),
            pltpu.VMEM((2, rows, layers), BF16),
            pltpu.VMEM((2, QPAD, 128), F32),
            pltpu.VMEM((2, nel, 128), F32),
            pltpu.VMEM((2, QPAD - nel, 128), F32),
            pltpu.VMEM(nodal.shape, F32),
            pltpu.SMEM((2,), jnp.int32),
            pltpu.SemaphoreType.DMA((34,)),
            pltpu.SemaphoreType.DMA((34,)),
            pltpu.SemaphoreType.DMA((4,)),
        ],
        compiler_params=pltpu.CompilerParams(
            collective_id=0, has_side_effects=True, vmem_limit_bytes=48 << 20),
        name="step",
    )(tile_map.reshape(2), deformed_image, reference_image, nodal)
    residual, updated = emit(kept, change, nodal)
    return (updated.transpose(0, 3, 1, 2), residual)


def solution(mesh):
    placed = (
        P("wide", "narrow", None),
        P("wide", "narrow", None),
        P(None, None, "wide", "narrow"),
        P("wide", "narrow", None),
    )
    return jax.shard_map(
        functools.partial(per_device, mesh.shape["wide"], mesh.shape["narrow"]),
        mesh=mesh,
        in_specs=placed,
        out_specs=(P(None, None, "wide", "narrow"), P("wide", "narrow", None)),
        check_vma=False,
    )
```

```python
import functools

import jax
import jax.numpy as jnp
from jax import lax
from jax.experimental import pallas as pl
from jax.experimental.pallas import tpu as pltpu
from jax.sharding import PartitionSpec as P

MU_SHEAR = 1.0
LAMBDA_BULK = 2.0
REG_WEIGHT = 256.0
STIFFNESS = 16.0
MESH = pl.DeviceIdType.MESH
F32 = jnp.float32
BF16 = jnp.bfloat16
SIDE = 48
QPAD = 24


def as_int(flag):
    return flag.astype(jnp.int32)


def hat(place, node):
    at = (place.astype(F32) + 0.5) * 0.125
    return jnp.maximum(1.0 - jnp.abs(at - node.astype(F32)), 0.0)


def build_tables(ns, inter, proj, up, down, down2, square, gather, dz):
    def grid(ref):
        return (lax.broadcasted_iota(jnp.int32, ref.shape, 0), lax.broadcasted_iota(jnp.int32, ref.shape, 1))

    cols = inter.shape[0]
    r, c = grid(inter)
    inter[...] = (0.5 * hat(r, jnp.where(c < QPAD, c, c - QPAD))).astype(BF16)
    r, c = grid(proj)
    proj[...] = hat(jnp.where(c < cols, c, c - cols), r).astype(BF16)
    r, c = grid(up)
    up[...] = hat(c % 128, r % 128 - ns * (c // 128)).astype(BF16)
    r, c = grid(down)
    layer = hat(r % 128, c - ns * (r // 128))
    down[...] = (-0.5 * layer).astype(BF16)
    down2[...] = (0.25 * layer * layer).astype(BF16)
    r, c = grid(square)
    along = (c // 16).astype(F32) * 0.125 + 0.0625
    along = jnp.where(r % 16 < 8, 1.0 - along, along)
    across = hat(c % 16, r % 8)
    whole = (along * along) * (across * across)
    head = whole.astype(BF16).astype(F32)
    square[...] = jnp.where(r < 16, head, whole - head).astype(BF16)
    r, c = grid(dz)
    dz[...] = (jnp.where(r == c + 1, 1.0, 0.0) - jnp.where(r == c - 1, 1.0, 0.0)).astype(BF16)
    r, c = grid(gather)
    low = r < QPAD
    node = jnp.where(low, r, r - QPAD)
    k = c % 128
    same = (node == 2 * (k // 16) + k % 8) & (k % 8 < 3) & (low == (k % 16 < 8))
    gather[...] = jnp.where(same, 1.0, 0.0).astype(BF16)


def split(value):
    high = value.astype(BF16)
    return high, (value - high.astype(F32)).astype(BF16)


def strain_pull(ns, nodes, pull):
    npx = nodes.shape[0]
    nel = npx - 1
    lane = lax.broadcasted_iota(jnp.int32, (nel, 128), 1)
    move = lambda a, by: pltpu.roll(a, by % 128, 1)
    pull[...] = jnp.zeros_like(pull)

    @pl.loop(0, nel)
    def _(p):
        a00, a01 = nodes[p, 0:nel], nodes[p, 1:nel + 1]
        a10, a11 = nodes[p + 1, 0:nel], nodes[p + 1, 1:nel + 1]
        dx = (a10 - a00) + (a11 - a01)
        dy = (a01 - a00) + (a11 - a10)
        every = (a00 + a01) + (a10 + a11)
        slopes = (dx + move(dx, -1), dy + move(dy, -1), move(every, -1) - every)
        f = [[0.03125 * (move(h, -ns * i) if i else h) + (1.0 if i == j else 0.0)
              for j, h in enumerate(slopes)] for i in range(3)]
        cof = [[f[(i + 1) % 3][(j + 1) % 3] * f[(i + 2) % 3][(j + 2) % 3]
                - f[(i + 1) % 3][(j + 2) % 3] * f[(i + 2) % 3][(j + 1) % 3]
                for j in range(3)] for i in range(3)]
        ratio = f[0][0] * cof[0][0] + f[0][1] * cof[0][1] + f[0][2] * cof[0][2]
        factor = (LAMBDA_BULK * jnp.log(ratio) - MU_SHEAR) / ratio
        back = []
        for j in range(3):
            parts = [jnp.where(lane < ns - 1, MU_SHEAR * f[i][j] + factor * cof[i][j], 0.0) for i in range(3)]
            back.append((parts[0] + move(parts[1], ns) + move(parts[2], 2 * ns)) * (0.03125 * REG_WEIGHT))
        gx = back[0] + move(back[0], 1)
        gy = back[1] + move(back[1], 1)
        gz = move(back[2], 1) - back[2]
        for dp, dq in ((0, 0), (0, 1), (1, 0), (1, 1)):
            add = (gx if dp else -gx) + (gy if dq else -gy) + gz
            pull[p + dp, dq:dq + nel] = pull[p + dp, dq:dq + nel] + add


def voxels(window, slope_z, ref_rows, left, right):
    back = []
    rows, squares = [None] * 8, [[None] * 3 for _ in range(8)]
    join = lambda a, b: jnp.concatenate([a, b], axis=0)
    for half in range(2):
        run, tot = [None] * 3, [None] * 3
        inc = [(right(c, half) - left(c, half)) * 0.125 for c in range(3)]
        mv = [left(c, half) + 0.5 * inc[c] for c in range(3)]
        prev, cur = window(0, 0, half), window(1, 0, half)
        for k in range(8):
            nxt = window(k + 2, 0, half)
            g = [nxt - prev,
                 window(k + 1, 1, half) - window(k + 1, -1, half),
                 slope_z(k, half)]
            r = ref_rows(k, half) - cur
            for c in range(3):
                r = r - g[c] * mv[c]
                if k < 7:
                    mv[c] = mv[c] + inc[c]
            rows[k] = r if half == 0 else join(rows[k], r).astype(BF16)
            for c in range(3):
                f = g[c] * r
                q = g[c] * g[c]
                run[c] = f if k == 0 else run[c] + f
                tot[c] = run[c] if k == 0 else tot[c] + run[c]
                squares[k][c] = q if half == 0 else join(squares[k][c], q).astype(BF16)
            prev, cur = cur, nxt
        part = []
        for c in range(3):
            low = (tot[c] - 0.5 * run[c]) * 0.125
            part.append((low, run[c] - low))
        back.append(part)
    return rows, squares, [[join(back[0][c][i], back[1][c][i]) for i in range(2)] for c in range(3)]


def step_kernel(nw, nn, rim, ns, map_hbm, own, ref_hbm, disp_hbm,
                res, change,
                inter, proj, up, down, down2, square, gather, dz,
                ext, passed, win, field, gsum, qbuf, zbuf, dpart, gacc, dacc, terms,
                extra, rimcol, nodes, pull, cube, column, side_in, corner_in, colf, colb,
                from_w, from_n, from_c, disp, map_ref, send, recv, lsem):
    rows, cols, layers = own.shape
    comps, nel = disp.shape[0], disp.shape[1]
    side = rim - 1
    w = lax.axis_index("wide")
    n = lax.axis_index("narrow")
    lo_w, hi_w, lo_n, hi_n = w > 0, w < nw - 1, n > 0, n < nn - 1
    up_w, dn_w = (w + 1, n), (w - 1, n)
    up_n, dn_n = (w, n + 1), (w, n - 1)
    mid = slice(side, side + cols)
    ylo = slice(0, side)
    yhi = slice(side + cols, 2 * side + cols)
    total = rows + 2 * rim
    emid = slice(SIDE, SIDE + rows)
    detour = nw == 8
    is0, is3, is4, is7 = (w == 0), (w == 3), (w == 4), (w == 7)

    barrier = pltpu.get_barrier_semaphore()
    greet = [(lo_w, dn_w), (hi_w, up_w), (lo_n, dn_n), (hi_n, up_n)]
    if detour:
        greet += [(is7, (3, n)), (is4, (7, n)), (is0, (4, n)), (is3, (0, n))]
    count = as_int(lo_w) + as_int(hi_w) + as_int(lo_n) + as_int(hi_n)
    if detour:
        count = count + as_int(is0 | is3 | is4 | is7)
    for there, device in greet:
        @pl.when(there)
        def _(device=device):
            pl.semaphore_signal(barrier, inc=1, device_id=device, device_id_type=MESH)
    loads = [pltpu.make_async_copy(disp_hbm, disp, lsem.at[2]),
             pltpu.make_async_copy(own, ext.at[rim:rim + rows, mid], lsem.at[0]),
             pltpu.make_async_copy(ref_hbm, res, lsem.at[1]),
             pltpu.make_async_copy(map_hbm, map_ref, lsem.at[3])]
    for load in loads:
        load.start()
    nodal, local, slab, offsets = loads

    def absent(there, *spans):
        @pl.when(jnp.logical_not(there))
        def _():
            for ref, span in spans:
                ref[span] = jnp.zeros(ref.at[span].shape, ref.dtype)

    elow, ehigh = slice(SIDE, 2 * SIDE), slice(rows, SIDE + rows)
    ebelow, eabove = slice(0, SIDE), slice(SIDE + rows, 2 * SIDE + rows)
    every = slice(None)
    absent(hi_w, (nodes, (nel, slice(0, nel))))
    absent(hi_n, (side_in, every), (extra, 1))
    absent(hi_w & hi_n, (corner_in, every), (extra, (1, eabove)))
    absent(lo_w & hi_n, (extra, (1, ebelow)))
    absent(lo_w, (from_w, every))
    absent(lo_n, (from_n, every), (extra, 0))
    absent(lo_w & lo_n, (from_c, every), (extra, (0, ebelow)))
    absent(hi_w & lo_n, (extra, (0, eabove)))
    pl.semaphore_wait(barrier, count)

    everything = []

    def remote(goes, comes, src, dst, device):
        k = len(everything)
        copy = pltpu.make_async_remote_copy(
            src_ref=src, dst_ref=dst, send_sem=send.at[k], recv_sem=recv.at[k],
            device_id=device, device_id_type=MESH)
        everything.append((goes, comes, copy))
        return k

    def go(*ks):
        for k in ks:
            @pl.when(everything[k][0])
            def _(k=k):
                everything[k][2].start()

    def come(*ks):
        for k in ks:
            @pl.when(everything[k][1])
            def _(k=k):
                everything[k][2].wait_recv()

    below, above = slice(0, rim), slice(rim + rows, total)
    edge_x = remote(lo_w, hi_w, nodes.at[0, 0:nel], nodes.at[nel, 0:nel], dn_w)
    edge_y = remote(lo_n, hi_n, column, side_in, dn_n)
    strips = []
    full = (slice(0, rim), slice(rows - rim, rows), slice(rim, rows - rim))
    for part in full:
        there = slice(part.start + rim, part.stop + rim)
        strips.append((
            remote(hi_n, lo_n, own.at[part, cols - side:cols], ext.at[there, ylo], up_n),
            remote(lo_n, hi_n, own.at[part, 0:side], ext.at[there, yhi], dn_n)))
    cut = cols // 2 if detour else cols
    near, far = slice(0, cut), slice(cut, cols)
    enear, efar = slice(side, side + cut), slice(side + cut, side + cols)
    high_own, low_own = slice(rows - rim, rows), slice(0, rim)
    bands = [
        remote(hi_w, lo_w, own.at[high_own, near], ext.at[below, enear], up_w),
        remote(lo_w, hi_w, own.at[low_own, near], ext.at[above, enear], dn_w)]
    first_hop, second_hop = [], []
    if detour:
        bands += [
            remote(hi_w & (w != 3), lo_w & (w != 4), own.at[high_own, far], ext.at[below, efar], up_w),
            remote(lo_w & (w != 4), hi_w & (w != 3), own.at[low_own, far], ext.at[above, efar], dn_w)]
        first_hop = [
            remote(is3, is7, own.at[high_own, far], passed, (7, n)),
            remote(is4, is0, own.at[low_own, far], passed, (0, n))]
        second_hop = [
            remote(is7, is4, passed, ext.at[below, efar], (4, n)),
            remote(is0, is3, passed, ext.at[above, efar], (3, n))]
    go(*strips[0], *strips[1], *first_hop, *bands)
    cube[...] = jnp.zeros_like(cube)
    nodal.wait()
    cube[:, :, :, 0:ns] = disp[...]
    for i in range(nel):
        value = cube[0, i]
        for c in range(1, comps):
            value = value + pltpu.roll(cube[c, i], ns * c, 1)
        nodes[i, 0:nel] = value
        column[i:i + 1] = value[0:1]
    go(edge_x, edge_y)

    def widen(first, count, columns, together):
        to = slice(columns.start + 8, columns.stop + 8)

        @pl.loop(0, count // together)
        def _(b):
            for a in range(together):
                win[first + together * b + a, to] = ext[first + together * b + a, columns].astype(F32)
        for r in range(first + count // together * together, first + count):
            win[r, to] = ext[r, columns].astype(F32)

    local.wait()
    widen(rim, rows, mid, 2)
    build_tables(ns, inter, proj, up, down, down2, square, gather, dz)
    absent(lo_n, (ext, (every, ylo)))
    absent(hi_n, (ext, (every, yhi)))
    absent(lo_w, (ext, below))
    absent(hi_w, (ext, above))
    come(edge_x)
    edge_c = remote(hi_w & lo_n, hi_w & hi_n, nodes.at[nel, 0:8], corner_in, dn_n)
    go(edge_c)
    come(edge_y)
    top = lax.broadcasted_iota(jnp.int32, (QPAD - nel, 128), 0) == 0
    for i in range(nel):
        nodes[i, nel:QPAD] = jnp.where(top, jnp.broadcast_to(side_in[i:i + 1], (QPAD - nel, 128)), 0.0)
    come(edge_c)
    nodes[nel, nel:QPAD] = jnp.where(top, jnp.broadcast_to(corner_in[0:1], (QPAD - nel, 128)), 0.0)
    come(*first_hop)
    go(*second_hop)
    corners = []
    come(*strips[0], *strips[1])
    gap_up, gap_dn = (w == 3, w == 4) if detour else (w < 0, w < 0)
    keep_up, keep_dn = hi_w & jnp.logical_not(gap_up), lo_w & jnp.logical_not(gap_dn)
    corners += [
        remote(keep_up & lo_n, keep_dn & lo_n, ext.at[rows:rows + rim, ylo], ext.at[below, ylo], up_w),
        remote(keep_up & hi_n, keep_dn & hi_n, ext.at[rows:rows + rim, yhi], ext.at[below, yhi], up_w),
        remote(keep_dn & lo_n, keep_up & lo_n, ext.at[rim:2 * rim, ylo], ext.at[above, ylo], dn_w),
        remote(keep_dn & hi_n, keep_up & hi_n, ext.at[rim:2 * rim, yhi], ext.at[above, yhi], dn_w)]
    go(*corners)
    for k in strips[0] + strips[1]:
        @pl.when(everything[k][0])
        def _(k=k):
            everything[k][2].wait_send()
    go(*strips[2])

    picks = (side + cols - rim, side + rim - 1)

    @pl.loop(0, rows // 8)
    def _(b):
        for a in range(8):
            for i, col in enumerate(picks):
                tile = ext[rim + 8 * b + a, col // 16 * 16:col // 16 * 16 + 16, :].astype(F32)
                colf[i, pl.ds(8 * b + a, 1), :] = tile[col % 16:col % 16 + 1]
    colb[...] = colf[...].astype(BF16)
    thin = [remote(hi_n, lo_n, colb.at[0], extra.at[0, emid], up_n),
            remote(lo_n, hi_n, colb.at[1], extra.at[1, emid], dn_n)]
    go(*thin)

    flat = nodes[...].reshape(-1, 128)
    high = flat.astype(BF16).astype(F32)
    both = jnp.concatenate([high, flat - high], axis=1).astype(BF16)
    level = jnp.dot(both, up[...], preferred_element_type=F32)
    for i in range(nel + 1):
        head, tail = split(level[i * QPAD:(i + 1) * QPAD])
        field[i] = jnp.dot(inter[...], jnp.concatenate([head, tail], axis=0), preferred_element_type=F32)
    for ref in (gsum, qbuf, dacc):
        ref[...] = jnp.zeros_like(ref)
    offsets.wait()
    slab.wait()
    steps, chunks = rows // 8, cols // 16
    start = map_ref[0] + side
    col0 = map_ref[1] + 8 + side

    def fold(u, t):
        got = jnp.dot(square[...], qbuf[u], preferred_element_type=F32)
        dpart[t] = got[0:16] + got[16:32]

    def slopes(p, j):
        row0 = start + 8 * p + 1
        at = col0 + 16 * j
        here = jnp.concatenate([win[row0 + k, pl.ds(at, 16), :].astype(BF16) for k in range(8)], axis=0)
        return jnp.dot(here, dz[...], preferred_element_type=F32)

    def phase(pairs, place, before):
        for u in range(2):
            zbuf[u] = slopes(*place(0, u))

        @pl.loop(0, pairs)
        def _(b):
            coming = [slopes(*place(jnp.minimum(b + 1, pairs - 1), u)) for u in range(2)]
            for u in range(2):
                last = place(jnp.maximum(b - 1, 0), u)
                fold(u, jnp.where(b == 0, before[u][0] * chunks + before[u][1], last[0] * chunks + last[1]))
            for u in range(2):
                p, j = place(b, u)
                at = 16 * j if isinstance(j, int) else pl.multiple_of(16 * j, 16)
                base = 8 * p
                row0 = start + base
                refs = [res[base + k, pl.ds(at, 16), :].astype(F32) for k in range(8)]
                out_rows, squares, parts = voxels(
                    lambda k, shift, half: win[row0 + k, pl.ds(col0 + at + (8 * half + shift), 8), :],
                    lambda k, half: zbuf[u, 16 * k + 8 * half:16 * k + 8 * half + 8, :],
                    lambda k, half: refs[k][8 * half:8 * half + 8],
                    lambda c, half: field[p, pl.ds(at + 8 * half, 8), c * layers:(c + 1) * layers],
                    lambda c, half: field[p + 1, pl.ds(at + 8 * half, 8), c * layers:(c + 1) * layers])
                for k in range(8):
                    res[base + k, pl.ds(at, 16), :] = out_rows[k]
                for c in range(comps):
                    lanes = slice(c * layers, (c + 1) * layers)
                    for k in range(8):
                        qbuf[u, 16 * k:16 * k + 16, lanes] = squares[k][c]
                    for i in range(2):
                        gsum[p + i, pl.ds(at, 16), lanes] = gsum[p + i, pl.ds(at, 16), lanes] + parts[c][i]
            for u in range(2):
                zbuf[u] = coming[u]
        return [place(pairs - 1, u) for u in range(2)]

    p_in = (rim + 7) // 8
    n_in = steps - 2 * p_in
    j_in = (rim + 15) // 16
    other = (chunks - 2) // 2

    def inner_rows(i):
        return p_in + i

    def outer_rows(i):
        return i + n_in * as_int(jnp.asarray(i) >= p_in) if not isinstance(i, int) else i + n_in * (i >= p_in)

    def outer_chunk(i, u):
        m = 2 * i + u
        return m + 2 * (m >= j_in) if isinstance(m, int) else m + 2 * as_int(m >= j_in)

    def by_row(rows_of):
        return lambda b, u: (rows_of(b), j_in + u)

    def by_rest(rows_of):
        def place(b, u):
            if isinstance(b, int):
                return rows_of(b // other), outer_chunk(b % other, u)
            return rows_of(lax.div(b, other)), outer_chunk(lax.rem(b, other), u)
        return place

    done = [by_row(inner_rows)(0, u) for u in range(2)]
    done = phase(n_in, by_row(inner_rows), done)
    strain_pull(ns, nodes, pull)
    for part in full[:2]:
        widen(part.start + rim, rim, ylo, 4)
        widen(part.start + rim, rim, yhi, 4)
    come(*thin)
    thin_corners = [
        remote(lo_n & lo_w, lo_n & hi_w, extra.at[0, elow], extra.at[0, eabove], dn_w),
        remote(lo_n & hi_w, lo_n & lo_w, extra.at[0, ehigh], extra.at[0, ebelow], up_w),
        remote(hi_n & lo_w, hi_n & hi_w, extra.at[1, elow], extra.at[1, eabove], dn_w),
        remote(hi_n & hi_w, hi_n & lo_w, extra.at[1, ehigh], extra.at[1, ebelow], up_w)]
    go(*thin_corners)
    spots = (7, 8 + cols + 2 * side)

    def rims(span, source, first, count):
        rimcol[:, span] = extra[:, span].astype(F32)
        for r in range(count % 4):
            for i, spot in enumerate(spots):
                win[first + r, spot:spot + 1] = rimcol[i, source + r:source + r + 1]

        @pl.loop(0, count // 4)
        def _(b):
            for a in range(4):
                r = count % 4 + 4 * b + a
                for i, spot in enumerate(spots):
                    win[first + r, spot:spot + 1] = rimcol[i, pl.ds(source + r, 1), :]

    come(*bands, *second_hop)
    if detour:
        follow = []
        for here, band in ((gap_dn, below), (gap_up, above)):
            follow += [
                remote(here & hi_n, here & lo_n, ext.at[band, cols:cols + side], ext.at[band, ylo], up_n),
                remote(here & lo_n, here & hi_n, ext.at[band, side:2 * side], ext.at[band, yhi], dn_n)]
        go(*follow)
        corners += follow
    widen(0, rim, mid, 2)
    widen(rim + rows, rim, mid, 2)
    done = phase(2 * p_in, by_row(outer_rows), done)
    rims(emid, SIDE, rim, rows)
    come(*strips[2])
    widen(2 * rim, rows - 2 * rim, ylo, 4)
    widen(2 * rim, rows - 2 * rim, yhi, 4)
    done = phase(n_in * other, by_rest(inner_rows), done)
    come(*corners, *thin_corners)
    for first in (0, rim + rows):
        widen(first, rim, ylo, 4)
        widen(first, rim, yhi, 4)
    rims(slice(0, SIDE), SIDE - rim, 0, rim)
    rims(slice(SIDE + rows, 2 * SIDE + rows), SIDE + rows, rim + rows, rim)
    done = phase(2 * p_in * other, by_rest(outer_rows), done)
    for u in range(2):
        fold(u, done[u][0] * chunks + done[u][1])
    for i in range(steps + 1):
        head, tail = split(gsum[i])
        gacc[i] = jnp.dot(proj[...], jnp.concatenate([head, tail], axis=0), preferred_element_type=F32)
    for i in range(steps):
        head, tail = split(dpart[i * chunks:(i + 1) * chunks].reshape(cols, comps * layers))
        got = jnp.dot(gather[...], jnp.concatenate([head, tail], axis=0), preferred_element_type=F32)
        dacc[i] = dacc[i] + got[0:QPAD]
        dacc[i + 1] = got[QPAD:2 * QPAD]
    for k, (acc, table) in enumerate(((gacc, down), (dacc, down2))):
        head, tail = split(acc[...].reshape(-1, comps * layers))
        got = (jnp.dot(head, table[...], preferred_element_type=F32)
               + jnp.dot(tail, table[...], preferred_element_type=F32)).reshape(pull.shape)
        terms[k] = got + pull[...] if k == 0 else got

    for k in range(2):
        for p in range(nel):
            colf[k, p:p + 1] = terms[k, p, nel:nel + 1]
    to_w = remote(hi_w, lo_w, terms.at[:, nel], from_w, up_w)
    to_n = remote(hi_n, lo_n, colf.at[:, 0:nel], from_n, up_n)
    to_c = remote(lo_w & hi_n, lo_w & lo_n, from_w.at[:, nel:QPAD], from_c, up_n)
    go(to_w, to_n)
    come(to_w)
    go(to_c)
    come(to_n, to_c)
    first_row = lax.broadcasted_iota(jnp.int32, (nel, 128), 0) == 0
    for p in range(nel):
        both = []
        for k in range(2):
            value = terms[k, p, 0:nel]
            beside = from_n[k, p:p + 1]
            if p == 0:
                value = value + from_w[k, 0:nel]
                beside = beside + from_c[k, 0:1]
            both.append(value + jnp.where(first_row, jnp.broadcast_to(beside, (nel, 128)), 0.0))
        step = both[0] / (both[1] + STIFFNESS)
        for c in range(comps):
            here = step if c == 0 else pltpu.roll(step, 128 - ns * c, 1)
            change[c, p] = here[:, 0:ns]
    sent = strips[0] + strips[1]
    for k, (goes, _c, copy) in enumerate(everything):
        if k not in sent:
            @pl.when(goes)
            def _(copy=copy):
                copy.wait_send()


def emit_kernel(parts, kept, change, disp, residual, updated, fresh, sem):
    rows = kept.shape[0] // parts
    copies = [pltpu.make_async_copy(kept.at[k * rows:(k + 1) * rows], residual.at[k * rows:(k + 1) * rows], sem.at[k])
              for k in range(parts)]
    for copy in copies:
        copy.start()
    fresh[...] = disp[...] - change[...]
    last = pltpu.make_async_copy(fresh, updated, sem.at[parts])
    last.start()
    for copy in copies + [last]:
        copy.wait()


def emit(kept, change, nodal):
    anywhere = pl.BlockSpec(memory_space=pl.ANY)
    near = pl.BlockSpec(memory_space=pltpu.VMEM)
    parts = 8
    return pl.pallas_call(
        functools.partial(emit_kernel, parts),
        out_shape=[jax.ShapeDtypeStruct(kept.shape, BF16), jax.ShapeDtypeStruct(nodal.shape, F32)],
        in_specs=[anywhere, near, near],
        out_specs=[anywhere, anywhere],
        scratch_shapes=[pltpu.VMEM(nodal.shape, F32), pltpu.SemaphoreType.DMA((parts + 1,))],
        compiler_params=pltpu.CompilerParams(vmem_limit_bytes=8 << 20),
        name="emit",
    )(kept, change, nodal)


def per_device(nw, nn, reference_image, deformed_image, displacement, tile_map):
    comps, ns, nel, _ = displacement.shape
    rows, cols, layers = reference_image.shape
    nodal = displacement.transpose(0, 2, 3, 1)
    rim = rows // 4 + 1
    npx, lanes = nel + 1, comps * layers
    total, across = rows + 2 * rim, cols + 2 * (rim - 1)
    anywhere = pl.BlockSpec(memory_space=pl.ANY)
    near = pl.BlockSpec(memory_space=pltpu.VMEM)
    kept, change = pl.pallas_call(
        functools.partial(step_kernel, nw, nn, rim, ns),
        out_shape=[jax.ShapeDtypeStruct(reference_image.shape, BF16),
                   jax.ShapeDtypeStruct(nodal.shape, F32)],
        in_specs=[anywhere] * 4,
        out_specs=[near, near],
        scratch_shapes=[
            pltpu.VMEM((cols, 2 * QPAD), BF16),
            pltpu.VMEM((QPAD, 2 * cols), BF16),
            pltpu.VMEM((2 * 128, lanes), BF16),
            pltpu.VMEM((lanes, 128), BF16),
            pltpu.VMEM((lanes, 128), BF16),
            pltpu.VMEM((32, 8 * 16), BF16),
            pltpu.VMEM((2 * QPAD, 2 * cols), BF16),
            pltpu.VMEM((layers, layers), BF16),
            pltpu.VMEM((total, across, layers), BF16),
            pltpu.VMEM((rim, cols - cols // 2, layers), BF16),
            pltpu.VMEM((total, across + 16, layers), F32),
            pltpu.VMEM((npx, cols, lanes), F32),
            pltpu.VMEM((npx, cols, lanes), F32),
            pltpu.VMEM((2, 8 * 16, lanes), BF16),
            pltpu.VMEM((2, 8 * 16, layers), F32),
            pltpu.VMEM((rows // 8 * (cols // 16), 16, lanes), F32),
            pltpu.VMEM((npx, QPAD, lanes), F32),
            pltpu.VMEM((npx, QPAD, lanes), F32),
            pltpu.VMEM((2, npx, QPAD, 128), F32),
            pltpu.VMEM((2, rows + 2 * SIDE, layers), BF16),
            pltpu.VMEM((2, rows + 2 * SIDE, layers), F32),
            pltpu.VMEM((npx, QPAD, 128), F32),
            pltpu.VMEM((npx, QPAD, 128), F32),
            pltpu.VMEM((comps, nel, nel, 128), F32),
            pltpu.VMEM((nel, 128), F32),
            pltpu.VMEM((nel, 128), F32),
            pltpu.VMEM((8, 128), F32),
            pltpu.VMEM((2, rows, layers), F32),
            pltpu.VMEM((2, rows, layers), BF16),
            pltpu.VMEM((2, QPAD, 128), F32),
            pltpu.VMEM((2, nel, 128), F32),
            pltpu.VMEM((2, QPAD - nel, 128), F32),
            pltpu.VMEM(nodal.shape, F32),
            pltpu.SMEM((2,), jnp.int32),
            pltpu.SemaphoreType.DMA((34,)),
            pltpu.SemaphoreType.DMA((34,)),
            pltpu.SemaphoreType.DMA((4,)),
        ],
        compiler_params=pltpu.CompilerParams(
            collective_id=0, has_side_effects=True, vmem_limit_bytes=48 << 20),
        name="step",
    )(tile_map.reshape(2), deformed_image, reference_image, nodal)
    residual, updated = emit(kept, change, nodal)
    return (updated.transpose(0, 3, 1, 2), residual)


def solution(mesh):
    placed = (
        P("wide", "narrow", None),
        P("wide", "narrow", None),
        P(None, None, "wide", "narrow"),
        P("wide", "narrow", None),
    )
    return jax.shard_map(
        functools.partial(per_device, mesh.shape["wide"], mesh.shape["narrow"]),
        mesh=mesh,
        in_specs=placed,
        out_specs=(P(None, None, "wide", "narrow"), P("wide", "narrow", None)),
        check_vma=False,
    )
```

```python
import functools

import jax
import jax.numpy as jnp
from jax import lax
from jax.experimental import pallas as pl
from jax.experimental.pallas import tpu as pltpu
from jax.sharding import PartitionSpec as P

MU_SHEAR = 1.0
LAMBDA_BULK = 2.0
REG_WEIGHT = 256.0
STIFFNESS = 16.0
MESH = pl.DeviceIdType.MESH
F32 = jnp.float32
BF16 = jnp.bfloat16
SIDE = 48
QPAD = 24


def as_int(flag):
    return flag.astype(jnp.int32)


def hat(place, node):
    at = (place.astype(F32) + 0.5) * 0.125
    return jnp.maximum(1.0 - jnp.abs(at - node.astype(F32)), 0.0)


def build_tables(ns, inter, proj, up, down, down2, square, gather, dz):
    def grid(ref):
        return (lax.broadcasted_iota(jnp.int32, ref.shape, 0), lax.broadcasted_iota(jnp.int32, ref.shape, 1))

    cols = inter.shape[0]
    r, c = grid(inter)
    inter[...] = (0.5 * hat(r, jnp.where(c < QPAD, c, c - QPAD))).astype(BF16)
    r, c = grid(proj)
    proj[...] = hat(jnp.where(c < cols, c, c - cols), r).astype(BF16)
    r, c = grid(up)
    up[...] = hat(c % 128, r % 128 - ns * (c // 128)).astype(BF16)
    r, c = grid(down)
    layer = hat(r % 128, c - ns * (r // 128))
    down[...] = (-0.5 * layer).astype(BF16)
    down2[...] = (0.25 * layer * layer).astype(BF16)
    r, c = grid(square)
    along = (c // 16).astype(F32) * 0.125 + 0.0625
    along = jnp.where(r % 16 < 8, 1.0 - along, along)
    across = hat(c % 16, r % 8)
    whole = (along * along) * (across * across)
    head = whole.astype(BF16).astype(F32)
    square[...] = jnp.where(r < 16, head, whole - head).astype(BF16)
    r, c = grid(dz)
    dz[...] = (jnp.where(r == c + 1, 1.0, 0.0) - jnp.where(r == c - 1, 1.0, 0.0)).astype(BF16)
    r, c = grid(gather)
    low = r < QPAD
    node = jnp.where(low, r, r - QPAD)
    k = c % 128
    same = (node == 2 * (k // 16) + k % 8) & (k % 8 < 3) & (low == (k % 16 < 8))
    gather[...] = jnp.where(same, 1.0, 0.0).astype(BF16)


def split(value):
    high = value.astype(BF16)
    return high, (value - high.astype(F32)).astype(BF16)


def strain_pull(ns, nodes, pull):
    npx = nodes.shape[0]
    nel = npx - 1
    lane = lax.broadcasted_iota(jnp.int32, (nel, 128), 1)
    move = lambda a, by: pltpu.roll(a, by % 128, 1)
    pull[...] = jnp.zeros_like(pull)

    @pl.loop(0, nel)
    def _(p):
        a00, a01 = nodes[p, 0:nel], nodes[p, 1:nel + 1]
        a10, a11 = nodes[p + 1, 0:nel], nodes[p + 1, 1:nel + 1]
        dx = (a10 - a00) + (a11 - a01)
        dy = (a01 - a00) + (a11 - a10)
        every = (a00 + a01) + (a10 + a11)
        slopes = (dx + move(dx, -1), dy + move(dy, -1), move(every, -1) - every)
        f = [[0.03125 * (move(h, -ns * i) if i else h) + (1.0 if i == j else 0.0)
              for j, h in enumerate(slopes)] for i in range(3)]
        cof = [[f[(i + 1) % 3][(j + 1) % 3] * f[(i + 2) % 3][(j + 2) % 3]
                - f[(i + 1) % 3][(j + 2) % 3] * f[(i + 2) % 3][(j + 1) % 3]
                for j in range(3)] for i in range(3)]
        ratio = f[0][0] * cof[0][0] + f[0][1] * cof[0][1] + f[0][2] * cof[0][2]
        factor = (LAMBDA_BULK * jnp.log(ratio) - MU_SHEAR) / ratio
        back = []
        for j in range(3):
            parts = [jnp.where(lane < ns - 1, MU_SHEAR * f[i][j] + factor * cof[i][j], 0.0) for i in range(3)]
            back.append((parts[0] + move(parts[1], ns) + move(parts[2], 2 * ns)) * (0.03125 * REG_WEIGHT))
        gx = back[0] + move(back[0], 1)
        gy = back[1] + move(back[1], 1)
        gz = move(back[2], 1) - back[2]
        for dp, dq in ((0, 0), (0, 1), (1, 0), (1, 1)):
            add = (gx if dp else -gx) + (gy if dq else -gy) + gz
            pull[p + dp, dq:dq + nel] = pull[p + dp, dq:dq + nel] + add


def voxels(window, slope_z, ref_rows, left, right):
    back = []
    rows, squares = [None] * 8, [[None] * 3 for _ in range(8)]
    join = lambda a, b: jnp.concatenate([a, b], axis=0)
    for half in range(2):
        run, tot = [None] * 3, [None] * 3
        inc = [(right(c, half) - left(c, half)) * 0.125 for c in range(3)]
        mv = [left(c, half) + 0.5 * inc[c] for c in range(3)]
        prev, cur = window(0, 0, half), window(1, 0, half)
        for k in range(8):
            nxt = window(k + 2, 0, half)
            g = [nxt - prev,
                 window(k + 1, 1, half) - window(k + 1, -1, half),
                 slope_z(k, half)]
            r = ref_rows(k, half) - cur
            for c in range(3):
                r = r - g[c] * mv[c]
                if k < 7:
                    mv[c] = mv[c] + inc[c]
            rows[k] = r if half == 0 else join(rows[k], r).astype(BF16)
            for c in range(3):
                f = g[c] * r
                q = g[c] * g[c]
                run[c] = f if k == 0 else run[c] + f
                tot[c] = run[c] if k == 0 else tot[c] + run[c]
                squares[k][c] = q if half == 0 else join(squares[k][c], q).astype(BF16)
            prev, cur = cur, nxt
        part = []
        for c in range(3):
            low = (tot[c] - 0.5 * run[c]) * 0.125
            part.append((low, run[c] - low))
        back.append(part)
    return rows, squares, [[join(back[0][c][i], back[1][c][i]) for i in range(2)] for c in range(3)]


def step_kernel(nw, nn, rim, ns, map_hbm, own, ref_hbm, disp_hbm,
                res, change,
                inter, proj, up, down, down2, square, gather, dz,
                ext, passed, win, field, gsum, qbuf, zbuf, dpart, gacc, dacc, terms,
                extra, rimcol, nodes, pull, cube, column, side_in, corner_in, colf, colb,
                from_w, from_n, from_c, disp, map_ref, send, recv, lsem):
    rows, cols, layers = own.shape
    comps, nel = disp.shape[0], disp.shape[1]
    side = rim - 1
    w = lax.axis_index("wide")
    n = lax.axis_index("narrow")
    lo_w, hi_w, lo_n, hi_n = w > 0, w < nw - 1, n > 0, n < nn - 1
    up_w, dn_w = (w + 1, n), (w - 1, n)
    up_n, dn_n = (w, n + 1), (w, n - 1)
    mid = slice(side, side + cols)
    ylo = slice(0, side)
    yhi = slice(side + cols, 2 * side + cols)
    total = rows + 2 * rim
    emid = slice(SIDE, SIDE + rows)
    detour = nw == 8
    is0, is3, is4, is7 = (w == 0), (w == 3), (w == 4), (w == 7)

    barrier = pltpu.get_barrier_semaphore()
    greet = [(lo_w, dn_w), (hi_w, up_w), (lo_n, dn_n), (hi_n, up_n)]
    if detour:
        greet += [(is7, (3, n)), (is4, (7, n)), (is0, (4, n)), (is3, (0, n))]
    count = as_int(lo_w) + as_int(hi_w) + as_int(lo_n) + as_int(hi_n)
    if detour:
        count = count + as_int(is0 | is3 | is4 | is7)
    for there, device in greet:
        @pl.when(there)
        def _(device=device):
            pl.semaphore_signal(barrier, inc=1, device_id=device, device_id_type=MESH)
    loads = [pltpu.make_async_copy(disp_hbm, disp, lsem.at[2]),
             pltpu.make_async_copy(own, ext.at[rim:rim + rows, mid], lsem.at[0]),
             pltpu.make_async_copy(ref_hbm, res, lsem.at[1]),
             pltpu.make_async_copy(map_hbm, map_ref, lsem.at[3])]
    for load in loads:
        load.start()
    nodal, local, slab, offsets = loads

    def absent(there, *spans):
        @pl.when(jnp.logical_not(there))
        def _():
            for ref, span in spans:
                ref[span] = jnp.zeros(ref.at[span].shape, ref.dtype)

    elow, ehigh = slice(SIDE, 2 * SIDE), slice(rows, SIDE + rows)
    ebelow, eabove = slice(0, SIDE), slice(SIDE + rows, 2 * SIDE + rows)
    every = slice(None)
    absent(hi_w, (nodes, (nel, slice(0, nel))))
    absent(hi_n, (side_in, every), (extra, 1))
    absent(hi_w & hi_n, (corner_in, every), (extra, (1, eabove)))
    absent(lo_w & hi_n, (extra, (1, ebelow)))
    absent(lo_w, (from_w, every))
    absent(lo_n, (from_n, every), (extra, 0))
    absent(lo_w & lo_n, (from_c, every), (extra, (0, ebelow)))
    absent(hi_w & lo_n, (extra, (0, eabove)))
    pl.semaphore_wait(barrier, count)

    everything = []

    def remote(goes, comes, src, dst, device):
        k = len(everything)
        copy = pltpu.make_async_remote_copy(
            src_ref=src, dst_ref=dst, send_sem=send.at[k], recv_sem=recv.at[k],
            device_id=device, device_id_type=MESH)
        everything.append((goes, comes, copy))
        return k

    def go(*ks):
        for k in ks:
            @pl.when(everything[k][0])
            def _(k=k):
                everything[k][2].start()

    def come(*ks):
        for k in ks:
            @pl.when(everything[k][1])
            def _(k=k):
                everything[k][2].wait_recv()

    below, above = slice(0, rim), slice(rim + rows, total)
    edge_x = remote(lo_w, hi_w, nodes.at[0, 0:nel], nodes.at[nel, 0:nel], dn_w)
    edge_y = remote(lo_n, hi_n, column, side_in, dn_n)
    strips = []
    full = (slice(0, rim), slice(rows - rim, rows), slice(rim, rows - rim))
    for part in full:
        there = slice(part.start + rim, part.stop + rim)
        strips.append((
            remote(hi_n, lo_n, own.at[part, cols - side:cols], ext.at[there, ylo], up_n),
            remote(lo_n, hi_n, own.at[part, 0:side], ext.at[there, yhi], dn_n)))
    cut = cols // 2 if detour else cols
    near, far = slice(0, cut), slice(cut, cols)
    enear, efar = slice(side, side + cut), slice(side + cut, side + cols)
    high_own, low_own = slice(rows - rim, rows), slice(0, rim)
    bands = [
        remote(hi_w, lo_w, own.at[high_own, near], ext.at[below, enear], up_w),
        remote(lo_w, hi_w, own.at[low_own, near], ext.at[above, enear], dn_w)]
    first_hop, second_hop = [], []
    if detour:
        bands += [
            remote(hi_w & (w != 3), lo_w & (w != 4), own.at[high_own, far], ext.at[below, efar], up_w),
            remote(lo_w & (w != 4), hi_w & (w != 3), own.at[low_own, far], ext.at[above, efar], dn_w)]
        first_hop = [
            remote(is3, is7, own.at[high_own, far], passed, (7, n)),
            remote(is4, is0, own.at[low_own, far], passed, (0, n))]
        second_hop = [
            remote(is7, is4, passed, ext.at[below, efar], (4, n)),
            remote(is0, is3, passed, ext.at[above, efar], (3, n))]
    go(*strips[0], *strips[1], *first_hop, *bands)
    cube[...] = jnp.zeros_like(cube)
    nodal.wait()
    cube[:, :, :, 0:ns] = disp[...]
    for i in range(nel):
        value = cube[0, i]
        for c in range(1, comps):
            value = value + pltpu.roll(cube[c, i], ns * c, 1)
        nodes[i, 0:nel] = value
        column[i:i + 1] = value[0:1]
    go(edge_x, edge_y)

    def widen(first, count, columns, together):
        to = slice(columns.start + 8, columns.stop + 8)

        @pl.loop(0, count // together)
        def _(b):
            for a in range(together):
                win[first + together * b + a, to] = ext[first + together * b + a, columns].astype(F32)
        for r in range(first + count // together * together, first + count):
            win[r, to] = ext[r, columns].astype(F32)

    local.wait()
    widen(rim, rows, mid, 2)
    build_tables(ns, inter, proj, up, down, down2, square, gather, dz)
    absent(lo_n, (ext, (every, ylo)))
    absent(hi_n, (ext, (every, yhi)))
    absent(lo_w, (ext, below))
    absent(hi_w, (ext, above))
    come(edge_x)
    edge_c = remote(hi_w & lo_n, hi_w & hi_n, nodes.at[nel, 0:8], corner_in, dn_n)
    go(edge_c)
    come(edge_y)
    top = lax.broadcasted_iota(jnp.int32, (QPAD - nel, 128), 0) == 0
    for i in range(nel):
        nodes[i, nel:QPAD] = jnp.where(top, jnp.broadcast_to(side_in[i:i + 1], (QPAD - nel, 128)), 0.0)
    come(edge_c)
    nodes[nel, nel:QPAD] = jnp.where(top, jnp.broadcast_to(corner_in[0:1], (QPAD - nel, 128)), 0.0)
    come(*first_hop)
    go(*second_hop)
    corners = []
    come(*strips[0], *strips[1])
    gap_up, gap_dn = (w == 3, w == 4) if detour else (w < 0, w < 0)
    keep_up, keep_dn = hi_w & jnp.logical_not(gap_up), lo_w & jnp.logical_not(gap_dn)
    corners += [
        remote(keep_up & lo_n, keep_dn & lo_n, ext.at[rows:rows + rim, ylo], ext.at[below, ylo], up_w),
        remote(keep_up & hi_n, keep_dn & hi_n, ext.at[rows:rows + rim, yhi], ext.at[below, yhi], up_w),
        remote(keep_dn & lo_n, keep_up & lo_n, ext.at[rim:2 * rim, ylo], ext.at[above, ylo], dn_w),
        remote(keep_dn & hi_n, keep_up & hi_n, ext.at[rim:2 * rim, yhi], ext.at[above, yhi], dn_w)]
    go(*corners)
    for k in strips[0] + strips[1]:
        @pl.when(everything[k][0])
        def _(k=k):
            everything[k][2].wait_send()
    go(*strips[2])

    picks = (side + cols - rim, side + rim - 1)

    @pl.loop(0, rows // 8)
    def _(b):
        for a in range(8):
            for i, col in enumerate(picks):
                tile = ext[rim + 8 * b + a, col // 16 * 16:col // 16 * 16 + 16, :].astype(F32)
                colf[i, pl.ds(8 * b + a, 1), :] = tile[col % 16:col % 16 + 1]
    colb[...] = colf[...].astype(BF16)
    thin = [remote(hi_n, lo_n, colb.at[0], extra.at[0, emid], up_n),
            remote(lo_n, hi_n, colb.at[1], extra.at[1, emid], dn_n)]
    go(*thin)

    flat = nodes[...].reshape(-1, 128)
    high = flat.astype(BF16).astype(F32)
    both = jnp.concatenate([high, flat - high], axis=1).astype(BF16)
    level = jnp.dot(both, up[...], preferred_element_type=F32)
    for i in range(nel + 1):
        head, tail = split(level[i * QPAD:(i + 1) * QPAD])
        field[i] = jnp.dot(inter[...], jnp.concatenate([head, tail], axis=0), preferred_element_type=F32)
    for ref in (gsum, qbuf, dacc):
        ref[...] = jnp.zeros_like(ref)
    offsets.wait()
    slab.wait()
    steps, chunks = rows // 8, cols // 16
    start = map_ref[0] + side
    col0 = map_ref[1] + 8 + side

    def fold(u, t):
        got = jnp.dot(square[...], qbuf[u], preferred_element_type=F32)
        dpart[t] = got[0:16] + got[16:32]

    def slopes(p, j):
        row0 = start + 8 * p + 1
        at = col0 + 16 * j
        here = jnp.concatenate([win[row0 + k, pl.ds(at, 16), :].astype(BF16) for k in range(8)], axis=0)
        return jnp.dot(here, dz[...], preferred_element_type=F32)

    def phase(pairs, place, before):
        for u in range(2):
            zbuf[u] = slopes(*place(0, u))

        @pl.loop(0, pairs)
        def _(b):
            coming = [slopes(*place(jnp.minimum(b + 1, pairs - 1), u)) for u in range(2)]
            for u in range(2):
                last = place(jnp.maximum(b - 1, 0), u)
                fold(u, jnp.where(b == 0, before[u][0] * chunks + before[u][1], last[0] * chunks + last[1]))
            for u in range(2):
                p, j = place(b, u)
                at = 16 * j if isinstance(j, int) else pl.multiple_of(16 * j, 16)
                base = 8 * p
                row0 = start + base
                refs = [res[base + k, pl.ds(at, 16), :].astype(F32) for k in range(8)]
                out_rows, squares, parts = voxels(
                    lambda k, shift, half: win[row0 + k, pl.ds(col0 + at + (8 * half + shift), 8), :],
                    lambda k, half: zbuf[u, 16 * k + 8 * half:16 * k + 8 * half + 8, :],
                    lambda k, half: refs[k][8 * half:8 * half + 8],
                    lambda c, half: field[p, pl.ds(at + 8 * half, 8), c * layers:(c + 1) * layers],
                    lambda c, half: field[p + 1, pl.ds(at + 8 * half, 8), c * layers:(c + 1) * layers])
                for k in range(8):
                    res[base + k, pl.ds(at, 16), :] = out_rows[k]
                for c in range(comps):
                    lanes = slice(c * layers, (c + 1) * layers)
                    for k in range(8):
                        qbuf[u, 16 * k:16 * k + 16, lanes] = squares[k][c]
                    for i in range(2):
                        gsum[p + i, pl.ds(at, 16), lanes] = gsum[p + i, pl.ds(at, 16), lanes] + parts[c][i]
            for u in range(2):
                zbuf[u] = coming[u]
        return [place(pairs - 1, u) for u in range(2)]

    p_in = (rim + 7) // 8
    n_in = steps - 2 * p_in
    j_in = (rim + 15) // 16
    other = (chunks - 2) // 2

    def inner_rows(i):
        return p_in + i

    def outer_rows(i):
        return i + n_in * as_int(jnp.asarray(i) >= p_in) if not isinstance(i, int) else i + n_in * (i >= p_in)

    def outer_chunk(i, u):
        m = 2 * i + u
        return m + 2 * (m >= j_in) if isinstance(m, int) else m + 2 * as_int(m >= j_in)

    def by_row(rows_of):
        return lambda b, u: (rows_of(b), j_in + u)

    def by_rest(rows_of):
        def place(b, u):
            if isinstance(b, int):
                return rows_of(b // other), outer_chunk(b % other, u)
            return rows_of(lax.div(b, other)), outer_chunk(lax.rem(b, other), u)
        return place

    done = [by_row(inner_rows)(0, u) for u in range(2)]
    done = phase(n_in, by_row(inner_rows), done)
    strain_pull(ns, nodes, pull)
    for part in full[:2]:
        widen(part.start + rim, rim, ylo, 4)
        widen(part.start + rim, rim, yhi, 4)
    come(*thin)
    thin_corners = [
        remote(lo_n & lo_w, lo_n & hi_w, extra.at[0, elow], extra.at[0, eabove], dn_w),
        remote(lo_n & hi_w, lo_n & lo_w, extra.at[0, ehigh], extra.at[0, ebelow], up_w),
        remote(hi_n & lo_w, hi_n & hi_w, extra.at[1, elow], extra.at[1, eabove], dn_w),
        remote(hi_n & hi_w, hi_n & lo_w, extra.at[1, ehigh], extra.at[1, ebelow], up_w)]
    go(*thin_corners)
    spots = (7, 8 + cols + 2 * side)

    def rims(span, source, first, count):
        rimcol[:, span] = extra[:, span].astype(F32)
        for r in range(count % 4):
            for i, spot in enumerate(spots):
                win[first + r, spot:spot + 1] = rimcol[i, source + r:source + r + 1]

        @pl.loop(0, count // 4)
        def _(b):
            for a in range(4):
                r = count % 4 + 4 * b + a
                for i, spot in enumerate(spots):
                    win[first + r, spot:spot + 1] = rimcol[i, pl.ds(source + r, 1), :]

    come(*bands, *second_hop)
    if detour:
        follow = []
        for here, band in ((gap_dn, below), (gap_up, above)):
            follow += [
                remote(here & hi_n, here & lo_n, ext.at[band, cols:cols + side], ext.at[band, ylo], up_n),
                remote(here & lo_n, here & hi_n, ext.at[band, side:2 * side], ext.at[band, yhi], dn_n)]
        go(*follow)
        corners += follow
    widen(0, rim, mid, 2)
    widen(rim + rows, rim, mid, 2)
    done = phase(2 * p_in, by_row(outer_rows), done)
    rims(emid, SIDE, rim, rows)
    come(*strips[2])
    widen(2 * rim, rows - 2 * rim, ylo, 4)
    widen(2 * rim, rows - 2 * rim, yhi, 4)
    done = phase(n_in * other, by_rest(inner_rows), done)
    even = lax.rem(w, 2) == 0
    odd = jnp.logical_not(even)
    lands_below = corners[0:2] + thin_corners[1::2] + corners[4:6]
    lands_above = corners[2:4] + thin_corners[0::2] + corners[6:8]

    def finish(cond, lands, first, span, source):
        for k in lands:
            @pl.when(everything[k][1] & cond)
            def _(k=k):
                everything[k][2].wait_recv()

        @pl.when(cond)
        def _():
            widen(first, rim, ylo, 4)
            widen(first, rim, yhi, 4)
            rims(span, source, first, rim)

    low_span, high_span = slice(0, SIDE), slice(SIDE + rows, 2 * SIDE + rows)
    for upper in (even, odd):
        finish(upper, lands_above, rim + rows, high_span, SIDE + rows)
        finish(jnp.logical_not(upper), lands_below, 0, low_span, SIDE - rim)
        shift = jnp.where(upper, steps - p_in, 0)
        done = phase(p_in * other, by_rest(lambda i, shift=shift: i + shift), done)
    for u in range(2):
        fold(u, done[u][0] * chunks + done[u][1])
    for i in range(steps + 1):
        head, tail = split(gsum[i])
        gacc[i] = jnp.dot(proj[...], jnp.concatenate([head, tail], axis=0), preferred_element_type=F32)
    for i in range(steps):
        head, tail = split(dpart[i * chunks:(i + 1) * chunks].reshape(cols, comps * layers))
        got = jnp.dot(gather[...], jnp.concatenate([head, tail], axis=0), preferred_element_type=F32)
        dacc[i] = dacc[i] + got[0:QPAD]
        dacc[i + 1] = got[QPAD:2 * QPAD]
    for k, (acc, table) in enumerate(((gacc, down), (dacc, down2))):
        head, tail = split(acc[...].reshape(-1, comps * layers))
        got = (jnp.dot(head, table[...], preferred_element_type=F32)
               + jnp.dot(tail, table[...], preferred_element_type=F32)).reshape(pull.shape)
        terms[k] = got + pull[...] if k == 0 else got

    for k in range(2):
        for p in range(nel):
            colf[k, p:p + 1] = terms[k, p, nel:nel + 1]
    to_w = remote(hi_w, lo_w, terms.at[:, nel], from_w, up_w)
    to_n = remote(hi_n, lo_n, colf.at[:, 0:nel], from_n, up_n)
    to_c = remote(lo_w & hi_n, lo_w & lo_n, from_w.at[:, nel:QPAD], from_c, up_n)
    go(to_w, to_n)
    come(to_w)
    go(to_c)
    come(to_n, to_c)
    first_row = lax.broadcasted_iota(jnp.int32, (nel, 128), 0) == 0
    for p in range(nel):
        both = []
        for k in range(2):
            value = terms[k, p, 0:nel]
            beside = from_n[k, p:p + 1]
            if p == 0:
                value = value + from_w[k, 0:nel]
                beside = beside + from_c[k, 0:1]
            both.append(value + jnp.where(first_row, jnp.broadcast_to(beside, (nel, 128)), 0.0))
        step = both[0] / (both[1] + STIFFNESS)
        for c in range(comps):
            here = step if c == 0 else pltpu.roll(step, 128 - ns * c, 1)
            change[c, p] = here[:, 0:ns]
    sent = strips[0] + strips[1]
    for k, (goes, _c, copy) in enumerate(everything):
        if k not in sent:
            @pl.when(goes)
            def _(copy=copy):
                copy.wait_send()


def emit_kernel(parts, kept, change, disp, residual, updated, fresh, sem):
    rows = kept.shape[0] // parts
    copies = [pltpu.make_async_copy(kept.at[k * rows:(k + 1) * rows], residual.at[k * rows:(k + 1) * rows], sem.at[k])
              for k in range(parts)]
    for copy in copies:
        copy.start()
    fresh[...] = disp[...] - change[...]
    last = pltpu.make_async_copy(fresh, updated, sem.at[parts])
    last.start()
    for copy in copies + [last]:
        copy.wait()


def emit(kept, change, nodal):
    anywhere = pl.BlockSpec(memory_space=pl.ANY)
    near = pl.BlockSpec(memory_space=pltpu.VMEM)
    parts = 8
    return pl.pallas_call(
        functools.partial(emit_kernel, parts),
        out_shape=[jax.ShapeDtypeStruct(kept.shape, BF16), jax.ShapeDtypeStruct(nodal.shape, F32)],
        in_specs=[anywhere, near, near],
        out_specs=[anywhere, anywhere],
        scratch_shapes=[pltpu.VMEM(nodal.shape, F32), pltpu.SemaphoreType.DMA((parts + 1,))],
        compiler_params=pltpu.CompilerParams(vmem_limit_bytes=8 << 20),
        name="emit",
    )(kept, change, nodal)


def per_device(nw, nn, reference_image, deformed_image, displacement, tile_map):
    comps, ns, nel, _ = displacement.shape
    rows, cols, layers = reference_image.shape
    nodal = displacement.transpose(0, 2, 3, 1)
    rim = rows // 4 + 1
    npx, lanes = nel + 1, comps * layers
    total, across = rows + 2 * rim, cols + 2 * (rim - 1)
    anywhere = pl.BlockSpec(memory_space=pl.ANY)
    near = pl.BlockSpec(memory_space=pltpu.VMEM)
    kept, change = pl.pallas_call(
        functools.partial(step_kernel, nw, nn, rim, ns),
        out_shape=[jax.ShapeDtypeStruct(reference_image.shape, BF16),
                   jax.ShapeDtypeStruct(nodal.shape, F32)],
        in_specs=[anywhere] * 4,
        out_specs=[near, near],
        scratch_shapes=[
            pltpu.VMEM((cols, 2 * QPAD), BF16),
            pltpu.VMEM((QPAD, 2 * cols), BF16),
            pltpu.VMEM((2 * 128, lanes), BF16),
            pltpu.VMEM((lanes, 128), BF16),
            pltpu.VMEM((lanes, 128), BF16),
            pltpu.VMEM((32, 8 * 16), BF16),
            pltpu.VMEM((2 * QPAD, 2 * cols), BF16),
            pltpu.VMEM((layers, layers), BF16),
            pltpu.VMEM((total, across, layers), BF16),
            pltpu.VMEM((rim, cols - cols // 2, layers), BF16),
            pltpu.VMEM((total, across + 16, layers), F32),
            pltpu.VMEM((npx, cols, lanes), F32),
            pltpu.VMEM((npx, cols, lanes), F32),
            pltpu.VMEM((2, 8 * 16, lanes), BF16),
            pltpu.VMEM((2, 8 * 16, layers), F32),
            pltpu.VMEM((rows // 8 * (cols // 16), 16, lanes), F32),
            pltpu.VMEM((npx, QPAD, lanes), F32),
            pltpu.VMEM((npx, QPAD, lanes), F32),
            pltpu.VMEM((2, npx, QPAD, 128), F32),
            pltpu.VMEM((2, rows + 2 * SIDE, layers), BF16),
            pltpu.VMEM((2, rows + 2 * SIDE, layers), F32),
            pltpu.VMEM((npx, QPAD, 128), F32),
            pltpu.VMEM((npx, QPAD, 128), F32),
            pltpu.VMEM((comps, nel, nel, 128), F32),
            pltpu.VMEM((nel, 128), F32),
            pltpu.VMEM((nel, 128), F32),
            pltpu.VMEM((8, 128), F32),
            pltpu.VMEM((2, rows, layers), F32),
            pltpu.VMEM((2, rows, layers), BF16),
            pltpu.VMEM((2, QPAD, 128), F32),
            pltpu.VMEM((2, nel, 128), F32),
            pltpu.VMEM((2, QPAD - nel, 128), F32),
            pltpu.VMEM(nodal.shape, F32),
            pltpu.SMEM((2,), jnp.int32),
            pltpu.SemaphoreType.DMA((34,)),
            pltpu.SemaphoreType.DMA((34,)),
            pltpu.SemaphoreType.DMA((4,)),
        ],
        compiler_params=pltpu.CompilerParams(
            collective_id=0, has_side_effects=True, vmem_limit_bytes=48 << 20),
        name="step",
    )(tile_map.reshape(2), deformed_image, reference_image, nodal)
    residual, updated = emit(kept, change, nodal)
    return (updated.transpose(0, 3, 1, 2), residual)


def solution(mesh):
    placed = (
        P("wide", "narrow", None),
        P("wide", "narrow", None),
        P(None, None, "wide", "narrow"),
        P("wide", "narrow", None),
    )
    return jax.shard_map(
        functools.partial(per_device, mesh.shape["wide"], mesh.shape["narrow"]),
        mesh=mesh,
        in_specs=placed,
        out_specs=(P(None, None, "wide", "narrow"), P("wide", "narrow", None)),
        check_vma=False,
    )
```

```python
import functools

import jax
import jax.numpy as jnp
from jax import lax
from jax.experimental import pallas as pl
from jax.experimental.pallas import tpu as pltpu
from jax.sharding import PartitionSpec as P

MU_SHEAR = 1.0
LAMBDA_BULK = 2.0
REG_WEIGHT = 256.0
STIFFNESS = 16.0
MESH = pl.DeviceIdType.MESH
F32 = jnp.float32
BF16 = jnp.bfloat16
SIDE = 48
QPAD = 24


def as_int(flag):
    return flag.astype(jnp.int32)


def hat(place, node):
    at = (place.astype(F32) + 0.5) * 0.125
    return jnp.maximum(1.0 - jnp.abs(at - node.astype(F32)), 0.0)


def build_tables(ns, inter, proj, up, down, down2, square, gather, dz):
    def grid(ref):
        return (lax.broadcasted_iota(jnp.int32, ref.shape, 0), lax.broadcasted_iota(jnp.int32, ref.shape, 1))

    cols = inter.shape[0]
    r, c = grid(inter)
    inter[...] = (0.5 * hat(r, jnp.where(c < QPAD, c, c - QPAD))).astype(BF16)
    r, c = grid(proj)
    proj[...] = hat(jnp.where(c < cols, c, c - cols), r).astype(BF16)
    r, c = grid(up)
    up[...] = hat(c % 128, r % 128 - ns * (c // 128)).astype(BF16)
    r, c = grid(down)
    layer = hat(r % 128, c - ns * (r // 128))
    down[...] = (-0.5 * layer).astype(BF16)
    down2[...] = (0.25 * layer * layer).astype(BF16)
    r, c = grid(square)
    along = (c // 16).astype(F32) * 0.125 + 0.0625
    along = jnp.where(r % 16 < 8, 1.0 - along, along)
    across = hat(c % 16, r % 8)
    whole = (along * along) * (across * across)
    head = whole.astype(BF16).astype(F32)
    square[...] = jnp.where(r < 16, head, whole - head).astype(BF16)
    r, c = grid(dz)
    dz[...] = (jnp.where(r == c + 1, 1.0, 0.0) - jnp.where(r == c - 1, 1.0, 0.0)).astype(BF16)
    r, c = grid(gather)
    low = r < QPAD
    node = jnp.where(low, r, r - QPAD)
    k = c % 128
    same = (node == 2 * (k // 16) + k % 8) & (k % 8 < 3) & (low == (k % 16 < 8))
    gather[...] = jnp.where(same, 1.0, 0.0).astype(BF16)


def split(value):
    high = value.astype(BF16)
    return high, (value - high.astype(F32)).astype(BF16)


def strain_pull(ns, nodes, pull):
    npx = nodes.shape[0]
    nel = npx - 1
    lane = lax.broadcasted_iota(jnp.int32, (nel, 128), 1)
    move = lambda a, by: pltpu.roll(a, by % 128, 1)
    pull[...] = jnp.zeros_like(pull)

    @pl.loop(0, nel)
    def _(p):
        a00, a01 = nodes[p, 0:nel], nodes[p, 1:nel + 1]
        a10, a11 = nodes[p + 1, 0:nel], nodes[p + 1, 1:nel + 1]
        dx = (a10 - a00) + (a11 - a01)
        dy = (a01 - a00) + (a11 - a10)
        every = (a00 + a01) + (a10 + a11)
        slopes = (dx + move(dx, -1), dy + move(dy, -1), move(every, -1) - every)
        f = [[0.03125 * (move(h, -ns * i) if i else h) + (1.0 if i == j else 0.0)
              for j, h in enumerate(slopes)] for i in range(3)]
        cof = [[f[(i + 1) % 3][(j + 1) % 3] * f[(i + 2) % 3][(j + 2) % 3]
                - f[(i + 1) % 3][(j + 2) % 3] * f[(i + 2) % 3][(j + 1) % 3]
                for j in range(3)] for i in range(3)]
        ratio = f[0][0] * cof[0][0] + f[0][1] * cof[0][1] + f[0][2] * cof[0][2]
        factor = (LAMBDA_BULK * jnp.log(ratio) - MU_SHEAR) / ratio
        back = []
        for j in range(3):
            parts = [jnp.where(lane < ns - 1, MU_SHEAR * f[i][j] + factor * cof[i][j], 0.0) for i in range(3)]
            back.append((parts[0] + move(parts[1], ns) + move(parts[2], 2 * ns)) * (0.03125 * REG_WEIGHT))
        gx = back[0] + move(back[0], 1)
        gy = back[1] + move(back[1], 1)
        gz = move(back[2], 1) - back[2]
        for dp, dq in ((0, 0), (0, 1), (1, 0), (1, 1)):
            add = (gx if dp else -gx) + (gy if dq else -gy) + gz
            pull[p + dp, dq:dq + nel] = pull[p + dp, dq:dq + nel] + add


def voxels(window, slope_z, ref_rows, left, right):
    back = []
    rows, squares = [None] * 8, [[None] * 3 for _ in range(8)]
    join = lambda a, b: jnp.concatenate([a, b], axis=0)
    for half in range(2):
        run, tot = [None] * 3, [None] * 3
        inc = [(right(c, half) - left(c, half)) * 0.125 for c in range(3)]
        mv = [left(c, half) + 0.5 * inc[c] for c in range(3)]
        prev, cur = window(0, 0, half), window(1, 0, half)
        for k in range(8):
            nxt = window(k + 2, 0, half)
            g = [nxt - prev,
                 window(k + 1, 1, half) - window(k + 1, -1, half),
                 slope_z(k, half)]
            r = ref_rows(k, half) - cur
            for c in range(3):
                r = r - g[c] * mv[c]
                if k < 7:
                    mv[c] = mv[c] + inc[c]
            rows[k] = r if half == 0 else join(rows[k], r).astype(BF16)
            for c in range(3):
                f = g[c] * r
                q = g[c] * g[c]
                run[c] = f if k == 0 else run[c] + f
                tot[c] = run[c] if k == 0 else tot[c] + run[c]
                squares[k][c] = q if half == 0 else join(squares[k][c], q).astype(BF16)
            prev, cur = cur, nxt
        part = []
        for c in range(3):
            low = (tot[c] - 0.5 * run[c]) * 0.125
            part.append((low, run[c] - low))
        back.append(part)
    return rows, squares, [[join(back[0][c][i], back[1][c][i]) for i in range(2)] for c in range(3)]


def step_kernel(nw, nn, rim, ns, map_hbm, own, ref_hbm, disp_hbm,
                res, change,
                inter, proj, up, down, down2, square, gather, dz,
                ext, passed, win, field, gsum, qbuf, zbuf, dpart, gacc, dacc, terms,
                extra, rimcol, nodes, pull, cube, column, side_in, corner_in, colf, colb,
                from_w, from_n, from_c, disp, map_ref, send, recv, lsem):
    rows, cols, layers = own.shape
    comps, nel = disp.shape[0], disp.shape[1]
    side = rim - 1
    w = lax.axis_index("wide")
    n = lax.axis_index("narrow")
    lo_w, hi_w, lo_n, hi_n = w > 0, w < nw - 1, n > 0, n < nn - 1
    up_w, dn_w = (w + 1, n), (w - 1, n)
    up_n, dn_n = (w, n + 1), (w, n - 1)
    mid = slice(side, side + cols)
    ylo = slice(0, side)
    yhi = slice(side + cols, 2 * side + cols)
    total = rows + 2 * rim
    emid = slice(SIDE, SIDE + rows)
    detour = nw == 8
    is0, is3, is4, is7 = (w == 0), (w == 3), (w == 4), (w == 7)

    barrier = pltpu.get_barrier_semaphore()
    greet = [(lo_w, dn_w), (hi_w, up_w), (lo_n, dn_n), (hi_n, up_n)]
    if detour:
        greet += [(is7, (3, n)), (is4, (7, n)), (is0, (4, n)), (is3, (0, n))]
    count = as_int(lo_w) + as_int(hi_w) + as_int(lo_n) + as_int(hi_n)
    if detour:
        count = count + as_int(is0 | is3 | is4 | is7)
    for there, device in greet:
        @pl.when(there)
        def _(device=device):
            pl.semaphore_signal(barrier, inc=1, device_id=device, device_id_type=MESH)
    loads = [pltpu.make_async_copy(disp_hbm, disp, lsem.at[2]),
             pltpu.make_async_copy(own, ext.at[rim:rim + rows, mid], lsem.at[0]),
             pltpu.make_async_copy(ref_hbm, res, lsem.at[1]),
             pltpu.make_async_copy(map_hbm, map_ref, lsem.at[3])]
    for load in loads:
        load.start()
    nodal, local, slab, offsets = loads

    def absent(there, *spans):
        @pl.when(jnp.logical_not(there))
        def _():
            for ref, span in spans:
                ref[span] = jnp.zeros(ref.at[span].shape, ref.dtype)

    elow, ehigh = slice(SIDE, 2 * SIDE), slice(rows, SIDE + rows)
    ebelow, eabove = slice(0, SIDE), slice(SIDE + rows, 2 * SIDE + rows)
    every = slice(None)
    absent(hi_w, (nodes, (nel, slice(0, nel))))
    absent(hi_n, (side_in, every), (extra, 1))
    absent(hi_w & hi_n, (corner_in, every), (extra, (1, eabove)))
    absent(lo_w & hi_n, (extra, (1, ebelow)))
    absent(lo_w, (from_w, every))
    absent(lo_n, (from_n, every), (extra, 0))
    absent(lo_w & lo_n, (from_c, every), (extra, (0, ebelow)))
    absent(hi_w & lo_n, (extra, (0, eabove)))
    pl.semaphore_wait(barrier, count)

    everything = []

    def remote(goes, comes, src, dst, device):
        k = len(everything)
        copy = pltpu.make_async_remote_copy(
            src_ref=src, dst_ref=dst, send_sem=send.at[k], recv_sem=recv.at[k],
            device_id=device, device_id_type=MESH)
        everything.append((goes, comes, copy))
        return k

    def go(*ks):
        for k in ks:
            @pl.when(everything[k][0])
            def _(k=k):
                everything[k][2].start()

    def come(*ks):
        for k in ks:
            @pl.when(everything[k][1])
            def _(k=k):
                everything[k][2].wait_recv()

    below, above = slice(0, rim), slice(rim + rows, total)
    edge_x = remote(lo_w, hi_w, nodes.at[0, 0:nel], nodes.at[nel, 0:nel], dn_w)
    edge_y = remote(lo_n, hi_n, column, side_in, dn_n)
    strips = []
    full = (slice(0, rim), slice(rows - rim, rows), slice(rim, rows - rim))
    for part in full:
        there = slice(part.start + rim, part.stop + rim)
        strips.append((
            remote(hi_n, lo_n, own.at[part, cols - side:cols], ext.at[there, ylo], up_n),
            remote(lo_n, hi_n, own.at[part, 0:side], ext.at[there, yhi], dn_n)))
    cut = cols // 2 if detour else cols
    near, far = slice(0, cut), slice(cut, cols)
    enear, efar = slice(side, side + cut), slice(side + cut, side + cols)
    high_own, low_own = slice(rows - rim, rows), slice(0, rim)
    bands = [
        remote(hi_w, lo_w, own.at[high_own, near], ext.at[below, enear], up_w),
        remote(lo_w, hi_w, own.at[low_own, near], ext.at[above, enear], dn_w)]
    first_hop, second_hop = [], []
    if detour:
        bands += [
            remote(hi_w & (w != 3), lo_w & (w != 4), own.at[high_own, far], ext.at[below, efar], up_w),
            remote(lo_w & (w != 4), hi_w & (w != 3), own.at[low_own, far], ext.at[above, efar], dn_w)]
        first_hop = [
            remote(is3, is7, own.at[high_own, far], passed, (7, n)),
            remote(is4, is0, own.at[low_own, far], passed, (0, n))]
        second_hop = [
            remote(is7, is4, passed, ext.at[below, efar], (4, n)),
            remote(is0, is3, passed, ext.at[above, efar], (3, n))]
    go(*strips[0], *strips[1], *first_hop, *bands)
    cube[...] = jnp.zeros_like(cube)
    nodal.wait()
    cube[:, :, :, 0:ns] = disp[...]
    for i in range(nel):
        value = cube[0, i]
        for c in range(1, comps):
            value = value + pltpu.roll(cube[c, i], ns * c, 1)
        nodes[i, 0:nel] = value
        column[i:i + 1] = value[0:1]
    go(edge_x, edge_y)

    def widen(first, count, columns, together):
        to = slice(columns.start + 8, columns.stop + 8)

        @pl.loop(0, count // together)
        def _(b):
            for a in range(together):
                win[first + together * b + a, to] = ext[first + together * b + a, columns].astype(F32)
        for r in range(first + count // together * together, first + count):
            win[r, to] = ext[r, columns].astype(F32)

    local.wait()
    widen(rim, rows, mid, 2)
    build_tables(ns, inter, proj, up, down, down2, square, gather, dz)
    absent(lo_n, (ext, (every, ylo)))
    absent(hi_n, (ext, (every, yhi)))
    absent(lo_w, (ext, below))
    absent(hi_w, (ext, above))
    come(edge_x)
    edge_c = remote(hi_w & lo_n, hi_w & hi_n, nodes.at[nel, 0:8], corner_in, dn_n)
    go(edge_c)
    come(edge_y)
    top = lax.broadcasted_iota(jnp.int32, (QPAD - nel, 128), 0) == 0
    for i in range(nel):
        nodes[i, nel:QPAD] = jnp.where(top, jnp.broadcast_to(side_in[i:i + 1], (QPAD - nel, 128)), 0.0)
    come(edge_c)
    nodes[nel, nel:QPAD] = jnp.where(top, jnp.broadcast_to(corner_in[0:1], (QPAD - nel, 128)), 0.0)
    come(*first_hop)
    go(*second_hop)
    corners = []
    come(*strips[0], *strips[1])
    gap_up, gap_dn = (w == 3, w == 4) if detour else (w < 0, w < 0)
    keep_up, keep_dn = hi_w & jnp.logical_not(gap_up), lo_w & jnp.logical_not(gap_dn)
    corners += [
        remote(keep_up & lo_n, keep_dn & lo_n, ext.at[rows:rows + rim, ylo], ext.at[below, ylo], up_w),
        remote(keep_up & hi_n, keep_dn & hi_n, ext.at[rows:rows + rim, yhi], ext.at[below, yhi], up_w),
        remote(keep_dn & lo_n, keep_up & lo_n, ext.at[rim:2 * rim, ylo], ext.at[above, ylo], dn_w),
        remote(keep_dn & hi_n, keep_up & hi_n, ext.at[rim:2 * rim, yhi], ext.at[above, yhi], dn_w)]
    go(*corners)
    for k in strips[0] + strips[1]:
        @pl.when(everything[k][0])
        def _(k=k):
            everything[k][2].wait_send()
    go(*strips[2])

    picks = (side + cols - rim, side + rim - 1)

    @pl.loop(0, rows // 8)
    def _(b):
        for a in range(8):
            for i, col in enumerate(picks):
                tile = ext[rim + 8 * b + a, col // 16 * 16:col // 16 * 16 + 16, :].astype(F32)
                colf[i, pl.ds(8 * b + a, 1), :] = tile[col % 16:col % 16 + 1]
    colb[...] = colf[...].astype(BF16)
    thin = [remote(hi_n, lo_n, colb.at[0], extra.at[0, emid], up_n),
            remote(lo_n, hi_n, colb.at[1], extra.at[1, emid], dn_n)]
    go(*thin)

    flat = nodes[...].reshape(-1, 128)
    high = flat.astype(BF16).astype(F32)
    both = jnp.concatenate([high, flat - high], axis=1).astype(BF16)
    level = jnp.dot(both, up[...], preferred_element_type=F32)
    for i in range(nel + 1):
        head, tail = split(level[i * QPAD:(i + 1) * QPAD])
        field[i] = jnp.dot(inter[...], jnp.concatenate([head, tail], axis=0), preferred_element_type=F32)
    for ref in (gsum, qbuf, dacc):
        ref[...] = jnp.zeros_like(ref)
    offsets.wait()
    slab.wait()
    steps, chunks = rows // 8, cols // 16
    start = map_ref[0] + side
    col0 = map_ref[1] + 8 + side

    def fold(u, t):
        got = jnp.dot(square[...], qbuf[u], preferred_element_type=F32)
        dpart[t] = got[0:16] + got[16:32]

    def slopes(p, j):
        row0 = start + 8 * p + 1
        at = col0 + 16 * j
        here = jnp.concatenate([win[row0 + k, pl.ds(at, 16), :].astype(BF16) for k in range(8)], axis=0)
        return jnp.dot(here, dz[...], preferred_element_type=F32)

    def phase(pairs, place, before):
        for u in range(2):
            zbuf[u] = slopes(*place(0, u))

        @pl.loop(0, pairs)
        def _(b):
            coming = [slopes(*place(jnp.minimum(b + 1, pairs - 1), u)) for u in range(2)]
            for u in range(2):
                last = place(jnp.maximum(b - 1, 0), u)
                fold(u, jnp.where(b == 0, before[u][0] * chunks + before[u][1], last[0] * chunks + last[1]))
            for u in range(2):
                p, j = place(b, u)
                at = 16 * j if isinstance(j, int) else pl.multiple_of(16 * j, 16)
                base = 8 * p
                row0 = start + base
                refs = [res[base + k, pl.ds(at, 16), :].astype(F32) for k in range(8)]
                out_rows, squares, parts = voxels(
                    lambda k, shift, half: win[row0 + k, pl.ds(col0 + at + (8 * half + shift), 8), :],
                    lambda k, half: zbuf[u, 16 * k + 8 * half:16 * k + 8 * half + 8, :],
                    lambda k, half: refs[k][8 * half:8 * half + 8],
                    lambda c, half: field[p, pl.ds(at + 8 * half, 8), c * layers:(c + 1) * layers],
                    lambda c, half: field[p + 1, pl.ds(at + 8 * half, 8), c * layers:(c + 1) * layers])
                for k in range(8):
                    res[base + k, pl.ds(at, 16), :] = out_rows[k]
                for c in range(comps):
                    lanes = slice(c * layers, (c + 1) * layers)
                    for k in range(8):
                        qbuf[u, 16 * k:16 * k + 16, lanes] = squares[k][c]
                    for i in range(2):
                        gsum[p + i, pl.ds(at, 16), lanes] = gsum[p + i, pl.ds(at, 16), lanes] + parts[c][i]
            for u in range(2):
                zbuf[u] = coming[u]
        return [place(pairs - 1, u) for u in range(2)]

    p_in = (rim + 7) // 8
    n_in = steps - 2 * p_in
    j_in = (rim + 15) // 16
    other = (chunks - 2) // 2

    def inner_rows(i):
        return p_in + i

    def outer_rows(i):
        return i + n_in * as_int(jnp.asarray(i) >= p_in) if not isinstance(i, int) else i + n_in * (i >= p_in)

    def outer_chunk(i, u):
        m = 2 * i + u
        return m + 2 * (m >= j_in) if isinstance(m, int) else m + 2 * as_int(m >= j_in)

    def by_row(rows_of):
        return lambda b, u: (rows_of(b), j_in + u)

    def by_rest(rows_of):
        def place(b, u):
            if isinstance(b, int):
                return rows_of(b // other), outer_chunk(b % other, u)
            return rows_of(lax.div(b, other)), outer_chunk(lax.rem(b, other), u)
        return place

    done = [by_row(inner_rows)(0, u) for u in range(2)]
    done = phase(n_in, by_row(inner_rows), done)
    strain_pull(ns, nodes, pull)
    for part in full[:2]:
        widen(part.start + rim, rim, ylo, 4)
        widen(part.start + rim, rim, yhi, 4)
    come(*thin)
    thin_corners = [
        remote(lo_n & lo_w, lo_n & hi_w, extra.at[0, elow], extra.at[0, eabove], dn_w),
        remote(lo_n & hi_w, lo_n & lo_w, extra.at[0, ehigh], extra.at[0, ebelow], up_w),
        remote(hi_n & lo_w, hi_n & hi_w, extra.at[1, elow], extra.at[1, eabove], dn_w),
        remote(hi_n & hi_w, hi_n & lo_w, extra.at[1, ehigh], extra.at[1, ebelow], up_w)]
    go(*thin_corners)
    spots = (7, 8 + cols + 2 * side)

    def rims(span, source, first, count):
        rimcol[:, span] = extra[:, span].astype(F32)
        for r in range(count % 4):
            for i, spot in enumerate(spots):
                win[first + r, spot:spot + 1] = rimcol[i, source + r:source + r + 1]

        @pl.loop(0, count // 4)
        def _(b):
            for a in range(4):
                r = count % 4 + 4 * b + a
                for i, spot in enumerate(spots):
                    win[first + r, spot:spot + 1] = rimcol[i, pl.ds(source + r, 1), :]

    def bands_wait(cond):
        for k in bands + second_hop:
            @pl.when(everything[k][1] & cond)
            def _(k=k):
                everything[k][2].wait_recv()

    bands_wait(gap_dn | gap_up)
    if detour:
        follow = []
        for here, band in ((gap_dn, below), (gap_up, above)):
            follow += [
                remote(here & hi_n, here & lo_n, ext.at[band, cols:cols + side], ext.at[band, ylo], up_n),
                remote(here & lo_n, here & hi_n, ext.at[band, side:2 * side], ext.at[band, yhi], dn_n)]
        go(*follow)
        corners += follow
    rims(emid, SIDE, rim, rows)
    come(*strips[2])
    widen(2 * rim, rows - 2 * rim, ylo, 4)
    widen(2 * rim, rows - 2 * rim, yhi, 4)
    done = phase(n_in * other, by_rest(inner_rows), done)
    bands_wait(jnp.logical_not(gap_dn | gap_up))
    widen(0, rim, mid, 2)
    widen(rim + rows, rim, mid, 2)
    done = phase(2 * p_in, by_row(outer_rows), done)
    come(*corners, *thin_corners)
    for first in (0, rim + rows):
        widen(first, rim, ylo, 4)
        widen(first, rim, yhi, 4)
    rims(slice(0, SIDE), SIDE - rim, 0, rim)
    rims(slice(SIDE + rows, 2 * SIDE + rows), SIDE + rows, rim + rows, rim)
    done = phase(2 * p_in * other, by_rest(outer_rows), done)
    for u in range(2):
        fold(u, done[u][0] * chunks + done[u][1])
    for i in range(steps + 1):
        head, tail = split(gsum[i])
        gacc[i] = jnp.dot(proj[...], jnp.concatenate([head, tail], axis=0), preferred_element_type=F32)
    for i in range(steps):
        head, tail = split(dpart[i * chunks:(i + 1) * chunks].reshape(cols, comps * layers))
        got = jnp.dot(gather[...], jnp.concatenate([head, tail], axis=0), preferred_element_type=F32)
        dacc[i] = dacc[i] + got[0:QPAD]
        dacc[i + 1] = got[QPAD:2 * QPAD]
    for k, (acc, table) in enumerate(((gacc, down), (dacc, down2))):
        head, tail = split(acc[...].reshape(-1, comps * layers))
        got = (jnp.dot(head, table[...], preferred_element_type=F32)
               + jnp.dot(tail, table[...], preferred_element_type=F32)).reshape(pull.shape)
        terms[k] = got + pull[...] if k == 0 else got

    for k in range(2):
        for p in range(nel):
            colf[k, p:p + 1] = terms[k, p, nel:nel + 1]
    to_w = remote(hi_w, lo_w, terms.at[:, nel], from_w, up_w)
    to_n = remote(hi_n, lo_n, colf.at[:, 0:nel], from_n, up_n)
    to_c = remote(lo_w & hi_n, lo_w & lo_n, from_w.at[:, nel:QPAD], from_c, up_n)
    go(to_w, to_n)
    come(to_w)
    go(to_c)
    come(to_n, to_c)
    first_row = lax.broadcasted_iota(jnp.int32, (nel, 128), 0) == 0
    for p in range(nel):
        both = []
        for k in range(2):
            value = terms[k, p, 0:nel]
            beside = from_n[k, p:p + 1]
            if p == 0:
                value = value + from_w[k, 0:nel]
                beside = beside + from_c[k, 0:1]
            both.append(value + jnp.where(first_row, jnp.broadcast_to(beside, (nel, 128)), 0.0))
        step = both[0] / (both[1] + STIFFNESS)
        for c in range(comps):
            here = step if c == 0 else pltpu.roll(step, 128 - ns * c, 1)
            change[c, p] = here[:, 0:ns]
    sent = strips[0] + strips[1]
    for k, (goes, _c, copy) in enumerate(everything):
        if k not in sent:
            @pl.when(goes)
            def _(copy=copy):
                copy.wait_send()


def emit_kernel(parts, kept, change, disp, residual, updated, fresh, sem):
    rows = kept.shape[0] // parts
    copies = [pltpu.make_async_copy(kept.at[k * rows:(k + 1) * rows], residual.at[k * rows:(k + 1) * rows], sem.at[k])
              for k in range(parts)]
    for copy in copies:
        copy.start()
    fresh[...] = disp[...] - change[...]
    last = pltpu.make_async_copy(fresh, updated, sem.at[parts])
    last.start()
    for copy in copies + [last]:
        copy.wait()


def emit(kept, change, nodal):
    anywhere = pl.BlockSpec(memory_space=pl.ANY)
    near = pl.BlockSpec(memory_space=pltpu.VMEM)
    parts = 8
    return pl.pallas_call(
        functools.partial(emit_kernel, parts),
        out_shape=[jax.ShapeDtypeStruct(kept.shape, BF16), jax.ShapeDtypeStruct(nodal.shape, F32)],
        in_specs=[anywhere, near, near],
        out_specs=[anywhere, anywhere],
        scratch_shapes=[pltpu.VMEM(nodal.shape, F32), pltpu.SemaphoreType.DMA((parts + 1,))],
        compiler_params=pltpu.CompilerParams(vmem_limit_bytes=8 << 20),
        name="emit",
    )(kept, change, nodal)


def per_device(nw, nn, reference_image, deformed_image, displacement, tile_map):
    comps, ns, nel, _ = displacement.shape
    rows, cols, layers = reference_image.shape
    nodal = displacement.transpose(0, 2, 3, 1)
    rim = rows // 4 + 1
    npx, lanes = nel + 1, comps * layers
    total, across = rows + 2 * rim, cols + 2 * (rim - 1)
    anywhere = pl.BlockSpec(memory_space=pl.ANY)
    near = pl.BlockSpec(memory_space=pltpu.VMEM)
    kept, change = pl.pallas_call(
        functools.partial(step_kernel, nw, nn, rim, ns),
        out_shape=[jax.ShapeDtypeStruct(reference_image.shape, BF16),
                   jax.ShapeDtypeStruct(nodal.shape, F32)],
        in_specs=[anywhere] * 4,
        out_specs=[near, near],
        scratch_shapes=[
            pltpu.VMEM((cols, 2 * QPAD), BF16),
            pltpu.VMEM((QPAD, 2 * cols), BF16),
            pltpu.VMEM((2 * 128, lanes), BF16),
            pltpu.VMEM((lanes, 128), BF16),
            pltpu.VMEM((lanes, 128), BF16),
            pltpu.VMEM((32, 8 * 16), BF16),
            pltpu.VMEM((2 * QPAD, 2 * cols), BF16),
            pltpu.VMEM((layers, layers), BF16),
            pltpu.VMEM((total, across, layers), BF16),
            pltpu.VMEM((rim, cols - cols // 2, layers), BF16),
            pltpu.VMEM((total, across + 16, layers), F32),
            pltpu.VMEM((npx, cols, lanes), F32),
            pltpu.VMEM((npx, cols, lanes), F32),
            pltpu.VMEM((2, 8 * 16, lanes), BF16),
            pltpu.VMEM((2, 8 * 16, layers), F32),
            pltpu.VMEM((rows // 8 * (cols // 16), 16, lanes), F32),
            pltpu.VMEM((npx, QPAD, lanes), F32),
            pltpu.VMEM((npx, QPAD, lanes), F32),
            pltpu.VMEM((2, npx, QPAD, 128), F32),
            pltpu.VMEM((2, rows + 2 * SIDE, layers), BF16),
            pltpu.VMEM((2, rows + 2 * SIDE, layers), F32),
            pltpu.VMEM((npx, QPAD, 128), F32),
            pltpu.VMEM((npx, QPAD, 128), F32),
            pltpu.VMEM((comps, nel, nel, 128), F32),
            pltpu.VMEM((nel, 128), F32),
            pltpu.VMEM((nel, 128), F32),
            pltpu.VMEM((8, 128), F32),
            pltpu.VMEM((2, rows, layers), F32),
            pltpu.VMEM((2, rows, layers), BF16),
            pltpu.VMEM((2, QPAD, 128), F32),
            pltpu.VMEM((2, nel, 128), F32),
            pltpu.VMEM((2, QPAD - nel, 128), F32),
            pltpu.VMEM(nodal.shape, F32),
            pltpu.SMEM((2,), jnp.int32),
            pltpu.SemaphoreType.DMA((34,)),
            pltpu.SemaphoreType.DMA((34,)),
            pltpu.SemaphoreType.DMA((4,)),
        ],
        compiler_params=pltpu.CompilerParams(
            collective_id=0, has_side_effects=True, vmem_limit_bytes=48 << 20),
        name="step",
    )(tile_map.reshape(2), deformed_image, reference_image, nodal)
    residual, updated = emit(kept, change, nodal)
    return (updated.transpose(0, 3, 1, 2), residual)


def solution(mesh):
    placed = (
        P("wide", "narrow", None),
        P("wide", "narrow", None),
        P(None, None, "wide", "narrow"),
        P("wide", "narrow", None),
    )
    return jax.shard_map(
        functools.partial(per_device, mesh.shape["wide"], mesh.shape["narrow"]),
        mesh=mesh,
        in_specs=placed,
        out_specs=(P(None, None, "wide", "narrow"), P("wide", "narrow", None)),
        check_vma=False,
    )
```

```python
import functools

import jax
import jax.numpy as jnp
from jax import lax
from jax.experimental import pallas as pl
from jax.experimental.pallas import tpu as pltpu
from jax.sharding import PartitionSpec as P

MU_SHEAR = 1.0
LAMBDA_BULK = 2.0
REG_WEIGHT = 256.0
STIFFNESS = 16.0
MESH = pl.DeviceIdType.MESH
F32 = jnp.float32
BF16 = jnp.bfloat16
SIDE = 48
QPAD = 24


def as_int(flag):
    return flag.astype(jnp.int32)


def hat(place, node):
    at = (place.astype(F32) + 0.5) * 0.125
    return jnp.maximum(1.0 - jnp.abs(at - node.astype(F32)), 0.0)


def build_tables(ns, inter, proj, up, down, down2, square, gather, dz):
    def grid(ref):
        return (lax.broadcasted_iota(jnp.int32, ref.shape, 0), lax.broadcasted_iota(jnp.int32, ref.shape, 1))

    cols = inter.shape[0]
    r, c = grid(inter)
    inter[...] = (0.5 * hat(r, jnp.where(c < QPAD, c, c - QPAD))).astype(BF16)
    r, c = grid(proj)
    proj[...] = hat(jnp.where(c < cols, c, c - cols), r).astype(BF16)
    r, c = grid(up)
    up[...] = hat(c % 128, r % 128 - ns * (c // 128)).astype(BF16)
    r, c = grid(down)
    layer = hat(r % 128, c - ns * (r // 128))
    down[...] = (-0.5 * layer).astype(BF16)
    down2[...] = (0.25 * layer * layer).astype(BF16)
    r, c = grid(square)
    along = (c // 16).astype(F32) * 0.125 + 0.0625
    along = jnp.where(r % 16 < 8, 1.0 - along, along)
    across = hat(c % 16, r % 8)
    whole = (along * along) * (across * across)
    head = whole.astype(BF16).astype(F32)
    square[...] = jnp.where(r < 16, head, whole - head).astype(BF16)
    r, c = grid(dz)
    dz[...] = (jnp.where(r == c + 1, 1.0, 0.0) - jnp.where(r == c - 1, 1.0, 0.0)).astype(BF16)
    r, c = grid(gather)
    low = r < QPAD
    node = jnp.where(low, r, r - QPAD)
    k = c % 128
    same = (node == 2 * (k // 16) + k % 8) & (k % 8 < 3) & (low == (k % 16 < 8))
    gather[...] = jnp.where(same, 1.0, 0.0).astype(BF16)


def split(value):
    high = value.astype(BF16)
    return high, (value - high.astype(F32)).astype(BF16)


def strain_pull(ns, nodes, pull):
    npx = nodes.shape[0]
    nel = npx - 1
    lane = lax.broadcasted_iota(jnp.int32, (nel, 128), 1)
    move = lambda a, by: pltpu.roll(a, by % 128, 1)
    pull[...] = jnp.zeros_like(pull)

    @pl.loop(0, nel)
    def _(p):
        a00, a01 = nodes[p, 0:nel], nodes[p, 1:nel + 1]
        a10, a11 = nodes[p + 1, 0:nel], nodes[p + 1, 1:nel + 1]
        dx = (a10 - a00) + (a11 - a01)
        dy = (a01 - a00) + (a11 - a10)
        every = (a00 + a01) + (a10 + a11)
        slopes = (dx + move(dx, -1), dy + move(dy, -1), move(every, -1) - every)
        f = [[0.03125 * (move(h, -ns * i) if i else h) + (1.0 if i == j else 0.0)
              for j, h in enumerate(slopes)] for i in range(3)]
        cof = [[f[(i + 1) % 3][(j + 1) % 3] * f[(i + 2) % 3][(j + 2) % 3]
                - f[(i + 1) % 3][(j + 2) % 3] * f[(i + 2) % 3][(j + 1) % 3]
                for j in range(3)] for i in range(3)]
        ratio = f[0][0] * cof[0][0] + f[0][1] * cof[0][1] + f[0][2] * cof[0][2]
        factor = (LAMBDA_BULK * jnp.log(ratio) - MU_SHEAR) / ratio
        back = []
        for j in range(3):
            parts = [jnp.where(lane < ns - 1, MU_SHEAR * f[i][j] + factor * cof[i][j], 0.0) for i in range(3)]
            back.append((parts[0] + move(parts[1], ns) + move(parts[2], 2 * ns)) * (0.03125 * REG_WEIGHT))
        gx = back[0] + move(back[0], 1)
        gy = back[1] + move(back[1], 1)
        gz = move(back[2], 1) - back[2]
        for dp, dq in ((0, 0), (0, 1), (1, 0), (1, 1)):
            add = (gx if dp else -gx) + (gy if dq else -gy) + gz
            pull[p + dp, dq:dq + nel] = pull[p + dp, dq:dq + nel] + add


def voxels(window, slope_z, ref_rows, left, right):
    back = []
    rows, squares = [None] * 8, [[None] * 3 for _ in range(8)]
    join = lambda a, b: jnp.concatenate([a, b], axis=0)
    for half in range(2):
        run, tot = [None] * 3, [None] * 3
        inc = [(right(c, half) - left(c, half)) * 0.125 for c in range(3)]
        mv = [left(c, half) + 0.5 * inc[c] for c in range(3)]
        prev, cur = window(0, 0, half), window(1, 0, half)
        for k in range(8):
            nxt = window(k + 2, 0, half)
            g = [nxt - prev,
                 window(k + 1, 1, half) - window(k + 1, -1, half),
                 slope_z(k, half)]
            r = ref_rows(k, half) - cur
            for c in range(3):
                r = r - g[c] * mv[c]
                if k < 7:
                    mv[c] = mv[c] + inc[c]
            rows[k] = r if half == 0 else join(rows[k], r).astype(BF16)
            for c in range(3):
                f = g[c] * r
                q = g[c] * g[c]
                run[c] = f if k == 0 else run[c] + f
                tot[c] = run[c] if k == 0 else tot[c] + run[c]
                squares[k][c] = q if half == 0 else join(squares[k][c], q).astype(BF16)
            prev, cur = cur, nxt
        part = []
        for c in range(3):
            low = (tot[c] - 0.5 * run[c]) * 0.125
            part.append((low, run[c] - low))
        back.append(part)
    return rows, squares, [[join(back[0][c][i], back[1][c][i]) for i in range(2)] for c in range(3)]


def step_kernel(nw, nn, rim, ns, map_hbm, own, ref_hbm, disp_hbm,
                res, change,
                inter, proj, up, down, down2, square, gather, dz,
                ext, passed, win, field, gsum, qbuf, zbuf, dpart, gacc, dacc, terms,
                extra, rimcol, nodes, pull, cube, column, side_in, corner_in, colf, colb,
                from_w, from_n, from_c, disp, map_ref, send, recv, lsem):
    rows, cols, layers = own.shape
    comps, nel = disp.shape[0], disp.shape[1]
    side = rim - 1
    w = lax.axis_index("wide")
    n = lax.axis_index("narrow")
    lo_w, hi_w, lo_n, hi_n = w > 0, w < nw - 1, n > 0, n < nn - 1
    up_w, dn_w = (w + 1, n), (w - 1, n)
    up_n, dn_n = (w, n + 1), (w, n - 1)
    mid = slice(side, side + cols)
    ylo = slice(0, side)
    yhi = slice(side + cols, 2 * side + cols)
    total = rows + 2 * rim
    emid = slice(SIDE, SIDE + rows)
    detour = nw == 8
    is0, is3, is4, is7 = (w == 0), (w == 3), (w == 4), (w == 7)

    barrier = pltpu.get_barrier_semaphore()
    greet = [(lo_w, dn_w), (hi_w, up_w), (lo_n, dn_n), (hi_n, up_n)]
    if detour:
        greet += [(is7, (3, n)), (is4, (7, n)), (is0, (4, n)), (is3, (0, n))]
    count = as_int(lo_w) + as_int(hi_w) + as_int(lo_n) + as_int(hi_n)
    if detour:
        count = count + as_int(is0 | is3 | is4 | is7)
    for there, device in greet:
        @pl.when(there)
        def _(device=device):
            pl.semaphore_signal(barrier, inc=1, device_id=device, device_id_type=MESH)
    loads = [pltpu.make_async_copy(disp_hbm, disp, lsem.at[2]),
             pltpu.make_async_copy(own, ext.at[rim:rim + rows, mid], lsem.at[0]),
             pltpu.make_async_copy(ref_hbm, res, lsem.at[1]),
             pltpu.make_async_copy(map_hbm, map_ref, lsem.at[3])]
    for load in loads:
        load.start()
    nodal, local, slab, offsets = loads

    def absent(there, *spans):
        @pl.when(jnp.logical_not(there))
        def _():
            for ref, span in spans:
                ref[span] = jnp.zeros(ref.at[span].shape, ref.dtype)

    elow, ehigh = slice(SIDE, 2 * SIDE), slice(rows, SIDE + rows)
    ebelow, eabove = slice(0, SIDE), slice(SIDE + rows, 2 * SIDE + rows)
    every = slice(None)
    absent(hi_w, (nodes, (nel, slice(0, nel))))
    absent(hi_n, (side_in, every), (extra, 1))
    absent(hi_w & hi_n, (corner_in, every), (extra, (1, eabove)))
    absent(lo_w & hi_n, (extra, (1, ebelow)))
    absent(lo_w, (from_w, every))
    absent(lo_n, (from_n, every), (extra, 0))
    absent(lo_w & lo_n, (from_c, every), (extra, (0, ebelow)))
    absent(hi_w & lo_n, (extra, (0, eabove)))
    pl.semaphore_wait(barrier, count)

    everything = []

    def remote(goes, comes, src, dst, device):
        k = len(everything)
        copy = pltpu.make_async_remote_copy(
            src_ref=src, dst_ref=dst, send_sem=send.at[k], recv_sem=recv.at[k],
            device_id=device, device_id_type=MESH)
        everything.append((goes, comes, copy))
        return k

    def go(*ks):
        for k in ks:
            @pl.when(everything[k][0])
            def _(k=k):
                everything[k][2].start()

    def come(*ks):
        for k in ks:
            @pl.when(everything[k][1])
            def _(k=k):
                everything[k][2].wait_recv()

    below, above = slice(0, rim), slice(rim + rows, total)
    edge_x = remote(lo_w, hi_w, nodes.at[0, 0:nel], nodes.at[nel, 0:nel], dn_w)
    edge_y = remote(lo_n, hi_n, column, side_in, dn_n)
    strips = []
    full = (slice(0, rim), slice(rows - rim, rows), slice(rim, rows - rim))
    for part in full:
        there = slice(part.start + rim, part.stop + rim)
        strips.append((
            remote(hi_n, lo_n, own.at[part, cols - side:cols], ext.at[there, ylo], up_n),
            remote(lo_n, hi_n, own.at[part, 0:side], ext.at[there, yhi], dn_n)))
    cut = cols // 2 if detour else cols
    near, far = slice(0, cut), slice(cut, cols)
    enear, efar = slice(side, side + cut), slice(side + cut, side + cols)
    high_own, low_own = slice(rows - rim, rows), slice(0, rim)
    bands = [
        remote(hi_w, lo_w, own.at[high_own, near], ext.at[below, enear], up_w),
        remote(lo_w, hi_w, own.at[low_own, near], ext.at[above, enear], dn_w)]
    first_hop, second_hop = [], []
    if detour:
        bands += [
            remote(hi_w & (w != 3), lo_w & (w != 4), own.at[high_own, far], ext.at[below, efar], up_w),
            remote(lo_w & (w != 4), hi_w & (w != 3), own.at[low_own, far], ext.at[above, efar], dn_w)]
        first_hop = [
            remote(is3, is7, own.at[high_own, far], passed, (7, n)),
            remote(is4, is0, own.at[low_own, far], passed, (0, n))]
        second_hop = [
            remote(is7, is4, passed, ext.at[below, efar], (4, n)),
            remote(is0, is3, passed, ext.at[above, efar], (3, n))]
    go(*strips[0], *strips[1], *first_hop, *bands)
    cube[...] = jnp.zeros_like(cube)
    nodal.wait()
    cube[:, :, :, 0:ns] = disp[...]
    for i in range(nel):
        value = cube[0, i]
        for c in range(1, comps):
            value = value + pltpu.roll(cube[c, i], ns * c, 1)
        nodes[i, 0:nel] = value
        column[i:i + 1] = value[0:1]
    go(edge_x, edge_y)

    def widen(first, count, columns, together):
        to = slice(columns.start + 8, columns.stop + 8)

        @pl.loop(0, count // together)
        def _(b):
            for a in range(together):
                win[first + together * b + a, to] = ext[first + together * b + a, columns].astype(F32)
        for r in range(first + count // together * together, first + count):
            win[r, to] = ext[r, columns].astype(F32)

    local.wait()
    widen(rim, rows, mid, 2)
    build_tables(ns, inter, proj, up, down, down2, square, gather, dz)
    absent(lo_n, (ext, (every, ylo)))
    absent(hi_n, (ext, (every, yhi)))
    absent(lo_w, (ext, below))
    absent(hi_w, (ext, above))
    come(edge_x)
    edge_c = remote(hi_w & lo_n, hi_w & hi_n, nodes.at[nel, 0:8], corner_in, dn_n)
    go(edge_c)
    come(edge_y)
    top = lax.broadcasted_iota(jnp.int32, (QPAD - nel, 128), 0) == 0
    for i in range(nel):
        nodes[i, nel:QPAD] = jnp.where(top, jnp.broadcast_to(side_in[i:i + 1], (QPAD - nel, 128)), 0.0)
    come(edge_c)
    nodes[nel, nel:QPAD] = jnp.where(top, jnp.broadcast_to(corner_in[0:1], (QPAD - nel, 128)), 0.0)
    come(*first_hop)
    go(*second_hop)
    corners = []
    come(*strips[0], *strips[1])
    gap_up, gap_dn = (w == 3, w == 4) if detour else (w < 0, w < 0)
    keep_up, keep_dn = hi_w & jnp.logical_not(gap_up), lo_w & jnp.logical_not(gap_dn)
    corners += [
        remote(keep_up & lo_n, keep_dn & lo_n, ext.at[rows:rows + rim, ylo], ext.at[below, ylo], up_w),
        remote(keep_up & hi_n, keep_dn & hi_n, ext.at[rows:rows + rim, yhi], ext.at[below, yhi], up_w),
        remote(keep_dn & lo_n, keep_up & lo_n, ext.at[rim:2 * rim, ylo], ext.at[above, ylo], dn_w),
        remote(keep_dn & hi_n, keep_up & hi_n, ext.at[rim:2 * rim, yhi], ext.at[above, yhi], dn_w)]
    go(*corners)
    for k in strips[0] + strips[1]:
        @pl.when(everything[k][0])
        def _(k=k):
            everything[k][2].wait_send()
    go(*strips[2])

    picks = (side + cols - rim, side + rim - 1)

    @pl.loop(0, rows // 8)
    def _(b):
        for a in range(8):
            for i, col in enumerate(picks):
                tile = ext[rim + 8 * b + a, col // 16 * 16:col // 16 * 16 + 16, :].astype(F32)
                colf[i, pl.ds(8 * b + a, 1), :] = tile[col % 16:col % 16 + 1]
    colb[...] = colf[...].astype(BF16)
    thin = [remote(hi_n, lo_n, colb.at[0], extra.at[0, emid], up_n),
            remote(lo_n, hi_n, colb.at[1], extra.at[1, emid], dn_n)]
    go(*thin)

    flat = nodes[...].reshape(-1, 128)
    high = flat.astype(BF16).astype(F32)
    both = jnp.concatenate([high, flat - high], axis=1).astype(BF16)
    level = jnp.dot(both, up[...], preferred_element_type=F32)
    for i in range(nel + 1):
        head, tail = split(level[i * QPAD:(i + 1) * QPAD])
        field[i] = jnp.dot(inter[...], jnp.concatenate([head, tail], axis=0), preferred_element_type=F32)
    for ref in (gsum, qbuf, dacc):
        ref[...] = jnp.zeros_like(ref)
    offsets.wait()
    slab.wait()
    steps, chunks = rows // 8, cols // 16
    start = map_ref[0] + side
    col0 = map_ref[1] + 8 + side

    def fold(u, t):
        got = jnp.dot(square[...], qbuf[u], preferred_element_type=F32)
        dpart[t] = got[0:16] + got[16:32]

    def slopes(p, j):
        row0 = start + 8 * p + 1
        at = col0 + 16 * j
        here = jnp.concatenate([win[row0 + k, pl.ds(at, 16), :].astype(BF16) for k in range(8)], axis=0)
        return jnp.dot(here, dz[...], preferred_element_type=F32)

    def phase(pairs, place, before):
        for u in range(2):
            zbuf[u] = slopes(*place(0, u))

        @pl.loop(0, pairs)
        def _(b):
            coming = [slopes(*place(jnp.minimum(b + 1, pairs - 1), u)) for u in range(2)]
            for u in range(2):
                last = place(jnp.maximum(b - 1, 0), u)
                fold(u, jnp.where(b == 0, before[u][0] * chunks + before[u][1], last[0] * chunks + last[1]))
            for u in range(2):
                p, j = place(b, u)
                at = 16 * j if isinstance(j, int) else pl.multiple_of(16 * j, 16)
                base = 8 * p
                row0 = start + base
                refs = [res[base + k, pl.ds(at, 16), :].astype(F32) for k in range(8)]
                out_rows, squares, parts = voxels(
                    lambda k, shift, half: win[row0 + k, pl.ds(col0 + at + (8 * half + shift), 8), :],
                    lambda k, half: zbuf[u, 16 * k + 8 * half:16 * k + 8 * half + 8, :],
                    lambda k, half: refs[k][8 * half:8 * half + 8],
                    lambda c, half: field[p, pl.ds(at + 8 * half, 8), c * layers:(c + 1) * layers],
                    lambda c, half: field[p + 1, pl.ds(at + 8 * half, 8), c * layers:(c + 1) * layers])
                for k in range(8):
                    res[base + k, pl.ds(at, 16), :] = out_rows[k]
                for c in range(comps):
                    lanes = slice(c * layers, (c + 1) * layers)
                    for k in range(8):
                        qbuf[u, 16 * k:16 * k + 16, lanes] = squares[k][c]
                    for i in range(2):
                        gsum[p + i, pl.ds(at, 16), lanes] = gsum[p + i, pl.ds(at, 16), lanes] + parts[c][i]
            for u in range(2):
                zbuf[u] = coming[u]
        return [place(pairs - 1, u) for u in range(2)]

    p_in = (rim + 7) // 8
    n_in = steps - 2 * p_in
    j_in = (rim + 15) // 16
    other = (chunks - 2) // 2

    def inner_rows(i):
        return p_in + i

    def outer_rows(i):
        return i + n_in * as_int(jnp.asarray(i) >= p_in) if not isinstance(i, int) else i + n_in * (i >= p_in)

    def outer_chunk(i, u):
        m = 2 * i + u
        return m + 2 * (m >= j_in) if isinstance(m, int) else m + 2 * as_int(m >= j_in)

    def by_row(rows_of):
        return lambda b, u: (rows_of(b), j_in + u)

    def by_rest(rows_of):
        def place(b, u):
            if isinstance(b, int):
                return rows_of(b // other), outer_chunk(b % other, u)
            return rows_of(lax.div(b, other)), outer_chunk(lax.rem(b, other), u)
        return place

    done = [by_row(inner_rows)(0, u) for u in range(2)]
    done = phase(n_in, by_row(inner_rows), done)
    strain_pull(ns, nodes, pull)
    for part in full[:2]:
        widen(part.start + rim, rim, ylo, 4)
        widen(part.start + rim, rim, yhi, 4)
    come(*thin)
    thin_corners = [
        remote(lo_n & lo_w, lo_n & hi_w, extra.at[0, elow], extra.at[0, eabove], dn_w),
        remote(lo_n & hi_w, lo_n & lo_w, extra.at[0, ehigh], extra.at[0, ebelow], up_w),
        remote(hi_n & lo_w, hi_n & hi_w, extra.at[1, elow], extra.at[1, eabove], dn_w),
        remote(hi_n & hi_w, hi_n & lo_w, extra.at[1, ehigh], extra.at[1, ebelow], up_w)]
    go(*thin_corners)
    spots = (7, 8 + cols + 2 * side)

    def rims(span, source, first, count):
        rimcol[:, span] = extra[:, span].astype(F32)
        for r in range(count % 4):
            for i, spot in enumerate(spots):
                win[first + r, spot:spot + 1] = rimcol[i, source + r:source + r + 1]

        @pl.loop(0, count // 4)
        def _(b):
            for a in range(4):
                r = count % 4 + 4 * b + a
                for i, spot in enumerate(spots):
                    win[first + r, spot:spot + 1] = rimcol[i, pl.ds(source + r, 1), :]

    even = lax.rem(w, 2) == 0
    odd = jnp.logical_not(even)
    plain = jnp.logical_not(gap_dn | gap_up)

    def bands_wait(cond, ks=bands + second_hop):
        for k in ks:
            @pl.when(everything[k][1] & cond)
            def _(k=k):
                everything[k][2].wait_recv()

    bands_wait(gap_dn | gap_up)
    if detour:
        follow = []
        for here, band in ((gap_dn, below), (gap_up, above)):
            follow += [
                remote(here & hi_n, here & lo_n, ext.at[band, cols:cols + side], ext.at[band, ylo], up_n),
                remote(here & lo_n, here & hi_n, ext.at[band, side:2 * side], ext.at[band, yhi], dn_n)]
        go(*follow)
        corners += follow
    def side_rows(upper):
        bands_wait(plain & upper, bands[1::2])
        bands_wait(plain & jnp.logical_not(upper), bands[0::2])

        @pl.when(upper)
        def _():
            widen(rim + rows, rim, mid, 2)

        @pl.when(jnp.logical_not(upper))
        def _():
            widen(0, rim, mid, 2)
        shift = jnp.where(upper, steps - p_in, 0)
        return phase(p_in, by_row(lambda i: i + shift), done)

    done = side_rows(even)
    rims(emid, SIDE, rim, rows)
    come(*strips[2])
    widen(2 * rim, rows - 2 * rim, ylo, 4)
    widen(2 * rim, rows - 2 * rim, yhi, 4)
    done = phase(n_in * other, by_rest(inner_rows), done)
    done = side_rows(odd)
    come(*corners, *thin_corners)
    for first in (0, rim + rows):
        widen(first, rim, ylo, 4)
        widen(first, rim, yhi, 4)
    rims(slice(0, SIDE), SIDE - rim, 0, rim)
    rims(slice(SIDE + rows, 2 * SIDE + rows), SIDE + rows, rim + rows, rim)
    done = phase(2 * p_in * other, by_rest(outer_rows), done)
    for u in range(2):
        fold(u, done[u][0] * chunks + done[u][1])
    for i in range(steps + 1):
        head, tail = split(gsum[i])
        gacc[i] = jnp.dot(proj[...], jnp.concatenate([head, tail], axis=0), preferred_element_type=F32)
    for i in range(steps):
        head, tail = split(dpart[i * chunks:(i + 1) * chunks].reshape(cols, comps * layers))
        got = jnp.dot(gather[...], jnp.concatenate([head, tail], axis=0), preferred_element_type=F32)
        dacc[i] = dacc[i] + got[0:QPAD]
        dacc[i + 1] = got[QPAD:2 * QPAD]
    for k, (acc, table) in enumerate(((gacc, down), (dacc, down2))):
        head, tail = split(acc[...].reshape(-1, comps * layers))
        got = (jnp.dot(head, table[...], preferred_element_type=F32)
               + jnp.dot(tail, table[...], preferred_element_type=F32)).reshape(pull.shape)
        terms[k] = got + pull[...] if k == 0 else got

    for k in range(2):
        for p in range(nel):
            colf[k, p:p + 1] = terms[k, p, nel:nel + 1]
    to_w = remote(hi_w, lo_w, terms.at[:, nel], from_w, up_w)
    to_n = remote(hi_n, lo_n, colf.at[:, 0:nel], from_n, up_n)
    to_c = remote(lo_w & hi_n, lo_w & lo_n, from_w.at[:, nel:QPAD], from_c, up_n)
    go(to_w, to_n)
    come(to_w)
    go(to_c)
    come(to_n, to_c)
    first_row = lax.broadcasted_iota(jnp.int32, (nel, 128), 0) == 0
    for p in range(nel):
        both = []
        for k in range(2):
            value = terms[k, p, 0:nel]
            beside = from_n[k, p:p + 1]
            if p == 0:
                value = value + from_w[k, 0:nel]
                beside = beside + from_c[k, 0:1]
            both.append(value + jnp.where(first_row, jnp.broadcast_to(beside, (nel, 128)), 0.0))
        step = both[0] / (both[1] + STIFFNESS)
        for c in range(comps):
            here = step if c == 0 else pltpu.roll(step, 128 - ns * c, 1)
            change[c, p] = here[:, 0:ns]
    sent = strips[0] + strips[1]
    for k, (goes, _c, copy) in enumerate(everything):
        if k not in sent:
            @pl.when(goes)
            def _(copy=copy):
                copy.wait_send()


def emit_kernel(parts, kept, change, disp, residual, updated, fresh, sem):
    rows = kept.shape[0] // parts
    copies = [pltpu.make_async_copy(kept.at[k * rows:(k + 1) * rows], residual.at[k * rows:(k + 1) * rows], sem.at[k])
              for k in range(parts)]
    for copy in copies:
        copy.start()
    fresh[...] = disp[...] - change[...]
    last = pltpu.make_async_copy(fresh, updated, sem.at[parts])
    last.start()
    for copy in copies + [last]:
        copy.wait()


def emit(kept, change, nodal):
    anywhere = pl.BlockSpec(memory_space=pl.ANY)
    near = pl.BlockSpec(memory_space=pltpu.VMEM)
    parts = 8
    return pl.pallas_call(
        functools.partial(emit_kernel, parts),
        out_shape=[jax.ShapeDtypeStruct(kept.shape, BF16), jax.ShapeDtypeStruct(nodal.shape, F32)],
        in_specs=[anywhere, near, near],
        out_specs=[anywhere, anywhere],
        scratch_shapes=[pltpu.VMEM(nodal.shape, F32), pltpu.SemaphoreType.DMA((parts + 1,))],
        compiler_params=pltpu.CompilerParams(vmem_limit_bytes=8 << 20),
        name="emit",
    )(kept, change, nodal)


def per_device(nw, nn, reference_image, deformed_image, displacement, tile_map):
    comps, ns, nel, _ = displacement.shape
    rows, cols, layers = reference_image.shape
    nodal = displacement.transpose(0, 2, 3, 1)
    rim = rows // 4 + 1
    npx, lanes = nel + 1, comps * layers
    total, across = rows + 2 * rim, cols + 2 * (rim - 1)
    anywhere = pl.BlockSpec(memory_space=pl.ANY)
    near = pl.BlockSpec(memory_space=pltpu.VMEM)
    kept, change = pl.pallas_call(
        functools.partial(step_kernel, nw, nn, rim, ns),
        out_shape=[jax.ShapeDtypeStruct(reference_image.shape, BF16),
                   jax.ShapeDtypeStruct(nodal.shape, F32)],
        in_specs=[anywhere] * 4,
        out_specs=[near, near],
        scratch_shapes=[
            pltpu.VMEM((cols, 2 * QPAD), BF16),
            pltpu.VMEM((QPAD, 2 * cols), BF16),
            pltpu.VMEM((2 * 128, lanes), BF16),
            pltpu.VMEM((lanes, 128), BF16),
            pltpu.VMEM((lanes, 128), BF16),
            pltpu.VMEM((32, 8 * 16), BF16),
            pltpu.VMEM((2 * QPAD, 2 * cols), BF16),
            pltpu.VMEM((layers, layers), BF16),
            pltpu.VMEM((total, across, layers), BF16),
            pltpu.VMEM((rim, cols - cols // 2, layers), BF16),
            pltpu.VMEM((total, across + 16, layers), F32),
            pltpu.VMEM((npx, cols, lanes), F32),
            pltpu.VMEM((npx, cols, lanes), F32),
            pltpu.VMEM((2, 8 * 16, lanes), BF16),
            pltpu.VMEM((2, 8 * 16, layers), F32),
            pltpu.VMEM((rows // 8 * (cols // 16), 16, lanes), F32),
            pltpu.VMEM((npx, QPAD, lanes), F32),
            pltpu.VMEM((npx, QPAD, lanes), F32),
            pltpu.VMEM((2, npx, QPAD, 128), F32),
            pltpu.VMEM((2, rows + 2 * SIDE, layers), BF16),
            pltpu.VMEM((2, rows + 2 * SIDE, layers), F32),
            pltpu.VMEM((npx, QPAD, 128), F32),
            pltpu.VMEM((npx, QPAD, 128), F32),
            pltpu.VMEM((comps, nel, nel, 128), F32),
            pltpu.VMEM((nel, 128), F32),
            pltpu.VMEM((nel, 128), F32),
            pltpu.VMEM((8, 128), F32),
            pltpu.VMEM((2, rows, layers), F32),
            pltpu.VMEM((2, rows, layers), BF16),
            pltpu.VMEM((2, QPAD, 128), F32),
            pltpu.VMEM((2, nel, 128), F32),
            pltpu.VMEM((2, QPAD - nel, 128), F32),
            pltpu.VMEM(nodal.shape, F32),
            pltpu.SMEM((2,), jnp.int32),
            pltpu.SemaphoreType.DMA((34,)),
            pltpu.SemaphoreType.DMA((34,)),
            pltpu.SemaphoreType.DMA((4,)),
        ],
        compiler_params=pltpu.CompilerParams(
            collective_id=0, has_side_effects=True, vmem_limit_bytes=48 << 20),
        name="step",
    )(tile_map.reshape(2), deformed_image, reference_image, nodal)
    residual, updated = emit(kept, change, nodal)
    return (updated.transpose(0, 3, 1, 2), residual)


def solution(mesh):
    placed = (
        P("wide", "narrow", None),
        P("wide", "narrow", None),
        P(None, None, "wide", "narrow"),
        P("wide", "narrow", None),
    )
    return jax.shard_map(
        functools.partial(per_device, mesh.shape["wide"], mesh.shape["narrow"]),
        mesh=mesh,
        in_specs=placed,
        out_specs=(P(None, None, "wide", "narrow"), P("wide", "narrow", None)),
        check_vma=False,
    )
```
